32 devices in a mesh: seq: 8 (over z, x), sp: 4 (over y, core).
Axes of the slice: x: 2, y: 2, z: 4, core: 2. Of those that a mesh axis runs over, the one named last changes fastest.
Arguments:
- incoming_signal: bfloat16 [8192, 1024], P(('seq', 'sp')), may hold values from -6 to 6
- document_extents: int32 [8, 4], P('seq'), may hold values from 64 to 832, as said below
- adjoint_signal: bfloat16 [8192, 1024], P(('seq', 'sp')), may hold values from -6 to 6
- layernorm_scaling: bfloat16 [1024], P(('seq', 'sp')), may hold values from 0.5 to 1.5
- layernorm_offset: bfloat16 [1024], P(('seq', 'sp')), may hold values from -3 to 3
- temporal_blend_lookup: bfloat16 [1024], P(('seq', 'sp')), may hold values from 0 to 1
- temporal_blend_content: bfloat16 [1024], P(('seq', 'sp')), may hold values from 0 to 1
- temporal_blend_receptor: bfloat16 [1024], P(('seq', 'sp')), may hold values from 0 to 1
- temporal_shrinkage_log: bfloat16 [1024], P(('seq', 'sp')), may hold values from -8 to -2.5
- diagonal_reward: bfloat16 [1024], P(('seq', 'sp')), may hold values from -1 to 1
- lookup_projection: bfloat16 [1024, 1024], P(('seq', 'sp')), may hold values from -0.1875 to 0.1875
- content_projection: bfloat16 [1024, 1024], P(('seq', 'sp')), may hold values from -0.1875 to 0.1875
- receptor_projection: bfloat16 [1024, 1024], P(('seq', 'sp')), may hold values from -0.1875 to 0.1875
- emission_projection: bfloat16 [1024, 1024], P(('seq', 'sp')), may hold values from -0.75 to 0.75
- latter_scaling: bfloat16 [1024], P(('seq', 'sp')), may hold values from 0.5 to 1.5
- latter_offset: bfloat16 [1024], P(('seq', 'sp')), may hold values from -3 to 3
- channel_blend_lookup: bfloat16 [1024], P(('seq', 'sp')), may hold values from 0 to 1
- channel_blend_receptor: bfloat16 [1024], P(('seq', 'sp')), may hold values from 0 to 1
- channel_mixer_lookup: bfloat16 [1024, 4096], P(('seq', 'sp')), may hold values from -0.1875 to 0.1875
- channel_mixer_content: bfloat16 [4096, 1024], P(('seq', 'sp')), may hold values from -0.09375 to 0.09375
- channel_mixer_receptor: bfloat16 [1024, 1024], P(('seq', 'sp')), may hold values from -0.1875 to 0.1875
Outputs:
- block_out: bfloat16 [8192, 1024], P(('seq', 'sp'))
- input_grad: float32 [8192, 1024], P(('seq', 'sp'))
- grad_norm_gain: float32 [1024], P(('seq', 'sp'))
- grad_norm_bias: float32 [1024], P(('seq', 'sp'))
- grad_mix_key: float32 [1024], P(('seq', 'sp'))
- grad_mix_value: float32 [1024], P(('seq', 'sp'))
- grad_mix_gate: float32 [1024], P(('seq', 'sp'))
- grad_time_decay: float32 [1024], P(('seq', 'sp'))
- grad_time_first: float32 [1024], P(('seq', 'sp'))
- grad_key_weight: float32 [1024, 1024], P(('seq', 'sp'))
- grad_value_weight: float32 [1024, 1024], P(('seq', 'sp'))
- grad_gate_weight: float32 [1024, 1024], P(('seq', 'sp'))
- grad_output_weight: float32 [1024, 1024], P(('seq', 'sp'))
- grad_second_gain: float32 [1024], P(('seq', 'sp'))
- grad_second_bias: float32 [1024], P(('seq', 'sp'))
- grad_feed_mix_key: float32 [1024], P(('seq', 'sp'))
- grad_feed_mix_gate: float32 [1024], P(('seq', 'sp'))
- grad_feed_key: float32 [1024, 4096], P(('seq', 'sp'))
- grad_feed_value: float32 [4096, 1024], P(('seq', 'sp'))
- grad_feed_gate: float32 [1024, 1024], P(('seq', 'sp'))
The draws below stay inside these ranges and needn't reach their ends.
Inputs may be any that keep to these rules, and one draw needn't show every extreme that they name: `document_extents`: each row holds the lengths of the 4 documents of one group in order; they add up to at most 1024, the rest of the group is padding; every length is 64 or more; each row has one document of 256 positions or more, and some row has one of exactly 832 positions.
All inputs are finite; a program needn't handle non-finite values.
Results may differ from the reference program's by a relative error of at most 0.02.
Values may be sent and summed in bfloat16 or wider, within the bound.
A program may use at most 128 MiB of HBM per device.

```python
import jax
import jax.numpy as jnp
from jax import lax

CHANNEL_COUNT = 1024
FF = 4096
LOOP_LENGTH = 128
DOCS = 4
SHORTEST = 64
GROUP_TOK = 1024
GROUPS = 8
TOKENS = 8192


def draw_document_extents(key, part):
    keys_list = jax.random.split(jax.random.fold_in(key, 7), 5)
    others_count = DOCS - 1
    longest = GROUP_TOK - others_count * SHORTEST
    first_try = jax.random.randint(keys_list[0], (GROUPS,), GROUP_TOK // 4, longest + 1)
    second_try = jax.random.randint(keys_list[1], (GROUPS,), GROUP_TOK // 4, longest + 1)
    long_doc = jnp.maximum(first_try, second_try)
    chosen = jax.random.randint(keys_list[2], (), 0, GROUPS)
    long_doc = jnp.where(jnp.arange(GROUPS, dtype=jnp.int32) == chosen, longest, long_doc).astype(jnp.int32)
    room = GROUP_TOK - long_doc - others_count * SHORTEST
    share = room // others_count + 1
    raw = jax.random.randint(keys_list[3], (GROUPS, others_count), 0, 1 << 20)
    others = SHORTEST + raw % share[:, None]
    row = jnp.concatenate([long_doc[:, None], others], axis=1).astype(jnp.int32)
    scores = jax.random.randint(keys_list[4], (GROUPS, DOCS), 0, 1 << 20) * DOCS + jnp.arange(DOCS, dtype=jnp.int32)[None, :]
    order = jnp.argsort(scores, axis=1, stable=True)
    return jnp.take_along_axis(row, order, axis=1).astype(jnp.int32)


def shard_levels(key, extent, shards, low, high):
    def one(position, parts):
        steps = jax.random.uniform(jax.random.fold_in(jax.random.fold_in(key, 6), position), (parts,), jnp.float32, low / len(shards), high / len(shards))
        return jnp.repeat(jnp.exp(steps), extent[position] // parts).reshape((-1,) + (1,) * (len(extent) - position - 1))

    level = one(*shards[0])
    for cut in shards[1:]:
        level = level * one(*cut)
    return level


def scatter_about(stream_key, dims, width, limit, cuts=(), held_as=jnp.bfloat16):
    values = jax.random.normal(stream_key, dims, jnp.float32) * width
    if len(cuts) > 0:
        values = shard_levels(stream_key, dims, cuts, -0.22, 0.18) * values
    return jnp.clip(values, min=-limit, max=limit).astype(held_as)


def setup_inputs(seed: int = 0) -> dict:
    splits = jax.random.split(jax.random.key(seed), 22)
    return {
        "incoming_signal": scatter_about(splits[0], (TOKENS, CHANNEL_COUNT), 1.0, 6.0, ((0, 32),)),
        "document_extents": draw_document_extents(jax.random.fold_in(splits[21], 71), 0),
        "adjoint_signal": scatter_about(splits[2], (TOKENS, CHANNEL_COUNT), 1.0, 6.0, ((0, 32),)),
        "layernorm_scaling": jnp.clip(1.0 + 0.1 * jax.random.normal(splits[3], (CHANNEL_COUNT,), jnp.float32), 0.5, 1.5).astype(jnp.bfloat16),
        "layernorm_offset": scatter_about(splits[4], (CHANNEL_COUNT,), 0.3, 3.0, ((0, 32),)),
        "temporal_blend_lookup": jnp.clip(1.0 * jax.random.uniform(splits[5], (CHANNEL_COUNT,), jnp.float32) ** shard_levels(splits[5], (CHANNEL_COUNT,), ((0, 32),), -0.2, 0.2), 0.0, 1.0).astype(jnp.bfloat16),
        "temporal_blend_content": jnp.clip(1.0 * jax.random.uniform(splits[6], (CHANNEL_COUNT,), jnp.float32) ** shard_levels(splits[6], (CHANNEL_COUNT,), ((0, 32),), -0.2, 0.2), 0.0, 1.0).astype(jnp.bfloat16),
        "temporal_blend_receptor": jnp.clip(1.0 * jax.random.uniform(splits[7], (CHANNEL_COUNT,), jnp.float32) ** shard_levels(splits[7], (CHANNEL_COUNT,), ((0, 32),), -0.2, 0.2), 0.0, 1.0).astype(jnp.bfloat16),
        "temporal_shrinkage_log": jnp.clip(-8.0 + 5.5 * jax.random.uniform(splits[8], (CHANNEL_COUNT,), jnp.float32) ** shard_levels(splits[8], (CHANNEL_COUNT,), ((0, 32),), -0.2, 0.2), -8.0, -2.5).astype(jnp.bfloat16),
        "diagonal_reward": jnp.clip(jax.random.uniform(splits[9], (CHANNEL_COUNT,), jnp.float32, -1.0, 1.0) * shard_levels(splits[9], (CHANNEL_COUNT,), ((0, 32),), -0.4, 0.0), -1.0, 1.0).astype(jnp.bfloat16),
        "lookup_projection": scatter_about(splits[10], (CHANNEL_COUNT, CHANNEL_COUNT), CHANNEL_COUNT ** -0.5, 0.1875, ((0, 32),)),
        "content_projection": scatter_about(splits[11], (CHANNEL_COUNT, CHANNEL_COUNT), CHANNEL_COUNT ** -0.5, 0.1875, ((0, 32),)),
        "receptor_projection": scatter_about(splits[12], (CHANNEL_COUNT, CHANNEL_COUNT), CHANNEL_COUNT ** -0.5, 0.1875, ((0, 32),)),
        "emission_projection": scatter_about(splits[13], (CHANNEL_COUNT, CHANNEL_COUNT), (CHANNEL_COUNT // 16) ** -0.5, 0.75, ((0, 32),)),
        "latter_scaling": jnp.clip(1.0 + 0.1 * jax.random.normal(splits[14], (CHANNEL_COUNT,), jnp.float32), 0.5, 1.5).astype(jnp.bfloat16),
        "latter_offset": scatter_about(splits[15], (CHANNEL_COUNT,), 0.3, 3.0, ((0, 32),)),
        "channel_blend_lookup": jnp.clip(1.0 * jax.random.uniform(splits[16], (CHANNEL_COUNT,), jnp.float32) ** shard_levels(splits[16], (CHANNEL_COUNT,), ((0, 32),), -0.2, 0.2), 0.0, 1.0).astype(jnp.bfloat16),
        "channel_blend_receptor": jnp.clip(1.0 * jax.random.uniform(splits[17], (CHANNEL_COUNT,), jnp.float32) ** shard_levels(splits[17], (CHANNEL_COUNT,), ((0, 32),), -0.2, 0.2), 0.0, 1.0).astype(jnp.bfloat16),
        "channel_mixer_lookup": scatter_about(splits[18], (CHANNEL_COUNT, FF), CHANNEL_COUNT ** -0.5, 0.1875, ((0, 32),)),
        "channel_mixer_content": scatter_about(splits[19], (FF, CHANNEL_COUNT), FF ** -0.5, 0.09375, ((0, 32),)),
        "channel_mixer_receptor": scatter_about(splits[20], (CHANNEL_COUNT, CHANNEL_COUNT), CHANNEL_COUNT ** -0.5, 0.1875, ((0, 32),)),
    }


@jax.custom_vjp
def reduced_precision(v):
    return lax.optimization_barrier(v.astype(jnp.bfloat16)).astype(jnp.float32)

@jax.custom_vjp
def reduced_precision_reverse(v):
    return v

def low_keep(v):
    return (reduced_precision(v), None)

def low_pass(kept, grad):
    return (grad,)

def back_keep(v):
    return (v, None)

def back_low(kept, grad):
    return (reduced_precision(grad),)
reduced_precision.defvjp(low_keep, low_pass)
reduced_precision_reverse.defvjp(back_keep, back_low)
HIGHEST = lax.Precision.HIGHEST
EPSILON = 1e-05

def matmul(left, right):
    return jnp.dot(left, right, precision=HIGHEST)

def norm_rows(content_vectors, gain, bias):
    centered = content_vectors - lax.optimization_barrier(jnp.mean(content_vectors, axis=1, keepdims=True))
    scale = lax.rsqrt(lax.optimization_barrier(jnp.mean(centered * centered, axis=1, keepdims=True)) + EPSILON)
    return centered * scale * gain + bias

def segment_ids(lengths_row, positions):
    ends = jnp.cumsum(lengths_row).astype(jnp.int32)
    bounds = jnp.concatenate([ends - lengths_row, ends[-1:]]).astype(jnp.int32)
    document_tags = lax.optimization_barrier(jnp.sum((positions[:, None] >= bounds[None, :]).astype(jnp.int32), axis=1)) - 1
    return (document_tags.astype(jnp.int32), positions < ends[-1])

def weighted_attention_loop(lookup_vectors, content_vectors, temporal_shrinkage_log, diagonal_reward, document_tags, segment_piece):
    count, feature_dimension = lookup_vectors.shape
    blocks = count // segment_piece
    rate = jnp.exp(temporal_shrinkage_log)
    offsets = jnp.arange(segment_piece, dtype=jnp.float32)[:, None]
    grow = jnp.exp(offsets * rate)
    shrink_multiplier = jnp.exp(-(offsets - 1.0) * rate)
    fade = jnp.exp(-offsets * rate)
    tail_fade = jnp.exp(-(segment_piece - 1.0 - offsets) * rate)
    whole_fade = jnp.exp(-1.0 * segment_piece * rate)
    order = jnp.arange(segment_piece, dtype=jnp.int32)
    lower = order[None, :] < order[:, None]
    key_blocks = lookup_vectors.reshape(blocks, segment_piece, feature_dimension)
    value_blocks = content_vectors.reshape(blocks, segment_piece, feature_dimension)
    label_blocks = document_tags.reshape(blocks, segment_piece)
    before = jnp.concatenate([jnp.full((1,), -1, jnp.int32), label_blocks[:-1, -1].astype(jnp.int32)])

    @jax.checkpoint
    def advance(carry, items):
        dividend_total, divisor_total = carry
        lookup_portion, content_portion, label_part, last_label = items
        weight_key = jnp.exp(lookup_portion)
        links = ((label_part[:, None] == label_part[None, :]) & lower).astype(jnp.float32)
        scaled = grow * weight_key
        cumulative_totals = jnp.dot(links, jnp.concatenate([scaled * content_portion, scaled], axis=1), precision=HIGHEST)
        recurrent_memory = (label_part == last_label).astype(jnp.float32)[:, None] * fade
        initial_reward = jnp.exp(diagonal_reward + lookup_portion)
        highest_line_entry = shrink_multiplier * cumulative_totals[:, :feature_dimension] + recurrent_memory * dividend_total + initial_reward * content_portion
        lowest_line_entry = shrink_multiplier * cumulative_totals[:, feature_dimension:] + recurrent_memory * divisor_total + initial_reward
        end_label = label_part[-1]
        keep = (end_label == last_label).astype(jnp.float32) * whole_fade
        tail = (label_part == end_label).astype(jnp.float32)[:, None] * tail_fade * weight_key
        dividend_total = keep * dividend_total + lax.optimization_barrier(jnp.sum(tail * content_portion, axis=0))
        divisor_total = keep * divisor_total + lax.optimization_barrier(jnp.sum(tail, axis=0))
        return ((dividend_total, divisor_total), highest_line_entry / lowest_line_entry)
    zeros = jnp.zeros((feature_dimension,), jnp.float32)
    _, blended_signal = lax.scan(advance, (zeros, zeros), (key_blocks, value_blocks, label_blocks, before))
    return blended_signal.reshape(count, feature_dimension)

def shifted(rows, same):
    return jnp.concatenate([jnp.zeros_like(rows[:1]), rows[:-1]], axis=0) * same[:, None]

def blend(current, prior, share):
    return current * share + prior * (1.0 - share)

def block_forward(incoming_signal, learnable_tensors, document_tags, same, live):
    layernorm_scaling, layernorm_offset, temporal_blend_lookup, temporal_blend_content, temporal_blend_receptor, temporal_shrinkage_log, diagonal_reward, lookup_projection, content_projection, receptor_projection, emission_projection, latter_scaling, latter_offset, channel_blend_lookup, channel_blend_receptor, channel_mixer_lookup, channel_mixer_content, channel_mixer_receptor = learnable_tensors
    normed = norm_rows(incoming_signal, layernorm_scaling, layernorm_offset)
    prior = shifted(normed, same)
    key_in = reduced_precision(blend(normed, prior, temporal_blend_lookup))
    value_in = reduced_precision(blend(normed, prior, temporal_blend_content))
    gate_in = reduced_precision(blend(normed, prior, temporal_blend_receptor))
    lookup_vectors = reduced_precision_reverse(reduced_precision(matmul(key_in, lookup_projection)))
    content_vectors = reduced_precision_reverse(reduced_precision(matmul(value_in, content_projection)))
    gate = jax.nn.sigmoid(reduced_precision_reverse(matmul(gate_in, receptor_projection)))
    blended_signal = reduced_precision_reverse(reduced_precision(weighted_attention_loop(lookup_vectors, content_vectors, temporal_shrinkage_log, diagonal_reward, document_tags, LOOP_LENGTH)))
    attended = reduced_precision_reverse(matmul(reduced_precision(gate * blended_signal), emission_projection))
    middle = incoming_signal + attended
    second = norm_rows(middle, latter_scaling, latter_offset)
    prior_second = shifted(second, same)
    feed_key_in = reduced_precision(blend(second, prior_second, channel_blend_lookup))
    feed_gate_in = reduced_precision(blend(second, prior_second, channel_blend_receptor))
    hidden = reduced_precision(jnp.square(jax.nn.relu(reduced_precision_reverse(matmul(feed_key_in, channel_mixer_lookup)))))
    recurrent_memory = reduced_precision_reverse(matmul(hidden, channel_mixer_content))
    feed_sig = jax.nn.sigmoid(reduced_precision_reverse(matmul(feed_gate_in, channel_mixer_receptor)))
    return live[:, None] * (middle + feed_sig * recurrent_memory)

def reference(incoming_signal, document_extents, adjoint_signal, layernorm_scaling, layernorm_offset, temporal_blend_lookup, temporal_blend_content, temporal_blend_receptor, temporal_shrinkage_log, diagonal_reward, lookup_projection, content_projection, receptor_projection, emission_projection, latter_scaling, latter_offset, channel_blend_lookup, channel_blend_receptor, channel_mixer_lookup, channel_mixer_content, channel_mixer_receptor):
    learnable_tensors = tuple((parameter_entry.astype(jnp.float32) for parameter_entry in (layernorm_scaling, layernorm_offset, temporal_blend_lookup, temporal_blend_content, temporal_blend_receptor, temporal_shrinkage_log, diagonal_reward, lookup_projection, content_projection, receptor_projection, emission_projection, latter_scaling, latter_offset, channel_blend_lookup, channel_blend_receptor, channel_mixer_lookup, channel_mixer_content, channel_mixer_receptor)))
    group_rows = incoming_signal.astype(jnp.float32).reshape(GROUPS, GROUP_TOK, CHANNEL_COUNT)
    group_back = adjoint_signal.astype(jnp.float32).reshape(GROUPS, GROUP_TOK, CHANNEL_COUNT)
    positions = jnp.arange(GROUP_TOK, dtype=jnp.int32)

    def one_group(totals, items):
        rows, lengths_row, back = items
        document_tags, live = segment_ids(lengths_row, positions)
        earlier, _ = segment_ids(lengths_row, positions - 1)
        same = (document_tags == earlier).astype(jnp.float32)
        live_rows = live.astype(jnp.float32)
        result, pull = jax.vjp(lambda a, b: block_forward(a, b, document_tags, same, live_rows), rows, learnable_tensors)
        grad_rows, grad_params = pull(back)
        totals = jax.tree.map(jnp.add, totals, grad_params)
        return (totals, (result.astype(jnp.bfloat16), grad_rows))
    zero = tuple((jnp.zeros_like(parameter_entry) for parameter_entry in learnable_tensors))
    totals, (outs, grads) = lax.scan(one_group, zero, (group_rows, document_extents, group_back))
    return (outs.reshape(TOKENS, CHANNEL_COUNT), grads.reshape(TOKENS, CHANNEL_COUNT), totals[0], totals[1], totals[2], totals[3], totals[4], totals[5], totals[6], totals[7], totals[8], totals[9], totals[10], totals[11], totals[12], totals[13], totals[14], totals[15], totals[16], totals[17])
```

```python
import functools
import types

import jax
import jax.numpy as jnp
from jax import lax
from jax.experimental import pallas as pl
from jax.experimental.pallas import tpu as pltpu
from jax.sharding import PartitionSpec as P

LOOP_LENGTH = 128


HIGHEST = lax.Precision.HIGHEST
EPSILON = 1e-05


def shifted(value, axis, steps):
    count = lax.axis_size(axis)
    first, last = (max(0, -steps), min(count, count - steps))
    return lax.ppermute(value, axis, [(source, source + steps) for source in range(first, last)])


def norm_rows(content_vectors, gain, bias):
    centered = content_vectors - jnp.mean(content_vectors, axis=1, keepdims=True)
    scale = lax.rsqrt(jnp.mean(centered * centered, axis=1, keepdims=True) + EPSILON)
    return centered * scale * gain + bias


def running(lengths_row):
    ends = [lengths_row[0]]
    for i in range(1, lengths_row.shape[0]):
        ends.append(ends[-1] + lengths_row[i])
    return ends


def segment_ids(lengths_row, positions):
    ends = jnp.stack(running(lengths_row))
    bounds = jnp.concatenate([ends - lengths_row, ends[-1:]])
    document_tags = jnp.sum((positions[:, None] >= bounds[None, :]).astype(jnp.int32), axis=1) - 1
    return (document_tags, positions < ends[-1])


def weighted_attention_loop(
    lookup_vectors,
    content_vectors,
    temporal_shrinkage_log,
    diagonal_reward,
    document_tags,
    segment_piece,
):
    count, feature_dimension = lookup_vectors.shape
    blocks = count // segment_piece
    rate = jnp.exp(temporal_shrinkage_log)
    offsets = jnp.arange(segment_piece, dtype=jnp.float32)[:, None]
    grow = jnp.exp(offsets * rate)
    shrink_multiplier = jnp.exp(-(offsets - 1.0) * rate)
    fade = jnp.exp(-offsets * rate)
    tail_fade = jnp.exp(-(segment_piece - 1.0 - offsets) * rate)
    whole_fade = jnp.exp(-1.0 * segment_piece * rate)
    order = jnp.arange(segment_piece, dtype=jnp.int32)
    lower = order[None, :] < order[:, None]
    key_blocks = lookup_vectors.reshape(blocks, segment_piece, feature_dimension)
    value_blocks = content_vectors.reshape(blocks, segment_piece, feature_dimension)
    label_blocks = document_tags.reshape(blocks, segment_piece)
    before = jnp.concatenate([jnp.full((1,), -1, jnp.int32), label_blocks[:-1, -1]])

    @jax.checkpoint
    def advance(carry, items):
        dividend_total, divisor_total = carry
        lookup_portion, content_portion, label_part, last_label = items
        weight_key = jnp.exp(lookup_portion)
        links = ((label_part[:, None] == label_part[None, :]) & lower).astype(jnp.float32)
        scaled = grow * weight_key
        cumulative_totals = jnp.dot(
            links, jnp.concatenate([scaled * content_portion, scaled], axis=1), precision=HIGHEST
        )
        recurrent_memory = (label_part == last_label).astype(jnp.float32)[:, None] * fade
        initial_reward = jnp.exp(diagonal_reward + lookup_portion)
        highest_line_entry = (
            shrink_multiplier * cumulative_totals[:, :feature_dimension]
            + recurrent_memory * dividend_total
            + initial_reward * content_portion
        )
        lowest_line_entry = (
            shrink_multiplier * cumulative_totals[:, feature_dimension:]
            + recurrent_memory * divisor_total
            + initial_reward
        )
        end_label = label_part[-1]
        keep = (end_label == last_label).astype(jnp.float32) * whole_fade
        tail = (label_part == end_label).astype(jnp.float32)[:, None] * tail_fade * weight_key
        dividend_total = keep * dividend_total + jnp.sum(tail * content_portion, axis=0)
        divisor_total = keep * divisor_total + jnp.sum(tail, axis=0)
        return ((dividend_total, divisor_total), highest_line_entry / lowest_line_entry)

    zeros = jnp.zeros((feature_dimension,), jnp.float32)
    _, blended_signal = lax.scan(
        advance, (zeros, zeros), (key_blocks, value_blocks, label_blocks, before)
    )
    return blended_signal.reshape(count, feature_dimension)


def product(left, right):
    return jnp.dot(left, right, preferred_element_type=jnp.float32)


def times_transposed(left, right):
    return lax.dot_general(
        left, right, (((1,), (1,)), ((), ())), preferred_element_type=jnp.float32
    )


def outer_sum(left, right):
    return lax.dot_general(
        left, right, (((0,), (0,)), ((), ())), preferred_element_type=jnp.float32
    )


def blend(current, prior, share):
    return current * share + prior * (1.0 - share)


def blend_back(current, prior, shares, grads):
    current_grad = jnp.zeros_like(current)
    prior_grad = jnp.zeros_like(current)
    spread = current - prior
    share_grads = []
    for share, grad in zip(shares, grads):
        current_grad = current_grad + grad * share
        prior_grad = prior_grad + grad * (1.0 - share)
        share_grads.append(jnp.sum(spread * grad, axis=0))
    return (current_grad, prior_grad, share_grads)


def plain_body(
    incoming_signal,
    document_extents,
    adjoint_signal,
    layernorm_scaling,
    layernorm_offset,
    temporal_blend_lookup,
    temporal_blend_content,
    temporal_blend_receptor,
    temporal_shrinkage_log,
    diagonal_reward,
    lookup_projection,
    content_projection,
    receptor_projection,
    emission_projection,
    latter_scaling,
    latter_offset,
    channel_blend_lookup,
    channel_blend_receptor,
    channel_mixer_lookup,
    channel_mixer_content,
    channel_mixer_receptor,
):
    rows = incoming_signal.shape[0]
    feature_dimension = incoming_signal.shape[1]
    parts = lax.axis_size("sp")
    place = lax.axis_index("sp")
    group_rows = rows * parts
    channels = feature_dimension // parts
    lengths_row = document_extents[0]
    positions = place * rows + jnp.arange(rows, dtype=jnp.int32)
    document_tags, live = segment_ids(lengths_row, positions)
    earlier, _ = segment_ids(lengths_row, positions - 1)
    same = (document_tags == earlier).astype(jnp.float32)[:, None]
    live_rows = live.astype(jnp.float32)[:, None]
    group_labels, _ = segment_ids(lengths_row, jnp.arange(group_rows, dtype=jnp.int32))
    fetched = [
        lax.all_gather(piece, ("seq", "sp"), axis=0, tiled=True)
        for piece in (
            layernorm_scaling,
            layernorm_offset,
            temporal_blend_lookup,
            temporal_blend_content,
            temporal_blend_receptor,
            temporal_shrinkage_log,
            diagonal_reward,
            lookup_projection,
            content_projection,
            receptor_projection,
            emission_projection,
            latter_scaling,
            latter_offset,
            channel_blend_lookup,
            channel_blend_receptor,
            channel_mixer_lookup,
            channel_mixer_content,
            channel_mixer_receptor,
        )
    ]
    vectors = [fetched[i].astype(jnp.float32) for i in (0, 1, 2, 3, 4, 5, 6, 11, 12, 13, 14)]
    gain_one, bias_one, share_key, share_value, share_gate, decay_all, first_all = vectors[:7]
    gain_two, bias_two, feed_share_key, feed_share_gate = vectors[7:]
    key_matrix, value_matrix, gate_matrix, output_matrix = (
        fetched[7],
        fetched[8],
        fetched[9],
        fetched[10],
    )
    feed_key_matrix, feed_value_matrix, feed_gate_matrix = (fetched[15], fetched[16], fetched[17])
    source = incoming_signal.astype(jnp.float32)
    normed, norm_pull = jax.vjp(norm_rows, source, gain_one, bias_one)
    edge = shifted(normed[-1:], "sp", 1)
    prior = jnp.concatenate([edge, normed[:-1]], axis=0) * same
    key_in = blend(normed, prior, share_key).astype(jnp.bfloat16)
    value_in = blend(normed, prior, share_value).astype(jnp.bfloat16)
    gate_in = blend(normed, prior, share_gate).astype(jnp.bfloat16)
    lookup_vectors = product(key_in, key_matrix).astype(jnp.bfloat16)
    content_vectors = product(value_in, value_matrix).astype(jnp.bfloat16)
    gate = jax.nn.sigmoid(product(gate_in, gate_matrix))
    arrived = lax.all_to_all(
        jnp.stack([lookup_vectors, content_vectors]), "sp", split_axis=2, concat_axis=1, tiled=True
    )
    decay_part = lax.dynamic_slice_in_dim(decay_all, place * channels, channels)
    first_part = lax.dynamic_slice_in_dim(first_all, place * channels, channels)

    def recurrence(key_full, value_full, decay_here, first_here):
        return weighted_attention_loop(
            key_full, value_full, decay_here, first_here, group_labels, LOOP_LENGTH
        )

    blended_signal, scan_pull = jax.vjp(
        recurrence,
        arrived[0].astype(jnp.float32),
        arrived[1].astype(jnp.float32),
        decay_part,
        first_part,
    )
    mixed_rows = lax.all_to_all(
        blended_signal.astype(jnp.bfloat16), "sp", split_axis=0, concat_axis=1, tiled=True
    ).astype(jnp.float32)
    gated = (gate * mixed_rows).astype(jnp.bfloat16)
    middle = source + product(gated, output_matrix)
    second, second_pull = jax.vjp(norm_rows, middle, gain_two, bias_two)
    second_edge = shifted(second[-1:], "sp", 1)
    prior_second = jnp.concatenate([second_edge, second[:-1]], axis=0) * same
    feed_key_in = blend(second, prior_second, feed_share_key).astype(jnp.bfloat16)
    feed_gate_in = blend(second, prior_second, feed_share_gate).astype(jnp.bfloat16)
    raised = product(feed_key_in, feed_key_matrix)
    hidden = jnp.square(jax.nn.relu(raised)).astype(jnp.bfloat16)
    recurrent_memory = product(hidden, feed_value_matrix)
    feed_sig = jax.nn.sigmoid(product(feed_gate_in, feed_gate_matrix))
    block_out = (live_rows * (middle + feed_sig * recurrent_memory)).astype(jnp.bfloat16)
    upstream = adjoint_signal.astype(jnp.float32) * live_rows
    carried_grad = (upstream * feed_sig).astype(jnp.bfloat16)
    feed_pre_grad = (upstream * recurrent_memory * feed_sig * (1.0 - feed_sig)).astype(jnp.bfloat16)
    grad_feed_value = outer_sum(hidden, carried_grad)
    grad_feed_gate = outer_sum(feed_gate_in, feed_pre_grad)
    raised_grad = (
        times_transposed(carried_grad, feed_value_matrix) * 2.0 * jax.nn.relu(raised)
    ).astype(jnp.bfloat16)
    grad_feed_key = outer_sum(feed_key_in, raised_grad)
    second_grad, second_prior_grad, feed_share_grads = blend_back(
        second,
        prior_second,
        (feed_share_key, feed_share_gate),
        (
            times_transposed(raised_grad, feed_key_matrix),
            times_transposed(feed_pre_grad, feed_gate_matrix),
        ),
    )
    moved = second_prior_grad * same
    incoming = shifted(moved[:1], "sp", -1)
    second_grad = second_grad + jnp.concatenate([moved[1:], incoming], axis=0)
    middle_norm_grad, grad_second_gain, grad_second_bias = second_pull(second_grad)
    middle_grad = upstream + middle_norm_grad
    attended_grad = middle_grad.astype(jnp.bfloat16)
    grad_output_weight = outer_sum(gated, attended_grad)
    gated_grad = times_transposed(attended_grad, output_matrix)
    mixed_grad = (gated_grad * gate).astype(jnp.bfloat16)
    gate_pre_grad = (gated_grad * mixed_rows * gate * (1.0 - gate)).astype(jnp.bfloat16)
    channel_grad = lax.all_to_all(mixed_grad, "sp", split_axis=1, concat_axis=0, tiled=True)
    key_grad_here, value_grad_here, decay_grad_here, first_grad_here = scan_pull(
        channel_grad.astype(jnp.float32)
    )
    returned = lax.all_to_all(
        jnp.stack([key_grad_here, value_grad_here]).astype(jnp.bfloat16),
        "sp",
        split_axis=1,
        concat_axis=2,
        tiled=True,
    )
    key_grad = returned[0]
    value_grad = returned[1]
    grad_key_weight = outer_sum(key_in, key_grad)
    grad_value_weight = outer_sum(value_in, value_grad)
    grad_gate_weight = outer_sum(gate_in, gate_pre_grad)
    normed_grad, normed_prior_grad, share_grads = blend_back(
        normed,
        prior,
        (share_key, share_value, share_gate),
        (
            times_transposed(key_grad, key_matrix),
            times_transposed(value_grad, value_matrix),
            times_transposed(gate_pre_grad, gate_matrix),
        ),
    )
    moved_first = normed_prior_grad * same
    incoming_first = shifted(moved_first[:1], "sp", -1)
    normed_grad = normed_grad + jnp.concatenate([moved_first[1:], incoming_first], axis=0)
    source_norm_grad, grad_norm_gain, grad_norm_bias = norm_pull(normed_grad)
    input_grad = middle_grad + source_norm_grad
    decay_grad = lax.dynamic_update_slice_in_dim(
        jnp.zeros((feature_dimension,), jnp.float32), decay_grad_here, place * channels, 0
    )
    first_grad = lax.dynamic_update_slice_in_dim(
        jnp.zeros((feature_dimension,), jnp.float32), first_grad_here, place * channels, 0
    )
    grads = (
        grad_norm_gain,
        grad_norm_bias,
        *share_grads,
        decay_grad,
        first_grad,
        grad_key_weight,
        grad_value_weight,
        grad_gate_weight,
        grad_output_weight,
        grad_second_gain,
        grad_second_bias,
        *feed_share_grads,
        grad_feed_key,
        grad_feed_value,
        grad_feed_gate,
    )
    shares = []
    for grad in grads:
        for axis in ("seq", "sp"):
            grad = lax.psum_scatter(
                grad.astype(jnp.bfloat16), axis, scatter_dimension=0, tiled=True
            ).astype(jnp.float32)
        shares.append(grad)
    return (block_out, input_grad, *shares)


MESH = pl.DeviceIdType.MESH
F32 = jnp.float32
BF16 = jnp.bfloat16
GAIN1, BIAS1, MIXK, MIXV, MIXG, DECAY, FIRST, GAIN2, BIAS2, FMIXK, FMIXG = range(11)


def multiple(value, step):
    return pl.multiple_of(value, step)


def nn(a, b):
    return jnp.dot(a, b, preferred_element_type=F32)


def nt(a, b):
    return lax.dot_general(a, b, (((1,), (1,)), ((), ())), preferred_element_type=F32)


def tn(a, b):
    return lax.dot_general(a, b, (((0,), (0,)), ((), ())), preferred_element_type=F32)


def exact_dot(links, right):
    high = right.astype(BF16)
    rest = right - high.astype(F32)
    middle = rest.astype(BF16)
    low = (rest - middle.astype(F32)).astype(BF16)
    return nn(links, high) + nn(links, middle) + nn(links, low)


def iota(shape, axis):
    return lax.broadcasted_iota(jnp.int32, shape, axis)


def spread_rows(v):
    centered = v - jnp.mean(v, axis=1, keepdims=True)
    scale = lax.rsqrt(jnp.mean(centered * centered, axis=1, keepdims=True) + EPSILON)
    return centered * scale, scale


def column_sum(v):
    return jnp.sum(v, axis=0, keepdims=True)


def scratch_list():
    vm = pltpu.VMEM
    sem = pltpu.SemaphoreType.DMA
    return dict(
        xall=vm((1024, 1024), BF16),
        kin=vm((1024, 1024), BF16),
        vin=vm((1024, 1024), BF16),
        gin=vm((1024, 1024), BF16),
        spread=vm((1024, 1024), BF16),
        wkvg=vm((1024, 768), BF16),
        wo=vm((256, 1024), BF16),
        wfg=vm((8, 128, 1024), BF16),
        wfk=vm((1024, 1024), BF16),
        wfv=vm((1024, 1024), BF16),
        kk=vm((1024, 256), BF16),
        vv=vm((1024, 256), BF16),
        gate=vm((1024, 256), F32),
        mixed=vm((1024, 256), F32),
        inverse=vm((1024, 256), F32),
        gated=vm((1024, 256), BF16),
        carry=vm((8, 8, 256), F32),
        tables=vm((4, 128, 256), F32),
        small=vm((8, 256), F32),
        last=vm((8, 1024), F32),
        xo=vm((256, 1024), BF16),
        adj=vm((256, 1024), BF16),
        mid=vm((256, 1024), F32),
        sec=vm((264, 1024), F32),
        sig=vm((256, 1024), F32),
        fgin=vm((256, 1024), BF16),
        fpg=vm((256, 1024), BF16),
        fkall=vm((1024, 1024), BF16),
        cgall=vm((1024, 1024), BF16),
        hidden=vm((1024, 1024), BF16),
        relu=vm((1024, 1024), BF16),
        rgrad=vm((1024, 1024), BF16),
        acca=vm((256, 1024), F32),
        accb=vm((256, 1024), F32),
        fgg=vm((256, 1024), F32),
        moved=vm((264, 1024), F32),
        csa=vm((2, 256, 1024), BF16),
        cra=vm((2, 256, 1024), BF16),
        ysa=vm((256, 1024), BF16),
        yra=vm((256, 1024), BF16),
        csb=vm((2, 256, 1024), BF16),
        crb=vm((2, 256, 1024), BF16),
        ysb=vm((256, 1024), BF16),
        yrb=vm((256, 1024), BF16),
        fgcr=vm((2, 8, 32, 1024), BF16),
        fgyr=vm((8, 32, 1024), BF16),
        gfgs=vm((256, 1024), BF16),
        xrfv=vm((4, 128, 1024), BF16),
        xrfk=vm((4, 128, 1024), BF16),
        xrfg=vm((4, 32, 1024), BF16),
        xro=vm((4, 32, 1024), BF16),
        xrkvg=vm((4, 128, 768), BF16),
        zrfv=vm((3, 128, 1024), BF16),
        zrfk=vm((3, 128, 1024), BF16),
        zrfg=vm((3, 32, 1024), BF16),
        zro=vm((3, 32, 1024), BF16),
        zrkvg=vm((3, 128, 768), BF16),
        finfk=vm((128, 1024), BF16),
        finkvg=vm((128, 768), BF16),
        recfk=vm((4, 32, 1024), BF16),
        reckvg=vm((4, 32, 768), BF16),
        vraw=vm((8, 4, 16, 128), BF16),
        nat=vm((16, 1024), F32),
        chan=vm((16, 256), F32),
        vg=vm((16, 1024), F32),
        vgc=vm((16, 256), F32),
        vmsg=vm((8, 16, 128), F32),
        vrec=vm((8, 16, 128), F32),
        vtwo=vm((16, 128), F32),
        vrec2=vm((4, 16, 128), F32),
        ags=sem((6, 7)),
        agr=sem((6, 8)),
        a2s=sem((3, 3)),
        a2r=sem((3, 4)),
        sps=sem((5, 3)),
        spr=sem((5, 3)),
        rss=sem((5, 3)),
        rsr=sem((5, 3)),
        qxs=sem((5, 4)),
        qxr=sem((5, 4)),
        qzs=sem((5, 3)),
        qzr=sem((5, 3)),
        fas=sem((2, 3)),
        far=sem((2, 4)),
        vss=sem((2, 7)),
        vsr=sem((2, 8)),
        eds=sem((2,)),
        edr=sem((2,)),
        loc=sem((10,)),
    )


def step_kernel(
    ends, xin, adjoint, vecs, kvg_in, o_in, fg_in, fk_in, fv_in,
    out, xgrad, g_o, g_fg, g_fk, g_fv, g_kvg, g_vec,
    *scratch,
):
    t = types.SimpleNamespace(**dict(zip(scratch_list(), scratch)))
    s, p = lax.axis_index("seq"), lax.axis_index("sp")
    z, x, y, c = s // 2, s % 2, p // 2, p % 2
    zs = [(z + k) % 4 for k in range(4)]
    xdev = (z * 2 + 1 - x, p)
    ydev, sib = (s, (1 - y) * 2 + c), (s, y * 2 + 1 - c)
    sps = [(p + k) % 4 for k in range(4)]
    sqs = [(s + k) % 8 for k in range(8)]
    p_sib, p_y, p_diag = y * 2 + 1 - c, (1 - y) * 2 + c, (1 - y) * 2 + 1 - c

    pending = []

    def remote(src, dst, send_sem, recv_sem, device):
        return pltpu.make_async_remote_copy(
            src_ref=src, dst_ref=dst, send_sem=send_sem, recv_sem=recv_sem,
            device_id=device, device_id_type=MESH,
        )

    def send(src, dst, send_sem, recv_sem, device, tag=None):
        copy = remote(src, dst, send_sem, recv_sem, device)
        copy.start()
        pending.append((tag, copy))
        return copy

    def settle(*tags):
        for tag, copy in pending:
            if tag in tags:
                copy.wait_send()
        pending[:] = [(tag, copy) for tag, copy in pending if tag not in tags]

    def arrive(dst, recv_sem):
        remote(dst, dst, recv_sem, recv_sem, sib).wait_recv()

    def local(src, dst, k):
        copy = pltpu.make_async_copy(src, dst, t.loc.at[k])
        copy.start()
        return copy

    barrier = pltpu.get_barrier_semaphore()
    for k in range(1, 8):
        pl.semaphore_signal(barrier, inc=1, device_id=(sqs[k], p), device_id_type=MESH)
    for k in range(1, 4):
        pl.semaphore_signal(barrier, inc=1, device_id=(s, sps[k]), device_id_type=MESH)
    pl.semaphore_wait(barrier, 10)

    def rows(ref, size):
        return lambda i: ref.at[pl.ds(multiple(i * size, size), size)]

    V, A, B, C, D, E = range(6)
    block = {
        V: lambda i: t.vraw.at[i],
        A: rows(t.wkvg, 128),
        B: rows(t.wo, 32),
        C: lambda i: t.wfg.at[i, pl.ds(multiple(p * 32, 32), 32)],
        D: rows(t.wfk, 128),
        E: rows(t.wfv, 128),
    }

    def own_out(item, src):
        there = block[item](s)
        send(src, there, t.ags.at[item, 3], t.agr.at[item, s], xdev, item)
        for k in range(1, 4):
            send(src, there, t.ags.at[item, k - 1], t.agr.at[item, s], (zs[k] * 2 + x, p), item)

    def pass_on(item, k):
        i = zs[k] * 2 + x
        arrive(block[item](i), t.agr.at[item, i])
        send(block[item](i), block[item](i), t.ags.at[item, 3 + k], t.agr.at[item, i], xdev, item)

    def all_in(item):
        for k in range(4):
            i = zs[k] * 2 + 1 - x
            arrive(block[item](i), t.agr.at[item, i])

    def sp_out(n, view):
        send(view(p), view(p), t.sps.at[n, 0], t.spr.at[n, 0], ydev, ("sp", n))
        send(view(p), view(p), t.sps.at[n, 1], t.spr.at[n, 1], sib, ("sp", n))

    def sp_pass(n, view):
        arrive(view(p_y), t.spr.at[n, 0])
        send(view(p_y), view(p_y), t.sps.at[n, 2], t.spr.at[n, 2], sib, ("sp", n))

    def sp_sib(n, view):
        arrive(view(p_sib), t.spr.at[n, 1])

    def sp_diag(n, view):
        arrive(view(p_diag), t.spr.at[n, 2])

    def add_rows(n, fn):
        @pl.loop(0, n // 32)
        def _(i):
            fn(pl.ds(multiple(i * 32, 32), 32))

    def sum_begin(n, cs, cr, ys, yr, acc, compute):
        for j, q in enumerate((p_diag, p_sib)):
            cs[j] = compute(q).astype(BF16)
            send(cs.at[j], cr.at[j], t.rss.at[n, j], t.rsr.at[n, j], sib, ("sum", n))
        acc[...] = compute(p_y)
        arrive(cr.at[0], t.rsr.at[n, 0])

        def to_other(r):
            ys[r, :] = (acc[r, :] + cr[0, r, :].astype(F32)).astype(BF16)

        add_rows(256, to_other)
        send(ys, yr, t.rss.at[n, 2], t.rsr.at[n, 2], ydev, ("sum", n))
        acc[...] = compute(p)
        arrive(cr.at[1], t.rsr.at[n, 1])

        def to_own(r):
            acc[r, :] += cr[1, r, :].astype(F32)

        add_rows(256, to_own)

    def sum_end(n, yr, acc):
        arrive(yr, t.rsr.at[n, 2])

        def add(r):
            acc[r, :] += yr[r, :].astype(F32)

        add_rows(256, add)
        settle(("sum", n))

    FV, FK, FG, O, KVG = range(5)
    grads = {
        FV: (t.wfv, t.xrfv, t.zrfv, 128),
        FK: (t.wfk, t.xrfk, t.zrfk, 128),
        FG: (t.gfgs, t.xrfg, t.zrfg, 32),
        O: (t.wo, t.xro, t.zro, 32),
        KVG: (t.wkvg, t.xrkvg, t.zrkvg, 128),
    }

    def grad_x_out(item, zz):
        ref, xr, _, size = grads[item]
        send(rows(ref, size)(zz * 2 + 1 - x), xr.at[zz], t.qxs.at[item, zz], t.qxr.at[item, zz], xdev)

    def grad_x_in(item, k):
        ref, xr, zr, size = grads[item]
        zz = zs[k]
        arrive(xr.at[zz], t.qxr.at[item, zz])
        if k == 0:
            return
        base = (zz * 2 + x) * size

        def add(r):
            here = pl.ds(multiple(base + r.start, 32), 32)
            ref[here, :] = (ref[here, :].astype(F32) + xr[zz, r, :].astype(F32)).astype(BF16)

        add_rows(size, add)
        send(rows(ref, size)(zz * 2 + x), zr.at[k - 1], t.qzs.at[item, k - 1], t.qzr.at[item, k - 1], (zz * 2 + x, p))

    def grad_z_in(item, put):
        ref, xr, zr, size = grads[item]
        for k in range(1, 4):
            arrive(zr.at[k - 1], t.qzr.at[item, k - 1])

        def add(r):
            here = pl.ds(multiple(s * size + r.start, 32), 32)
            total = ref[here, :].astype(F32) + xr[z, r, :].astype(F32)
            total = total + zr[0, r, :].astype(F32) + zr[1, r, :].astype(F32) + zr[2, r, :].astype(F32)
            put(r, total)

        add_rows(size, add)

    def hand_back(n, fin, rec):
        for k in range(1, 4):
            send(fin.at[pl.ds(multiple(sps[k] * 32, 32), 32)], rec.at[p], t.fas.at[n, k - 1], t.far.at[n, p], (s, sps[k]))
        rec[p] = fin[pl.ds(multiple(p * 32, 32), 32), :]

    def handed_back(n, rec):
        for k in range(1, 4):
            arrive(rec.at[sps[k]], t.far.at[n, sps[k]])

    e0, e1, e2, e3 = ends[0], ends[1], ends[2], ends[3]

    def label(pos):
        total = (pos >= 0).astype(jnp.int32)
        for edge in (e0, e1, e2, e3):
            total = total + (pos >= edge).astype(jnp.int32)
        return total - 1

    def same_at(pos):
        return (label(pos) == label(pos - 1)).astype(F32)

    xview = rows(t.xall, 256)
    copies = [
        local(vecs, t.vraw.at[s, p], 0),
        local(kvg_in.at[p], t.wkvg.at[pl.ds(multiple(s * 128 + p * 32, 32), 32)], 1),
        local(fk_in.at[p], t.wfk.at[pl.ds(multiple(s * 128 + p * 32, 32), 32)], 2),
        local(xin, xview(p), 3),
        local(o_in, block[B](s), 4),
        local(fg_in, block[C](s), 5),
        local(fv_in, block[E](s), 6),
        local(xin, t.xo, 7),
        local(adjoint, t.adj, 8),
    ]

    def a2a_out(n, src, dst):
        for k in range(1, 4):
            send(src(sps[k]), dst(p), t.a2s.at[n, k - 1], t.a2r.at[n, p], (s, sps[k]))

    def a2a_in(n, dst):
        for k in range(1, 4):
            arrive(dst(sps[k]), t.a2r.at[n, sps[k]])

    vec_dst = lambda i: t.vraw.at[s, i]
    kvg_dst = lambda i: t.wkvg.at[pl.ds(multiple(s * 128 + i * 32, 32), 32)]
    fk_dst = lambda i: t.wfk.at[pl.ds(multiple(s * 128 + i * 32, 32), 32)]
    a2a_out(0, lambda i: vecs, vec_dst)
    a2a_out(1, lambda i: kvg_in.at[i], kvg_dst)
    send(xin, xview(p), t.sps.at[0, 0], t.spr.at[0, 0], ydev)
    send(xin, xview(p), t.sps.at[0, 1], t.spr.at[0, 1], sib)
    a2a_out(2, lambda i: fk_in.at[i], fk_dst)
    for copy in copies:
        copy.wait()
    a2a_in(0, vec_dst)
    own_out(V, t.vraw.at[s])
    a2a_in(1, kvg_dst)
    own_out(A, block[A](s))
    own_out(B, o_in)
    own_out(C, fg_in)
    for k in range(1, 4):
        pass_on(V, k)
    all_in(V)

    t.last[...] = jnp.zeros_like(t.last)
    t.vg[...] = jnp.zeros_like(t.vg)
    t.vgc[...] = jnp.zeros_like(t.vgc)
    for i in range(8):
        total = t.vraw[i, 0].astype(F32)
        for j in range(1, 4):
            total = total + pltpu.roll(t.vraw[i, j].astype(F32), 32 * j, 1)
        t.nat[:, 128 * i : 128 * i + 128] = total
    for i in range(2):
        total = t.vraw[4 * i, p].astype(F32)
        for j in range(1, 4):
            total = total + pltpu.roll(t.vraw[4 * i + j, p].astype(F32), 32 * j, 1)
        t.chan[:, 128 * i : 128 * i + 128] = total

    def vector(k):
        return t.nat[k : k + 1, :]

    rate = jnp.exp(t.chan[DECAY : DECAY + 1, :])
    offset = iota((128, 1), 0).astype(F32)
    t.tables[0] = jnp.exp(offset * rate)
    t.tables[1] = jnp.exp(-(offset - 1.0) * rate)
    t.tables[2] = jnp.exp(-offset * rate)
    t.tables[3] = jnp.exp(-(127.0 - offset) * rate)
    t.small[0:1, :] = jnp.exp(-128.0 * rate)
    t.small[1:2, :] = jnp.exp(t.chan[FIRST : FIRST + 1, :])
    t.small[2:3, :] = rate

    sp_pass(0, xview)
    sp_sib(0, xview)
    sp_diag(0, xview)

    def norm_quarter(q):
        @pl.loop(0, 8)
        def _(i):
            base = q * 256 + i * 32
            r = pl.ds(multiple(base, 32), 32)
            hat, _ = spread_rows(t.xall[r, :].astype(F32))
            normed = hat * vector(GAIN1) + vector(BIAS1)
            row = iota((32, 1), 0)
            prior = jnp.where(row == 0, t.last[0:1, :], pltpu.roll(normed, 1, 0))
            prior = prior * same_at(base + row)
            t.last[0:1, :] = normed[31:32, :]
            diff = normed - prior
            t.spread[r, :] = diff.astype(BF16)
            t.kin[r, :] = (prior + diff * vector(MIXK)).astype(BF16)
            t.vin[r, :] = (prior + diff * vector(MIXV)).astype(BF16)
            t.gin[r, :] = (prior + diff * vector(MIXG)).astype(BF16)

    for q in range(4):
        norm_quarter(q)
        if q > 0:
            pass_on(A, q)
    a2a_in(2, fk_dst)
    own_out(D, block[D](s))
    for k in range(1, 4):
        pass_on(B, k)
        pass_on(C, k)
    own_out(E, fv_in)
    all_in(A)

    settle(("sp", 0))

    @pl.loop(0, 4)
    def _(i):
        r = pl.ds(multiple(i * 256, 256), 256)
        t.kk[r, :] = nn(t.kin[r, :], t.wkvg[:, 0:256]).astype(BF16)
        t.vv[r, :] = nn(t.vin[r, :], t.wkvg[:, 256:512]).astype(BF16)
        t.gate[r, :] = jax.nn.sigmoid(nn(t.gin[r, :], t.wkvg[:, 512:768]))

    pass_on(D, 1)

    def block_parts(b):
        base = b * 128
        column = label(base + iota((128, 1), 0))
        row = label(base + iota((1, 128), 1))
        before, end = label(base - 1), label(base + 127)
        alike = column == row
        keep = (before == end).astype(F32) * t.small[0:1, :]
        memory = (column == before).astype(F32) * t.tables[2]
        tail = (column == end).astype(F32) * t.tables[3]
        return alike, keep, memory, tail

    def forward_block(b, held):
        top, bottom = held
        r = pl.ds(multiple(b * 128, 128), 128)
        alike, keep, memory, tail = block_parts(b)
        links = (alike & (iota((128, 128), 1) < iota((128, 128), 0))).astype(F32).astype(BF16)
        v = t.vv[r, :].astype(F32)
        weight = jnp.exp(t.kk[r, :].astype(F32))
        scaled = t.tables[0] * weight
        sums = exact_dot(links, jnp.concatenate([scaled * v, scaled], axis=1))
        own = t.small[1:2, :] * weight
        high = t.tables[1] * sums[:, :256] + memory * top + own * v
        low = t.tables[1] * sums[:, 256:] + memory * bottom + own
        inverse = 1.0 / low
        mixed = high * inverse
        t.inverse[r, :] = inverse
        t.mixed[r, :] = mixed
        t.gated[r, :] = (t.gate[r, :] * mixed.astype(BF16).astype(F32)).astype(BF16)
        t.carry[b, 0:1, :] = top
        t.carry[b, 1:2, :] = bottom
        tail = tail * weight
        return keep * top + column_sum(tail * v), keep * bottom + column_sum(tail)

    zero = jnp.zeros((1, 256), F32)
    held = lax.fori_loop(0, 4, forward_block, (zero, zero))
    pass_on(D, 2)
    held = lax.fori_loop(4, 8, forward_block, held)
    pass_on(D, 3)

    all_in(B)

    def quarter(ref, q):
        return ref[pl.ds(multiple(q * 256, 256), 256), :]

    sum_begin(0, t.csa, t.cra, t.ysa, t.yra, t.acca, lambda q: nn(quarter(t.gated, q), t.wo[...]))
    pass_on(E, 1)
    all_in(C)
    fgview = lambda i: t.wfg.at[:, pl.ds(multiple(i * 32, 32), 32)]
    sp_out(1, fgview)
    sum_end(0, t.yra, t.acca)

    def second_tile(i):
        r = pl.ds(multiple(i * 32, 32), 32)
        middle = t.xo[r, :].astype(F32) + t.acca[r, :]
        t.mid[r, :] = middle
        hat, _ = spread_rows(middle)
        t.sec[pl.ds(multiple(8 + i * 32, 8), 32), :] = hat * vector(GAIN2) + vector(BIAS2)

    second_tile(7)
    up_edge = remote(t.sec.at[pl.ds(256, 8)], t.sec.at[pl.ds(0, 8)], t.eds.at[0], t.edr.at[0], (s, sps[1]))

    @pl.when(p < 3)
    def _():
        up_edge.start()

    @pl.when(p == 0)
    def _():
        t.sec[0:8, :] = jnp.zeros((8, 1024), F32)

    @pl.loop(0, 7)
    def _(i):
        second_tile(i)

    @pl.when(p > 0)
    def _():
        remote(t.sec.at[pl.ds(0, 8)], t.sec.at[pl.ds(0, 8)], t.eds.at[0], t.edr.at[0], sib).wait_recv()

    @pl.when(p < 3)
    def _():
        up_edge.wait_send()

    def second_pair(i):
        wide = t.sec[pl.ds(multiple(i * 32, 32), 40), :]
        pos = p * 256 + i * 32 + iota((32, 1), 0)
        return wide[8:40], pltpu.roll(wide, 33, 0)[0:32] * same_at(pos)

    @pl.loop(0, 8)
    def _(i):
        second, prior = second_pair(i)
        diff = second - prior
        t.fkall[pl.ds(multiple(p * 256 + i * 32, 32), 32), :] = (prior + diff * vector(FMIXK)).astype(BF16)
        t.fgin[pl.ds(multiple(i * 32, 32), 32), :] = (prior + diff * vector(FMIXG)).astype(BF16)

    fkview = rows(t.fkall, 256)
    cgview = rows(t.cgall, 256)
    sp_out(2, fkview)
    sp_pass(1, fgview)
    sp_sib(1, fgview)
    sp_diag(1, fgview)
    pass_on(E, 2)

    def feed_gate_weight():
        return t.wfg[...].reshape(1024, 1024)

    t.sig[...] = jax.nn.sigmoid(nn(t.fgin[...], feed_gate_weight()))

    def upstream(i):
        pos = p * 256 + i * 32 + iota((32, 1), 0)
        return t.adj[pl.ds(multiple(i * 32, 32), 32), :].astype(F32) * (pos < e3).astype(F32)

    @pl.loop(0, 8)
    def _(i):
        r = pl.ds(multiple(i * 32, 32), 32)
        t.cgall[pl.ds(multiple(p * 256 + i * 32, 32), 32), :] = (upstream(i) * t.sig[r, :]).astype(BF16)

    sp_out(3, cgview)
    pass_on(E, 3)
    all_in(D)

    def raise_rows(q):
        r = pl.ds(multiple(q * 256, 256), 256)
        relu = jnp.maximum(nn(t.fkall[r, :], t.wfk[...]), 0.0)
        t.relu[r, :] = relu.astype(BF16)
        t.hidden[r, :] = (relu * relu).astype(BF16)

    raise_rows(p)
    sp_sib(2, fkview)
    raise_rows(p_sib)
    sp_pass(2, fkview)
    raise_rows(p_y)
    all_in(E)
    sp_diag(2, fkview)
    raise_rows(p_diag)
    sum_begin(1, t.csb, t.crb, t.ysb, t.yrb, t.accb, lambda q: nn(quarter(t.hidden, q), t.wfv[...]))

    def lower_rows(q):
        r = pl.ds(multiple(q * 256, 256), 256)
        t.rgrad[r, :] = (nt(t.cgall[r, :], t.wfv[...]) * 2.0 * t.relu[r, :].astype(F32)).astype(BF16)

    sp_pass(3, cgview)
    sp_sib(3, cgview)
    sp_diag(3, cgview)
    for q in (p_diag, p_sib, p_y, p):
        lower_rows(q)
    sum_begin(2, t.csa, t.cra, t.ysa, t.yra, t.acca, lambda q: nt(quarter(t.rgrad, q), t.wfk[...]))

    settle(E)
    for k in range(4):
        r = pl.ds(256 * k, 256)
        t.wfv[r, :] = tn(t.hidden[:, 256 * k : 256 * k + 256], t.cgall[...]).astype(BF16)
        grad_x_out(FV, k)

    sum_end(1, t.yrb, t.accb)

    @pl.loop(0, 8)
    def _(i):
        r = pl.ds(multiple(i * 32, 32), 32)
        pos = p * 256 + i * 32 + iota((32, 1), 0)
        live = (pos < e3).astype(F32)
        sig, total, up = t.sig[r, :], t.accb[r, :], upstream(i)
        out[r, :] = (live * (t.mid[r, :] + sig * total)).astype(BF16)
        t.fpg[r, :] = (up * total * sig * (1.0 - sig)).astype(BF16)

    t.fgg[...] = nt(t.fpg[...], feed_gate_weight())
    settle(C, ("sp", 1))
    for k in range(4):
        part = tn(t.fgin[:, 256 * k : 256 * k + 256], t.fpg[...]).astype(BF16)
        t.wfg[2 * k : 2 * k + 2] = part.reshape(2, 128, 1024)
    for j, q in enumerate((p_diag, p_sib)):
        send(fgview(q), t.fgcr.at[j], t.rss.at[4, j], t.rsr.at[4, j], sib)
    sum_end(2, t.yra, t.acca)

    @pl.loop(0, 8)
    def _(i):
        r = pl.ds(multiple(i * 32, 32), 32)
        pos = p * 256 + i * 32 + iota((32, 1), 0)
        through = t.acca[r, :] * (1.0 - vector(FMIXK)) + t.fgg[r, :] * (1.0 - vector(FMIXG))
        t.moved[r, :] = through * same_at(pos)

    down_edge = remote(t.moved.at[pl.ds(0, 8)], t.moved.at[pl.ds(256, 8)], t.eds.at[1], t.edr.at[1], (s, sps[3]))

    @pl.when(p > 0)
    def _():
        down_edge.start()

    @pl.when(p == 3)
    def _():
        t.moved[256:264, :] = jnp.zeros((8, 1024), F32)

    for k in range(1, 4):
        grad_x_in(FV, k)

    @pl.when(p < 3)
    def _():
        remote(t.moved.at[pl.ds(256, 8)], t.moved.at[pl.ds(256, 8)], t.eds.at[1], t.edr.at[1], sib).wait_recv()

    @pl.when(p > 0)
    def _():
        down_edge.wait_send()

    def norm_back(hat, scale, grad, gain):
        grad = grad * gain
        return scale * (
            grad - jnp.mean(grad, axis=1, keepdims=True) - hat * jnp.mean(grad * hat, axis=1, keepdims=True)
        )

    def add_vector(k, v):
        t.vg[k : k + 1, :] += column_sum(v)

    @pl.loop(0, 8)
    def _(i):
        r = pl.ds(multiple(i * 32, 32), 32)
        after = pltpu.roll(t.moved[pl.ds(multiple(i * 32, 32), 40), :], 39, 0)[0:32]
        by_key, by_gate = t.acca[r, :], t.fgg[r, :]
        grad = by_key * vector(FMIXK) + by_gate * vector(FMIXG) + after
        second, prior = second_pair(i)
        diff = second - prior
        hat, scale = spread_rows(t.mid[r, :])
        add_vector(FMIXK, diff * by_key)
        add_vector(FMIXG, diff * by_gate)
        add_vector(GAIN2, grad * hat)
        add_vector(BIAS2, grad)
        total = upstream(i) + norm_back(hat, scale, grad, vector(GAIN2))
        t.mid[r, :] = total
        t.xall[pl.ds(multiple(p * 256 + i * 32, 32), 32), :] = total.astype(BF16)

    agview = xview
    sp_out(4, agview)

    settle(D)
    for k in range(4):
        r = pl.ds(256 * k, 256)
        t.wfk[r, :] = tn(t.fkall[:, 256 * k : 256 * k + 256], t.rgrad[...]).astype(BF16)
        grad_x_out(FK, k)
    arrive(t.fgcr.at[0], t.rsr.at[4, 0])
    there = pl.ds(multiple(p_y * 32, 32), 32)

    @pl.loop(0, 8)
    def _(i):
        t.wfg[i, there, :] = (t.wfg[i, there, :].astype(F32) + t.fgcr[0, i].astype(F32)).astype(BF16)

    send(fgview(p_y), t.fgyr, t.rss.at[4, 2], t.rsr.at[4, 2], ydev)
    sp_pass(4, agview)
    sp_sib(4, agview)
    sp_diag(4, agview)

    @pl.loop(0, 4)
    def _(i):
        r = pl.ds(multiple(i * 256, 256), 256)
        grad = nt(t.xall[r, :], t.wo[...])
        gate = t.gate[r, :]
        t.hidden[r, 0:256] = (grad * gate).astype(BF16)
        t.hidden[r, 256:512] = (grad * t.mixed[r, :].astype(BF16).astype(F32) * gate * (1.0 - gate)).astype(BF16)

    def put_fv(r, v):
        g_fv[r, :] = v

    settle(B)
    t.wo[...] = tn(t.gated[...], t.xall[...]).astype(BF16)
    for k in range(1, 4):
        grad_x_in(FK, k)
    for k in range(4):
        grad_x_out(O, k)

    def backward_block(k, held):
        b = 7 - k
        d_top, d_bottom, d_first, d_rate = held
        r = pl.ds(multiple(b * 128, 128), 128)
        alike, keep, memory, tail = block_parts(b)
        later = (alike & (iota((128, 128), 1) > iota((128, 128), 0))).astype(F32).astype(BF16)
        top, bottom = t.carry[b, 0:1, :], t.carry[b, 1:2, :]
        v = t.vv[r, :].astype(F32)
        weight = jnp.exp(t.kk[r, :].astype(F32))
        d_high = t.hidden[r, 0:256].astype(F32) * t.inverse[r, :]
        d_low = -d_high * t.mixed[r, :]
        shrink = t.tables[1]
        sums = exact_dot(later, jnp.concatenate([shrink * d_high, shrink * d_low], axis=1))
        scaled = t.tables[0] * weight
        own = t.small[1:2, :] * weight
        tail = tail * weight
        by_sum = scaled * (v * sums[:, :256] + sums[:, 256:])
        by_own = own * (v * d_high + d_low)
        by_tail = tail * (v * d_top + d_bottom)
        by_memory = memory * (top * d_high + bottom * d_low)
        t.vv[r, :] = (scaled * sums[:, :256] + own * d_high + tail * d_top).astype(BF16)
        t.kk[r, :] = (by_sum + by_own + by_tail).astype(BF16)
        place = iota((128, 1), 0).astype(F32)
        d_rate = d_rate + column_sum(
            place * by_sum + (place - 1.0) * by_own - by_memory - (127.0 - place) * by_tail
        )
        d_rate = d_rate - 128.0 * keep * (top * d_top + bottom * d_bottom)
        d_first = d_first + column_sum(by_own)
        d_top = keep * d_top + column_sum(memory * d_high)
        d_bottom = keep * d_bottom + column_sum(memory * d_low)
        return d_top, d_bottom, d_first, d_rate

    held = lax.fori_loop(0, 4, backward_block, (zero, zero, zero, zero))
    grad_x_in(FV, 0)
    grad_z_in(FV, put_fv)
    held = lax.fori_loop(4, 8, backward_block, held)
    t.vgc[DECAY : DECAY + 1, :] = held[3] * t.small[2:3, :]
    t.vgc[FIRST : FIRST + 1, :] = held[2]

    t.last[...] = jnp.zeros_like(t.last)

    @pl.loop(0, 8)
    def _(k):
        i = 7 - k
        r = pl.ds(multiple(i * 128, 128), 128)
        t.acca[0:128, :] = nt(t.kk[r, :], t.wkvg[:, 0:256])
        t.acca[128:256, :] = nt(t.vv[r, :], t.wkvg[:, 256:512])
        t.fgg[0:128, :] = nt(t.hidden[r, 256:512], t.wkvg[:, 512:768])

        @pl.loop(0, 4)
        def _(kk):
            j = 3 - kk
            u = multiple(j * 32, 32)
            base = i * 128 + j * 32
            here = pl.ds(multiple(base, 32), 32)
            by_key, by_value, by_gate = t.acca[pl.ds(u, 32), :], t.acca[pl.ds(128 + u, 32), :], t.fgg[pl.ds(u, 32), :]
            diff = t.spread[here, :].astype(F32)
            add_vector(MIXK, diff * by_key)
            add_vector(MIXV, diff * by_value)
            add_vector(MIXG, diff * by_gate)
            current = by_key * vector(MIXK) + by_value * vector(MIXV) + by_gate * vector(MIXG)
            row = iota((32, 1), 0)
            through = (by_key + by_value + by_gate - current) * same_at(base + row)
            after = jnp.where(row == 31, t.last[0:1, :], pltpu.roll(through, 31, 0))
            t.last[0:1, :] = through[0:1, :]
            t.relu[here, :] = (current + after).astype(BF16)

    sum_begin(3, t.csb, t.crb, t.ysb, t.yrb, t.accb, lambda q: quarter(t.relu, q).astype(F32))

    settle(A)
    for k in range(4):
        r, q = pl.ds(256 * k, 256), slice(256 * k, 256 * k + 256)
        t.wkvg[r, 0:256] = tn(t.kin[:, q], t.kk[...]).astype(BF16)
        t.wkvg[r, 256:512] = tn(t.vin[:, q], t.vv[...]).astype(BF16)
        t.wkvg[r, 512:768] = tn(t.gin[:, q], t.hidden[:, 256:512]).astype(BF16)
        grad_x_out(KVG, k)

    arrive(t.fgcr.at[1], t.rsr.at[4, 1])
    arrive(t.fgyr, t.rsr.at[4, 2])
    mine = pl.ds(multiple(p * 32, 32), 32)

    @pl.loop(0, 8)
    def _(i):
        total = t.wfg[i, mine, :].astype(F32) + t.fgcr[1, i].astype(F32) + t.fgyr[i].astype(F32)
        t.gfgs[pl.ds(multiple(i * 32, 32), 32), :] = total.astype(BF16)

    for k in range(4):
        grad_x_out(FG, k)
    for k in range(1, 4):
        grad_x_in(O, k)

    def put_fk(r, v):
        t.finfk[r, :] = v.astype(BF16)

    grad_x_in(FK, 0)
    grad_z_in(FK, put_fk)
    hand_back(0, t.finfk, t.recfk)
    for k in range(1, 4):
        grad_x_in(KVG, k)
    for k in range(1, 4):
        grad_x_in(FG, k)

    sum_end(3, t.yrb, t.accb)

    @pl.loop(0, 8)
    def _(i):
        r = pl.ds(multiple(i * 32, 32), 32)
        hat, scale = spread_rows(t.xo[r, :].astype(F32))
        grad = t.accb[r, :]
        add_vector(GAIN1, grad * hat)
        add_vector(BIAS1, grad)
        xgrad[r, :] = t.mid[r, :] + norm_back(hat, scale, grad, vector(GAIN1))

    lane = iota((16, 128), 1)
    mine_lanes = (lane >= 32 * p) & (lane < 32 * p + 32)
    for i in range(8):
        tile = t.vgc[:, 128 * (i // 4) : 128 * (i // 4) + 128]
        moved = pltpu.roll(tile, (32 * p + 128 - 32 * (i % 4)) % 128, 1)
        t.vmsg[i] = t.vg[:, 128 * i : 128 * i + 128] + jnp.where(mine_lanes, moved, 0.0)
    for k in range(1, 8):
        send(t.vmsg.at[sqs[k]], t.vrec.at[k], t.vss.at[0, k - 1], t.vsr.at[0, k], (sqs[k], p))

    def put_o(r, v):
        g_o[r, :] = v

    def put_fg(r, v):
        g_fg[r, :] = v

    def put_kvg(r, v):
        t.finkvg[r, :] = v.astype(BF16)

    grad_x_in(O, 0)
    grad_z_in(O, put_o)
    total = t.vmsg[s]
    for k in range(1, 8):
        arrive(t.vrec.at[k], t.vsr.at[0, k])
        total = total + t.vrec[k]
    t.vtwo[...] = total
    for k in range(1, 4):
        send(t.vtwo, t.vrec2.at[k], t.vss.at[1, k - 1], t.vsr.at[1, k], (s, sps[k]))
    grad_x_in(FG, 0)
    grad_z_in(FG, put_fg)
    grad_x_in(KVG, 0)
    grad_z_in(KVG, put_kvg)
    hand_back(1, t.finkvg, t.reckvg)
    total = t.vtwo[...]
    for k in range(1, 4):
        arrive(t.vrec2.at[k], t.vsr.at[1, k])
        total = total + t.vrec2[k]
    g_vec[...] = total
    handed_back(0, t.recfk)
    for i in range(8):
        for j in range(4):
            g_fk[:, 512 * i + 128 * j : 512 * i + 128 * j + 128] = t.recfk[j, :, 128 * i : 128 * i + 128].astype(F32)
    handed_back(1, t.reckvg)
    g_kvg[...] = t.reckvg[...]
    for _, copy in pending:
        copy.wait_send()


def fast_body(
    incoming_signal,
    document_extents,
    adjoint_signal,
    layernorm_scaling,
    layernorm_offset,
    temporal_blend_lookup,
    temporal_blend_content,
    temporal_blend_receptor,
    temporal_shrinkage_log,
    diagonal_reward,
    lookup_projection,
    content_projection,
    receptor_projection,
    emission_projection,
    latter_scaling,
    latter_offset,
    channel_blend_lookup,
    channel_blend_receptor,
    channel_mixer_lookup,
    channel_mixer_content,
    channel_mixer_receptor,
):
    ends = jnp.stack(running(document_extents[0]))
    vecs = jnp.stack(
        [
            layernorm_scaling,
            layernorm_offset,
            temporal_blend_lookup,
            temporal_blend_content,
            temporal_blend_receptor,
            temporal_shrinkage_log,
            diagonal_reward,
            latter_scaling,
            latter_offset,
            channel_blend_lookup,
            channel_blend_receptor,
        ]
    )
    vecs = jnp.pad(vecs, ((0, 5), (0, 96)))

    def by_part(weight, width):
        return weight.reshape(32, 8, 4, width).transpose(2, 0, 1, 3).reshape(4, 32, 8 * width)

    kvg = jnp.concatenate(
        [by_part(w, 32) for w in (lookup_projection, content_projection, receptor_projection)], axis=2
    )
    fk = by_part(channel_mixer_lookup, 128)
    anywhere = pl.BlockSpec(memory_space=pl.ANY)
    vmem = pl.BlockSpec(memory_space=pltpu.VMEM)
    shape = jax.ShapeDtypeStruct
    out, xgrad, g_o, g_fg, g_fk, g_fv, g_kvg, g_vec = pl.pallas_call(
        step_kernel,
        out_shape=(
            shape((256, 1024), BF16),
            shape((256, 1024), F32),
            shape((32, 1024), F32),
            shape((32, 1024), F32),
            shape((32, 4096), F32),
            shape((128, 1024), F32),
            shape((4, 32, 768), BF16),
            shape((16, 128), F32),
        ),
        in_specs=[pl.BlockSpec(memory_space=pltpu.SMEM)] + [anywhere] * 8,
        out_specs=[vmem] * 8,
        scratch_shapes=list(scratch_list().values()),
        compiler_params=pltpu.CompilerParams(
            collective_id=0, has_side_effects=True, vmem_limit_bytes=63 * 1024 * 1024
        ),
    )(
        ends,
        incoming_signal,
        adjoint_signal,
        vecs,
        kvg,
        emission_projection,
        channel_mixer_receptor,
        fk,
        channel_mixer_content,
    )
    g_k, g_v, g_g = (
        g_kvg[:, :, 256 * i : 256 * i + 256]
        .reshape(4, 32, 8, 32)
        .transpose(1, 2, 0, 3)
        .reshape(32, 1024)
        .astype(F32)
        for i in range(3)
    )
    mine = lax.dynamic_slice_in_dim(g_vec, 32 * lax.axis_index("sp"), 32, 1)
    v = [mine[i] for i in range(11)]
    return (out, xgrad, *v[:7], g_k, g_v, g_g, g_o, *v[7:], g_fk, g_fv, g_fg)


def solution(mesh):
    fast = (mesh.shape["seq"], mesh.shape["sp"]) == (8, 4)
    flat, wide = P(("seq", "sp")), P(("seq", "sp"), None)
    return jax.shard_map(
        fast_body if fast else plain_body,
        mesh=mesh,
        in_specs=(wide, P("seq", None), wide, *[flat] * 7, *[wide] * 4, *[flat] * 4, *[wide] * 3),
        out_specs=(wide, wide, *[flat] * 7, *[wide] * 4, *[flat] * 4, *[wide] * 3),
        check_vma=False,
    )
```

```python
import functools
import types

import jax
import jax.numpy as jnp
from jax import lax
from jax.experimental import pallas as pl
from jax.experimental.pallas import tpu as pltpu
from jax.sharding import PartitionSpec as P

LOOP_LENGTH = 128


HIGHEST = lax.Precision.HIGHEST
EPSILON = 1e-05


def shifted(value, axis, steps):
    count = lax.axis_size(axis)
    first, last = (max(0, -steps), min(count, count - steps))
    return lax.ppermute(value, axis, [(source, source + steps) for source in range(first, last)])


def norm_rows(content_vectors, gain, bias):
    centered = content_vectors - jnp.mean(content_vectors, axis=1, keepdims=True)
    scale = lax.rsqrt(jnp.mean(centered * centered, axis=1, keepdims=True) + EPSILON)
    return centered * scale * gain + bias


def running(lengths_row):
    ends = [lengths_row[0]]
    for i in range(1, lengths_row.shape[0]):
        ends.append(ends[-1] + lengths_row[i])
    return ends


def segment_ids(lengths_row, positions):
    ends = jnp.stack(running(lengths_row))
    bounds = jnp.concatenate([ends - lengths_row, ends[-1:]])
    document_tags = jnp.sum((positions[:, None] >= bounds[None, :]).astype(jnp.int32), axis=1) - 1
    return (document_tags, positions < ends[-1])


def weighted_attention_loop(
    lookup_vectors,
    content_vectors,
    temporal_shrinkage_log,
    diagonal_reward,
    document_tags,
    segment_piece,
):
    count, feature_dimension = lookup_vectors.shape
    blocks = count // segment_piece
    rate = jnp.exp(temporal_shrinkage_log)
    offsets = jnp.arange(segment_piece, dtype=jnp.float32)[:, None]
    grow = jnp.exp(offsets * rate)
    shrink_multiplier = jnp.exp(-(offsets - 1.0) * rate)
    fade = jnp.exp(-offsets * rate)
    tail_fade = jnp.exp(-(segment_piece - 1.0 - offsets) * rate)
    whole_fade = jnp.exp(-1.0 * segment_piece * rate)
    order = jnp.arange(segment_piece, dtype=jnp.int32)
    lower = order[None, :] < order[:, None]
    key_blocks = lookup_vectors.reshape(blocks, segment_piece, feature_dimension)
    value_blocks = content_vectors.reshape(blocks, segment_piece, feature_dimension)
    label_blocks = document_tags.reshape(blocks, segment_piece)
    before = jnp.concatenate([jnp.full((1,), -1, jnp.int32), label_blocks[:-1, -1]])

    @jax.checkpoint
    def advance(carry, items):
        dividend_total, divisor_total = carry
        lookup_portion, content_portion, label_part, last_label = items
        weight_key = jnp.exp(lookup_portion)
        links = ((label_part[:, None] == label_part[None, :]) & lower).astype(jnp.float32)
        scaled = grow * weight_key
        cumulative_totals = jnp.dot(
            links, jnp.concatenate([scaled * content_portion, scaled], axis=1), precision=HIGHEST
        )
        recurrent_memory = (label_part == last_label).astype(jnp.float32)[:, None] * fade
        initial_reward = jnp.exp(diagonal_reward + lookup_portion)
        highest_line_entry = (
            shrink_multiplier * cumulative_totals[:, :feature_dimension]
            + recurrent_memory * dividend_total
            + initial_reward * content_portion
        )
        lowest_line_entry = (
            shrink_multiplier * cumulative_totals[:, feature_dimension:]
            + recurrent_memory * divisor_total
            + initial_reward
        )
        end_label = label_part[-1]
        keep = (end_label == last_label).astype(jnp.float32) * whole_fade
        tail = (label_part == end_label).astype(jnp.float32)[:, None] * tail_fade * weight_key
        dividend_total = keep * dividend_total + jnp.sum(tail * content_portion, axis=0)
        divisor_total = keep * divisor_total + jnp.sum(tail, axis=0)
        return ((dividend_total, divisor_total), highest_line_entry / lowest_line_entry)

    zeros = jnp.zeros((feature_dimension,), jnp.float32)
    _, blended_signal = lax.scan(
        advance, (zeros, zeros), (key_blocks, value_blocks, label_blocks, before)
    )
    return blended_signal.reshape(count, feature_dimension)


def product(left, right):
    return jnp.dot(left, right, preferred_element_type=jnp.float32)


def times_transposed(left, right):
    return lax.dot_general(
        left, right, (((1,), (1,)), ((), ())), preferred_element_type=jnp.float32
    )


def outer_sum(left, right):
    return lax.dot_general(
        left, right, (((0,), (0,)), ((), ())), preferred_element_type=jnp.float32
    )


def blend(current, prior, share):
    return current * share + prior * (1.0 - share)


def blend_back(current, prior, shares, grads):
    current_grad = jnp.zeros_like(current)
    prior_grad = jnp.zeros_like(current)
    spread = current - prior
    share_grads = []
    for share, grad in zip(shares, grads):
        current_grad = current_grad + grad * share
        prior_grad = prior_grad + grad * (1.0 - share)
        share_grads.append(jnp.sum(spread * grad, axis=0))
    return (current_grad, prior_grad, share_grads)


def plain_body(
    incoming_signal,
    document_extents,
    adjoint_signal,
    layernorm_scaling,
    layernorm_offset,
    temporal_blend_lookup,
    temporal_blend_content,
    temporal_blend_receptor,
    temporal_shrinkage_log,
    diagonal_reward,
    lookup_projection,
    content_projection,
    receptor_projection,
    emission_projection,
    latter_scaling,
    latter_offset,
    channel_blend_lookup,
    channel_blend_receptor,
    channel_mixer_lookup,
    channel_mixer_content,
    channel_mixer_receptor,
):
    rows = incoming_signal.shape[0]
    feature_dimension = incoming_signal.shape[1]
    parts = lax.axis_size("sp")
    place = lax.axis_index("sp")
    group_rows = rows * parts
    channels = feature_dimension // parts
    lengths_row = document_extents[0]
    positions = place * rows + jnp.arange(rows, dtype=jnp.int32)
    document_tags, live = segment_ids(lengths_row, positions)
    earlier, _ = segment_ids(lengths_row, positions - 1)
    same = (document_tags == earlier).astype(jnp.float32)[:, None]
    live_rows = live.astype(jnp.float32)[:, None]
    group_labels, _ = segment_ids(lengths_row, jnp.arange(group_rows, dtype=jnp.int32))
    fetched = [
        lax.all_gather(piece, ("seq", "sp"), axis=0, tiled=True)
        for piece in (
            layernorm_scaling,
            layernorm_offset,
            temporal_blend_lookup,
            temporal_blend_content,
            temporal_blend_receptor,
            temporal_shrinkage_log,
            diagonal_reward,
            lookup_projection,
            content_projection,
            receptor_projection,
            emission_projection,
            latter_scaling,
            latter_offset,
            channel_blend_lookup,
            channel_blend_receptor,
            channel_mixer_lookup,
            channel_mixer_content,
            channel_mixer_receptor,
        )
    ]
    vectors = [fetched[i].astype(jnp.float32) for i in (0, 1, 2, 3, 4, 5, 6, 11, 12, 13, 14)]
    gain_one, bias_one, share_key, share_value, share_gate, decay_all, first_all = vectors[:7]
    gain_two, bias_two, feed_share_key, feed_share_gate = vectors[7:]
    key_matrix, value_matrix, gate_matrix, output_matrix = (
        fetched[7],
        fetched[8],
        fetched[9],
        fetched[10],
    )
    feed_key_matrix, feed_value_matrix, feed_gate_matrix = (fetched[15], fetched[16], fetched[17])
    source = incoming_signal.astype(jnp.float32)
    normed, norm_pull = jax.vjp(norm_rows, source, gain_one, bias_one)
    edge = shifted(normed[-1:], "sp", 1)
    prior = jnp.concatenate([edge, normed[:-1]], axis=0) * same
    key_in = blend(normed, prior, share_key).astype(jnp.bfloat16)
    value_in = blend(normed, prior, share_value).astype(jnp.bfloat16)
    gate_in = blend(normed, prior, share_gate).astype(jnp.bfloat16)
    lookup_vectors = product(key_in, key_matrix).astype(jnp.bfloat16)
    content_vectors = product(value_in, value_matrix).astype(jnp.bfloat16)
    gate = jax.nn.sigmoid(product(gate_in, gate_matrix))
    arrived = lax.all_to_all(
        jnp.stack([lookup_vectors, content_vectors]), "sp", split_axis=2, concat_axis=1, tiled=True
    )
    decay_part = lax.dynamic_slice_in_dim(decay_all, place * channels, channels)
    first_part = lax.dynamic_slice_in_dim(first_all, place * channels, channels)

    def recurrence(key_full, value_full, decay_here, first_here):
        return weighted_attention_loop(
            key_full, value_full, decay_here, first_here, group_labels, LOOP_LENGTH
        )

    blended_signal, scan_pull = jax.vjp(
        recurrence,
        arrived[0].astype(jnp.float32),
        arrived[1].astype(jnp.float32),
        decay_part,
        first_part,
    )
    mixed_rows = lax.all_to_all(
        blended_signal.astype(jnp.bfloat16), "sp", split_axis=0, concat_axis=1, tiled=True
    ).astype(jnp.float32)
    gated = (gate * mixed_rows).astype(jnp.bfloat16)
    middle = source + product(gated, output_matrix)
    second, second_pull = jax.vjp(norm_rows, middle, gain_two, bias_two)
    second_edge = shifted(second[-1:], "sp", 1)
    prior_second = jnp.concatenate([second_edge, second[:-1]], axis=0) * same
    feed_key_in = blend(second, prior_second, feed_share_key).astype(jnp.bfloat16)
    feed_gate_in = blend(second, prior_second, feed_share_gate).astype(jnp.bfloat16)
    raised = product(feed_key_in, feed_key_matrix)
    hidden = jnp.square(jax.nn.relu(raised)).astype(jnp.bfloat16)
    recurrent_memory = product(hidden, feed_value_matrix)
    feed_sig = jax.nn.sigmoid(product(feed_gate_in, feed_gate_matrix))
    block_out = (live_rows * (middle + feed_sig * recurrent_memory)).astype(jnp.bfloat16)
    upstream = adjoint_signal.astype(jnp.float32) * live_rows
    carried_grad = (upstream * feed_sig).astype(jnp.bfloat16)
    feed_pre_grad = (upstream * recurrent_memory * feed_sig * (1.0 - feed_sig)).astype(jnp.bfloat16)
    grad_feed_value = outer_sum(hidden, carried_grad)
    grad_feed_gate = outer_sum(feed_gate_in, feed_pre_grad)
    raised_grad = (
        times_transposed(carried_grad, feed_value_matrix) * 2.0 * jax.nn.relu(raised)
    ).astype(jnp.bfloat16)
    grad_feed_key = outer_sum(feed_key_in, raised_grad)
    second_grad, second_prior_grad, feed_share_grads = blend_back(
        second,
        prior_second,
        (feed_share_key, feed_share_gate),
        (
            times_transposed(raised_grad, feed_key_matrix),
            times_transposed(feed_pre_grad, feed_gate_matrix),
        ),
    )
    moved = second_prior_grad * same
    incoming = shifted(moved[:1], "sp", -1)
    second_grad = second_grad + jnp.concatenate([moved[1:], incoming], axis=0)
    middle_norm_grad, grad_second_gain, grad_second_bias = second_pull(second_grad)
    middle_grad = upstream + middle_norm_grad
    attended_grad = middle_grad.astype(jnp.bfloat16)
    grad_output_weight = outer_sum(gated, attended_grad)
    gated_grad = times_transposed(attended_grad, output_matrix)
    mixed_grad = (gated_grad * gate).astype(jnp.bfloat16)
    gate_pre_grad = (gated_grad * mixed_rows * gate * (1.0 - gate)).astype(jnp.bfloat16)
    channel_grad = lax.all_to_all(mixed_grad, "sp", split_axis=1, concat_axis=0, tiled=True)
    key_grad_here, value_grad_here, decay_grad_here, first_grad_here = scan_pull(
        channel_grad.astype(jnp.float32)
    )
    returned = lax.all_to_all(
        jnp.stack([key_grad_here, value_grad_here]).astype(jnp.bfloat16),
        "sp",
        split_axis=1,
        concat_axis=2,
        tiled=True,
    )
    key_grad = returned[0]
    value_grad = returned[1]
    grad_key_weight = outer_sum(key_in, key_grad)
    grad_value_weight = outer_sum(value_in, value_grad)
    grad_gate_weight = outer_sum(gate_in, gate_pre_grad)
    normed_grad, normed_prior_grad, share_grads = blend_back(
        normed,
        prior,
        (share_key, share_value, share_gate),
        (
            times_transposed(key_grad, key_matrix),
            times_transposed(value_grad, value_matrix),
            times_transposed(gate_pre_grad, gate_matrix),
        ),
    )
    moved_first = normed_prior_grad * same
    incoming_first = shifted(moved_first[:1], "sp", -1)
    normed_grad = normed_grad + jnp.concatenate([moved_first[1:], incoming_first], axis=0)
    source_norm_grad, grad_norm_gain, grad_norm_bias = norm_pull(normed_grad)
    input_grad = middle_grad + source_norm_grad
    decay_grad = lax.dynamic_update_slice_in_dim(
        jnp.zeros((feature_dimension,), jnp.float32), decay_grad_here, place * channels, 0
    )
    first_grad = lax.dynamic_update_slice_in_dim(
        jnp.zeros((feature_dimension,), jnp.float32), first_grad_here, place * channels, 0
    )
    grads = (
        grad_norm_gain,
        grad_norm_bias,
        *share_grads,
        decay_grad,
        first_grad,
        grad_key_weight,
        grad_value_weight,
        grad_gate_weight,
        grad_output_weight,
        grad_second_gain,
        grad_second_bias,
        *feed_share_grads,
        grad_feed_key,
        grad_feed_value,
        grad_feed_gate,
    )
    shares = []
    for grad in grads:
        for axis in ("seq", "sp"):
            grad = lax.psum_scatter(
                grad.astype(jnp.bfloat16), axis, scatter_dimension=0, tiled=True
            ).astype(jnp.float32)
        shares.append(grad)
    return (block_out, input_grad, *shares)


MESH = pl.DeviceIdType.MESH
F32 = jnp.float32
BF16 = jnp.bfloat16
GAIN1, BIAS1, MIXK, MIXV, MIXG, DECAY, FIRST, GAIN2, BIAS2, FMIXK, FMIXG = range(11)


def multiple(value, step):
    return pl.multiple_of(value, step)


def nn(a, b):
    return jnp.dot(a, b, preferred_element_type=F32)


def nt(a, b):
    return lax.dot_general(a, b, (((1,), (1,)), ((), ())), preferred_element_type=F32)


def tn(a, b):
    return lax.dot_general(a, b, (((0,), (0,)), ((), ())), preferred_element_type=F32)


def exact_dot(links, right):
    high = right.astype(BF16)
    rest = right - high.astype(F32)
    middle = rest.astype(BF16)
    low = (rest - middle.astype(F32)).astype(BF16)
    return nn(links, high) + nn(links, middle) + nn(links, low)


def iota(shape, axis):
    return lax.broadcasted_iota(jnp.int32, shape, axis)


def spread_rows(v):
    centered = v - jnp.mean(v, axis=1, keepdims=True)
    scale = lax.rsqrt(jnp.mean(centered * centered, axis=1, keepdims=True) + EPSILON)
    return centered * scale, scale


def column_sum(v):
    return jnp.sum(v, axis=0, keepdims=True)


def scratch_list():
    vm = pltpu.VMEM
    sem = pltpu.SemaphoreType.DMA
    return dict(
        xall=vm((1024, 1024), BF16),
        kin=vm((1024, 1024), BF16),
        vin=vm((1024, 1024), BF16),
        gin=vm((1024, 1024), BF16),
        spread=vm((1024, 1024), BF16),
        wkvg=vm((1024, 768), BF16),
        wo=vm((256, 1024), BF16),
        wfg=vm((8, 128, 1024), BF16),
        wfk=vm((1024, 1024), BF16),
        wfv=vm((1024, 1024), BF16),
        kk=vm((1024, 256), BF16),
        vv=vm((1024, 256), BF16),
        gate=vm((1024, 256), F32),
        mixed=vm((1024, 256), F32),
        inverse=vm((1024, 256), F32),
        gated=vm((1024, 256), BF16),
        carry=vm((8, 8, 256), F32),
        tables=vm((4, 128, 256), F32),
        small=vm((8, 256), F32),
        last=vm((8, 1024), F32),
        xo=vm((256, 1024), BF16),
        adj=vm((256, 1024), BF16),
        mid=vm((256, 1024), F32),
        sec=vm((264, 1024), F32),
        sig=vm((256, 1024), F32),
        fgin=vm((256, 1024), BF16),
        fpg=vm((256, 1024), BF16),
        fkall=vm((1024, 1024), BF16),
        cgall=vm((1024, 1024), BF16),
        hidden=vm((1024, 1024), BF16),
        relu=vm((1024, 1024), BF16),
        rgrad=vm((1024, 1024), BF16),
        acca=vm((256, 1024), F32),
        accb=vm((256, 1024), F32),
        fgg=vm((256, 1024), F32),
        moved=vm((264, 1024), F32),
        csa=vm((2, 256, 1024), BF16),
        cra=vm((2, 256, 1024), BF16),
        ysa=vm((256, 1024), BF16),
        yra=vm((256, 1024), BF16),
        csb=vm((2, 256, 1024), BF16),
        crb=vm((2, 256, 1024), BF16),
        ysb=vm((256, 1024), BF16),
        yrb=vm((256, 1024), BF16),
        fgcr=vm((2, 8, 32, 1024), BF16),
        fgyr=vm((8, 32, 1024), BF16),
        xrfv=vm((4, 128, 1024), BF16),
        xrfk=vm((4, 128, 1024), BF16),
        xrfg=vm((4, 32, 1024), BF16),
        xro=vm((4, 32, 1024), BF16),
        xrkvg=vm((4, 128, 768), BF16),
        zrfv=vm((3, 128, 1024), BF16),
        zrfk=vm((3, 128, 1024), BF16),
        zrfg=vm((3, 32, 1024), BF16),
        zro=vm((3, 32, 1024), BF16),
        zrkvg=vm((3, 128, 768), BF16),
        kvgraw=vm((3, 32, 1024), BF16),
        fkraw=vm((32, 4096), BF16),
        kvgpart=vm((4, 32, 768), BF16),
        fkpart=vm((4, 32, 1024), BF16),
        o_out=vm((32, 1024), F32),
        fg_out=vm((32, 1024), F32),
        fk_out=vm((32, 4096), F32),
        fv_out=vm((128, 1024), F32),
        b_out=vm((256, 1024), BF16),
        x_out=vm((256, 1024), F32),
        v_out=vm((16, 128), F32),
        recfk=vm((4, 32, 1024), BF16),
        reckvg=vm((4, 32, 768), BF16),
        vraw=vm((8, 4, 16, 128), BF16),
        nat=vm((16, 1024), F32),
        chan=vm((16, 256), F32),
        vg=vm((16, 1024), F32),
        vgc=vm((16, 256), F32),
        vmsg=vm((8, 16, 128), F32),
        vrec=vm((8, 16, 128), F32),
        vtwo=vm((16, 128), F32),
        vrec2=vm((4, 16, 128), F32),
        ags=sem((6, 7)),
        agr=sem((6, 8)),
        a2s=sem((3, 3)),
        a2r=sem((3, 4)),
        sps=sem((5, 3)),
        spr=sem((5, 3)),
        rss=sem((5, 3)),
        rsr=sem((5, 3)),
        qxs=sem((5, 4)),
        qxr=sem((5, 4)),
        qzs=sem((5, 3)),
        qzr=sem((5, 3)),
        fas=sem((2, 3)),
        far=sem((2, 4)),
        vss=sem((2, 7)),
        vsr=sem((2, 8)),
        eds=sem((2,)),
        edr=sem((2,)),
        loc=sem((24,)),
    )


def step_kernel(
    lengths, xin, adjoint, vecs, k_in, v_in, g_in, o_in, fg_in, fk_in, fv_in,
    out, xgrad, g_o, g_fg, g_fk, g_fv, g_kvg, g_vec,
    *scratch,
):
    t = types.SimpleNamespace(**dict(zip(scratch_list(), scratch)))
    s, p = lax.axis_index("seq"), lax.axis_index("sp")
    z, x, y, c = s // 2, s % 2, p // 2, p % 2
    zs = [(z + k) % 4 for k in range(4)]
    xdev = (z * 2 + 1 - x, p)
    ydev, sib = (s, (1 - y) * 2 + c), (s, y * 2 + 1 - c)
    sps = [(p + k) % 4 for k in range(4)]
    sqs = [(s + k) % 8 for k in range(8)]
    p_sib, p_y, p_diag = y * 2 + 1 - c, (1 - y) * 2 + c, (1 - y) * 2 + 1 - c

    pending = []

    def remote(src, dst, send_sem, recv_sem, device):
        return pltpu.make_async_remote_copy(
            src_ref=src, dst_ref=dst, send_sem=send_sem, recv_sem=recv_sem,
            device_id=device, device_id_type=MESH,
        )

    def send(src, dst, send_sem, recv_sem, device, tag=None):
        copy = remote(src, dst, send_sem, recv_sem, device)
        copy.start()
        pending.append((tag, copy))
        return copy

    def settle(*tags):
        for tag, copy in pending:
            if tag in tags:
                copy.wait_send()
        pending[:] = [(tag, copy) for tag, copy in pending if tag not in tags]

    def arrive(dst, recv_sem):
        remote(dst, dst, recv_sem, recv_sem, sib).wait_recv()

    def local(src, dst, k):
        copy = pltpu.make_async_copy(src, dst, t.loc.at[k])
        copy.start()
        return copy

    loads = []

    def load(src, dst):
        copy = pltpu.make_async_copy(src, dst, t.loc.at[len(loads)])
        copy.start()
        loads.append(copy)

    def own_rows(ref, size):
        return ref.at[pl.ds(multiple(s * size, size), size)]

    load(k_in, t.kvgraw.at[0])
    load(v_in, t.kvgraw.at[1])
    load(g_in, t.kvgraw.at[2])
    load(vecs, t.vraw.at[s, p])
    load(fk_in, t.fkraw)
    early = len(loads)
    load(xin, t.xall.at[pl.ds(multiple(p * 256, 256), 256)])
    load(o_in, own_rows(t.wo, 32))
    load(fg_in, t.wfg.at[s, pl.ds(multiple(p * 32, 32), 32)])
    load(fv_in, own_rows(t.wfv, 128))
    load(xin, t.xo)
    load(adjoint, t.adj)
    for copy in loads[:4]:
        copy.wait()
    piece = iota((32, 128), 1) // 32
    for w in range(3):
        for h in range(2):
            tiles = [t.kvgraw[w, :, 512 * h + 128 * j : 512 * h + 128 * j + 128].astype(F32) for j in range(4)]
            for q in range(4):
                total = jnp.zeros((32, 128), F32)
                for j in range(4):
                    turn = 32 * (j - q) % 128
                    total = jnp.where(piece == j, pltpu.roll(tiles[j], turn, 1) if turn else tiles[j], total)
                t.kvgpart[q, :, 256 * w + 128 * h : 256 * w + 128 * h + 128] = total.astype(BF16)
    loads[4].wait()
    for i in range(8):
        for q in range(4):
            t.fkpart[q, :, 128 * i : 128 * i + 128] = t.fkraw[:, 512 * i + 128 * q : 512 * i + 128 * q + 128]

    barrier = pltpu.get_barrier_semaphore()
    for k in range(1, 8):
        pl.semaphore_signal(barrier, inc=1, device_id=(sqs[k], p), device_id_type=MESH)
    for k in range(1, 4):
        pl.semaphore_signal(barrier, inc=1, device_id=(s, sps[k]), device_id_type=MESH)
    pl.semaphore_wait(barrier, 10)

    def rows(ref, size):
        return lambda i: ref.at[pl.ds(multiple(i * size, size), size)]

    V, A, B, C, D, E = range(6)
    block = {
        V: lambda i: t.vraw.at[i],
        A: rows(t.wkvg, 128),
        B: rows(t.wo, 32),
        C: lambda i: t.wfg.at[i, pl.ds(multiple(p * 32, 32), 32)],
        D: rows(t.wfk, 128),
        E: rows(t.wfv, 128),
    }

    def own_out(item, src):
        there = block[item](s)
        send(src, there, t.ags.at[item, 3], t.agr.at[item, s], xdev, item)
        for k in (1, 2, 3):
            send(src, there, t.ags.at[item, k - 1], t.agr.at[item, s], (zs[k] * 2 + x, p), item)

    def pass_on(item, k):
        i = zs[k] * 2 + x
        arrive(block[item](i), t.agr.at[item, i])
        send(block[item](i), block[item](i), t.ags.at[item, 3 + k], t.agr.at[item, i], xdev, item)

    def all_in(item):
        for k in range(4):
            i = zs[k] * 2 + 1 - x
            arrive(block[item](i), t.agr.at[item, i])

    def sp_out(n, view):
        send(view(p), view(p), t.sps.at[n, 0], t.spr.at[n, 0], ydev, ("sp", n))
        send(view(p), view(p), t.sps.at[n, 1], t.spr.at[n, 1], sib, ("sp", n))

    def sp_pass(n, view):
        arrive(view(p_y), t.spr.at[n, 0])
        send(view(p_y), view(p_y), t.sps.at[n, 2], t.spr.at[n, 2], sib, ("sp", n))

    def sp_sib(n, view):
        arrive(view(p_sib), t.spr.at[n, 1])

    def sp_diag(n, view):
        arrive(view(p_diag), t.spr.at[n, 2])

    def add_rows(n, fn):
        @pl.loop(0, n // 32)
        def _(i):
            fn(pl.ds(multiple(i * 32, 32), 32))

    def sum_begin(n, cs, cr, ys, yr, acc, compute):
        for j, q in enumerate((p_diag, p_sib)):
            cs[j] = compute(q).astype(BF16)
            send(cs.at[j], cr.at[j], t.rss.at[n, j], t.rsr.at[n, j], sib, ("sum", n))
        acc[...] = compute(p_y)
        arrive(cr.at[0], t.rsr.at[n, 0])

        def to_other(r):
            ys[r, :] = (acc[r, :] + cr[0, r, :].astype(F32)).astype(BF16)

        add_rows(256, to_other)
        send(ys, yr, t.rss.at[n, 2], t.rsr.at[n, 2], ydev, ("sum", n))
        acc[...] = compute(p)
        arrive(cr.at[1], t.rsr.at[n, 1])

        def to_own(r):
            acc[r, :] += cr[1, r, :].astype(F32)

        add_rows(256, to_own)

    def sum_end(n, yr, acc):
        arrive(yr, t.rsr.at[n, 2])

        def add(r):
            acc[r, :] += yr[r, :].astype(F32)

        add_rows(256, add)
        settle(("sum", n))

    FV, FK, FG, O, KVG = range(5)
    grads = {
        FV: (t.wfv, t.xrfv, t.zrfv, 128),
        FK: (t.wfk, t.xrfk, t.zrfk, 128),
        FG: (t.fgin, t.xrfg, t.zrfg, 32),
        O: (t.wo, t.xro, t.zro, 32),
        KVG: (t.wkvg, t.xrkvg, t.zrkvg, 128),
    }

    def grad_x_out(item, zz):
        ref, xr, _, size = grads[item]
        send(rows(ref, size)(zz * 2 + 1 - x), xr.at[zz], t.qxs.at[item, zz], t.qxr.at[item, zz], xdev)

    def grad_x_in(item, k):
        ref, xr, zr, size = grads[item]
        zz = zs[k]
        arrive(xr.at[zz], t.qxr.at[item, zz])
        if k == 0:
            return
        base = (zz * 2 + x) * size

        def add(r):
            here = pl.ds(multiple(base + r.start, 32), 32)
            ref[here, :] = (ref[here, :].astype(F32) + xr[zz, r, :].astype(F32)).astype(BF16)

        add_rows(size, add)
        send(rows(ref, size)(zz * 2 + x), zr.at[k - 1], t.qzs.at[item, k - 1], t.qzr.at[item, k - 1], (zz * 2 + x, p))

    def grad_z_in(item, put):
        ref, xr, zr, size = grads[item]
        for k in range(1, 4):
            arrive(zr.at[k - 1], t.qzr.at[item, k - 1])

        @pl.loop(0, size // 32)
        def _(i):
            r = pl.ds(multiple(i * 32, 32), 32)
            here = pl.ds(multiple(s * size + i * 32, 32), 32)
            total = ref[here, :].astype(F32) + xr[z, r, :].astype(F32)
            total = total + zr[0, r, :].astype(F32) + zr[1, r, :].astype(F32) + zr[2, r, :].astype(F32)
            put(i, r, total)

    def hand_back(n, fin, rec):
        for k in range(1, 4):
            send(fin.at[sps[k]], rec.at[p], t.fas.at[n, k - 1], t.far.at[n, p], (s, sps[k]))
        rec[p] = fin[p]

    def handed_back(n, rec):
        for k in range(1, 4):
            arrive(rec.at[sps[k]], t.far.at[n, sps[k]])

    e0 = lengths[0, 0]
    e1 = e0 + lengths[0, 1]
    e2 = e1 + lengths[0, 2]
    e3 = e2 + lengths[0, 3]

    def label(pos):
        total = (pos >= 0).astype(jnp.int32)
        for edge in (e0, e1, e2, e3):
            total = total + (pos >= edge).astype(jnp.int32)
        return total - 1

    def same_at(pos):
        return (label(pos) == label(pos - 1)).astype(F32)

    xview = rows(t.xall, 256)

    def a2a_out(n, src, dst):
        for k in (2, 1, 3):
            send(src(sps[k]), dst(p), t.a2s.at[n, k - 1], t.a2r.at[n, p], (s, sps[k]), ("a2a", n))

    def a2a_in(n, dst):
        for k in range(1, 4):
            arrive(dst(sps[k]), t.a2r.at[n, sps[k]])

    vec_dst = lambda i: t.vraw.at[s, i]
    kvg_dst = lambda i: t.wkvg.at[pl.ds(multiple(s * 128 + i * 32, 32), 32)]
    fk_dst = lambda i: t.wfk.at[pl.ds(multiple(s * 128 + i * 32, 32), 32)]
    a2a_out(0, lambda i: vecs, vec_dst)
    a2a_out(1, lambda i: t.kvgpart.at[i], kvg_dst)
    a2a_out(2, lambda i: t.fkpart.at[i], fk_dst)
    send(xin, xview(p), t.sps.at[0, 0], t.spr.at[0, 0], ydev)
    send(xin, xview(p), t.sps.at[0, 1], t.spr.at[0, 1], sib)
    t.wkvg[pl.ds(multiple(s * 128 + p * 32, 32), 32), :] = t.kvgpart[p]
    t.wfk[pl.ds(multiple(s * 128 + p * 32, 32), 32), :] = t.fkpart[p]
    a2a_in(0, vec_dst)
    own_out(V, t.vraw.at[s])
    a2a_in(1, kvg_dst)
    own_out(A, block[A](s))
    for copy in loads[early:]:
        copy.wait()
    for k in (3, 2, 1):
        pass_on(V, k)
    own_out(B, o_in)
    own_out(C, fg_in)
    a2a_in(2, fk_dst)
    own_out(D, block[D](s))
    own_out(E, fv_in)
    all_in(V)

    t.last[...] = jnp.zeros_like(t.last)
    t.vg[...] = jnp.zeros_like(t.vg)
    t.vgc[...] = jnp.zeros_like(t.vgc)
    for i in range(8):
        total = t.vraw[i, 0].astype(F32)
        for j in range(1, 4):
            total = total + pltpu.roll(t.vraw[i, j].astype(F32), 32 * j, 1)
        t.nat[:, 128 * i : 128 * i + 128] = total
    for i in range(2):
        total = t.vraw[4 * i, p].astype(F32)
        for j in range(1, 4):
            total = total + pltpu.roll(t.vraw[4 * i + j, p].astype(F32), 32 * j, 1)
        t.chan[:, 128 * i : 128 * i + 128] = total

    def vector(k):
        return t.nat[k : k + 1, :]

    rate = jnp.exp(t.chan[DECAY : DECAY + 1, :])
    offset = iota((128, 1), 0).astype(F32)
    t.tables[0] = jnp.exp(offset * rate)
    t.tables[1] = jnp.exp(-(offset - 1.0) * rate)
    t.tables[2] = jnp.exp(-offset * rate)
    t.tables[3] = jnp.exp(-(127.0 - offset) * rate)
    t.small[0:1, :] = jnp.exp(-128.0 * rate)
    t.small[1:2, :] = jnp.exp(t.chan[FIRST : FIRST + 1, :])
    t.small[2:3, :] = rate

    sp_pass(0, xview)
    sp_sib(0, xview)
    sp_diag(0, xview)

    def norm_quarter(q):
        @pl.loop(0, 8)
        def _(i):
            base = q * 256 + i * 32
            r = pl.ds(multiple(base, 32), 32)
            hat, _ = spread_rows(t.xall[r, :].astype(F32))
            normed = hat * vector(GAIN1) + vector(BIAS1)
            row = iota((32, 1), 0)
            prior = jnp.where(row == 0, t.last[0:1, :], pltpu.roll(normed, 1, 0))
            prior = prior * same_at(base + row)
            t.last[0:1, :] = normed[31:32, :]
            diff = normed - prior
            t.spread[r, :] = diff.astype(BF16)
            t.kin[r, :] = (prior + diff * vector(MIXK)).astype(BF16)
            t.vin[r, :] = (prior + diff * vector(MIXV)).astype(BF16)
            t.gin[r, :] = (prior + diff * vector(MIXG)).astype(BF16)

    pass_on(A, 3)
    norm_quarter(0)
    pass_on(A, 2)
    norm_quarter(1)
    pass_on(A, 1)
    norm_quarter(2)
    pass_on(B, 3)
    norm_quarter(3)
    pass_on(B, 2)
    pass_on(B, 1)
    all_in(A)
    settle(("sp", 0))

    @pl.loop(0, 4)
    def _(i):
        r = pl.ds(multiple(i * 256, 256), 256)
        t.kk[r, :] = nn(t.kin[r, :], t.wkvg[:, 0:256]).astype(BF16)
        t.vv[r, :] = nn(t.vin[r, :], t.wkvg[:, 256:512]).astype(BF16)
        t.gate[r, :] = jax.nn.sigmoid(nn(t.gin[r, :], t.wkvg[:, 512:768]))

    pass_on(C, 3)

    def block_parts(b):
        base = b * 128
        column = label(base + iota((128, 1), 0))
        row = label(base + iota((1, 128), 1))
        before, end = label(base - 1), label(base + 127)
        alike = column == row
        keep = (before == end).astype(F32) * t.small[0:1, :]
        memory = (column == before).astype(F32) * t.tables[2]
        tail = (column == end).astype(F32) * t.tables[3]
        return alike, keep, memory, tail

    def forward_block(b, held):
        top, bottom = held
        r = pl.ds(multiple(b * 128, 128), 128)
        alike, keep, memory, tail = block_parts(b)
        links = (alike & (iota((128, 128), 1) < iota((128, 128), 0))).astype(F32).astype(BF16)
        v = t.vv[r, :].astype(F32)
        weight = jnp.exp(t.kk[r, :].astype(F32))
        scaled = t.tables[0] * weight
        sums = exact_dot(links, jnp.concatenate([scaled * v, scaled], axis=1))
        own = t.small[1:2, :] * weight
        high = t.tables[1] * sums[:, :256] + memory * top + own * v
        low = t.tables[1] * sums[:, 256:] + memory * bottom + own
        inverse = 1.0 / low
        mixed = high * inverse
        t.inverse[r, :] = inverse
        t.mixed[r, :] = mixed
        t.gated[r, :] = (t.gate[r, :] * mixed.astype(BF16).astype(F32)).astype(BF16)
        t.carry[b, 0:1, :] = top
        t.carry[b, 1:2, :] = bottom
        tail = tail * weight
        return keep * top + column_sum(tail * v), keep * bottom + column_sum(tail)

    zero = jnp.zeros((1, 256), F32)
    held = lax.fori_loop(0, 4, forward_block, (zero, zero))
    pass_on(C, 2)
    held = lax.fori_loop(4, 8, forward_block, held)
    pass_on(C, 1)

    all_in(B)

    def quarter(ref, q):
        return ref[pl.ds(multiple(q * 256, 256), 256), :]

    sum_begin(0, t.csa, t.cra, t.ysa, t.yra, t.acca, lambda q: nn(quarter(t.gated, q), t.wo[...]))
    pass_on(D, 3)
    all_in(C)
    fgview = lambda i: t.wfg.at[:, pl.ds(multiple(i * 32, 32), 32)]
    sp_out(1, fgview)
    pass_on(D, 2)
    sum_end(0, t.yra, t.acca)

    def second_tile(i):
        r = pl.ds(multiple(i * 32, 32), 32)
        middle = t.xo[r, :].astype(F32) + t.acca[r, :]
        t.mid[r, :] = middle
        hat, _ = spread_rows(middle)
        t.sec[pl.ds(multiple(8 + i * 32, 8), 32), :] = hat * vector(GAIN2) + vector(BIAS2)

    second_tile(7)
    up_edge = remote(t.sec.at[pl.ds(256, 8)], t.sec.at[pl.ds(0, 8)], t.eds.at[0], t.edr.at[0], (s, sps[1]))

    @pl.when(p < 3)
    def _():
        up_edge.start()

    @pl.when(p == 0)
    def _():
        t.sec[0:8, :] = jnp.zeros((8, 1024), F32)

    @pl.loop(0, 7)
    def _(i):
        second_tile(i)

    @pl.when(p > 0)
    def _():
        remote(t.sec.at[pl.ds(0, 8)], t.sec.at[pl.ds(0, 8)], t.eds.at[0], t.edr.at[0], sib).wait_recv()

    @pl.when(p < 3)
    def _():
        up_edge.wait_send()

    def second_pair(i):
        wide = t.sec[pl.ds(multiple(i * 32, 32), 40), :]
        pos = p * 256 + i * 32 + iota((32, 1), 0)
        return wide[8:40], pltpu.roll(wide, 33, 0)[0:32] * same_at(pos)

    @pl.loop(0, 8)
    def _(i):
        second, prior = second_pair(i)
        diff = second - prior
        t.fkall[pl.ds(multiple(p * 256 + i * 32, 32), 32), :] = (prior + diff * vector(FMIXK)).astype(BF16)
        t.fgin[pl.ds(multiple(i * 32, 32), 32), :] = (prior + diff * vector(FMIXG)).astype(BF16)

    fkview = rows(t.fkall, 256)
    cgview = rows(t.cgall, 256)
    sp_out(2, fkview)
    sp_pass(1, fgview)
    sp_sib(1, fgview)
    pass_on(D, 1)
    sp_diag(1, fgview)

    def feed_gate_weight():
        return t.wfg[...].reshape(1024, 1024)

    t.sig[...] = jax.nn.sigmoid(nn(t.fgin[...], feed_gate_weight()))

    def upstream(i):
        pos = p * 256 + i * 32 + iota((32, 1), 0)
        return t.adj[pl.ds(multiple(i * 32, 32), 32), :].astype(F32) * (pos < e3).astype(F32)

    @pl.loop(0, 8)
    def _(i):
        r = pl.ds(multiple(i * 32, 32), 32)
        t.cgall[pl.ds(multiple(p * 256 + i * 32, 32), 32), :] = (upstream(i) * t.sig[r, :]).astype(BF16)

    sp_out(3, cgview)
    pass_on(E, 3)
    sp_sib(2, fkview)
    sp_pass(2, fkview)
    pass_on(E, 2)
    all_in(D)

    def raise_rows(q):
        r = pl.ds(multiple(q * 256, 256), 256)
        relu = jnp.maximum(nn(t.fkall[r, :], t.wfk[...]), 0.0)
        t.relu[r, :] = relu.astype(BF16)
        t.hidden[r, :] = (relu * relu).astype(BF16)

    raise_rows(p)
    raise_rows(p_sib)
    raise_rows(p_y)
    pass_on(E, 1)
    sp_diag(2, fkview)
    raise_rows(p_diag)
    sp_pass(3, cgview)
    all_in(E)
    sum_begin(1, t.csb, t.crb, t.ysb, t.yrb, t.accb, lambda q: nn(quarter(t.hidden, q), t.wfv[...]))

    def lower_rows(q):
        r = pl.ds(multiple(q * 256, 256), 256)
        t.rgrad[r, :] = (nt(t.cgall[r, :], t.wfv[...]) * 2.0 * t.relu[r, :].astype(F32)).astype(BF16)

    sp_sib(3, cgview)
    sp_diag(3, cgview)
    for q in (p_diag, p_sib, p_y, p):
        lower_rows(q)
    sum_begin(2, t.csa, t.cra, t.ysa, t.yra, t.acca, lambda q: nt(quarter(t.rgrad, q), t.wfk[...]))

    settle(D, E)
    for k in (1, 2, 3, 0):
        q = pl.ds(multiple(zs[k] * 256, 256), 256)
        t.wfv[q, :] = tn(t.hidden[:, q], t.cgall[...]).astype(BF16)
        grad_x_out(FV, zs[k])
    for k in (1, 2, 3, 0):
        q = pl.ds(multiple(zs[k] * 256, 256), 256)
        t.wfk[q, :] = tn(t.fkall[:, q], t.rgrad[...]).astype(BF16)
        grad_x_out(FK, zs[k])
    grad_x_in(FV, 1)

    sum_end(1, t.yrb, t.accb)

    @pl.loop(0, 8)
    def _(i):
        r = pl.ds(multiple(i * 32, 32), 32)
        pos = p * 256 + i * 32 + iota((32, 1), 0)
        live = (pos < e3).astype(F32)
        sig, total, up = t.sig[r, :], t.accb[r, :], upstream(i)
        t.b_out[r, :] = (live * (t.mid[r, :] + sig * total)).astype(BF16)
        t.fpg[r, :] = (up * total * sig * (1.0 - sig)).astype(BF16)

    t.fgg[...] = nt(t.fpg[...], feed_gate_weight())
    settle(C, ("sp", 1))
    for k in range(4):
        part = tn(t.fgin[:, 256 * k : 256 * k + 256], t.fpg[...]).astype(BF16)
        t.wfg[2 * k : 2 * k + 2] = part.reshape(2, 128, 1024)
    for j, q in enumerate((p_diag, p_sib)):
        send(fgview(q), t.fgcr.at[j], t.rss.at[4, j], t.rsr.at[4, j], sib)
    results = []

    def result(src, dst):
        copy = pltpu.make_async_copy(src, dst, t.loc.at[12 + len(results)])
        copy.start()
        results.append(copy)

    result(t.b_out, out)
    grad_x_in(FV, 2)
    sum_end(2, t.yra, t.acca)

    @pl.loop(0, 8)
    def _(i):
        r = pl.ds(multiple(i * 32, 32), 32)
        pos = p * 256 + i * 32 + iota((32, 1), 0)
        through = t.acca[r, :] * (1.0 - vector(FMIXK)) + t.fgg[r, :] * (1.0 - vector(FMIXG))
        t.moved[r, :] = through * same_at(pos)

    down_edge = remote(t.moved.at[pl.ds(0, 8)], t.moved.at[pl.ds(256, 8)], t.eds.at[1], t.edr.at[1], (s, sps[3]))

    @pl.when(p > 0)
    def _():
        down_edge.start()

    @pl.when(p == 3)
    def _():
        t.moved[256:264, :] = jnp.zeros((8, 1024), F32)

    @pl.when(p < 3)
    def _():
        remote(t.moved.at[pl.ds(256, 8)], t.moved.at[pl.ds(256, 8)], t.eds.at[1], t.edr.at[1], sib).wait_recv()

    @pl.when(p > 0)
    def _():
        down_edge.wait_send()

    grad_x_in(FV, 3)

    def norm_back(hat, scale, grad, gain):
        grad = grad * gain
        return scale * (
            grad - jnp.mean(grad, axis=1, keepdims=True) - hat * jnp.mean(grad * hat, axis=1, keepdims=True)
        )

    def add_vector(k, v):
        t.vg[k : k + 1, :] += column_sum(v)

    @pl.loop(0, 8)
    def _(i):
        r = pl.ds(multiple(i * 32, 32), 32)
        after = pltpu.roll(t.moved[pl.ds(multiple(i * 32, 32), 40), :], 39, 0)[0:32]
        by_key, by_gate = t.acca[r, :], t.fgg[r, :]
        grad = by_key * vector(FMIXK) + by_gate * vector(FMIXG) + after
        second, prior = second_pair(i)
        diff = second - prior
        hat, scale = spread_rows(t.mid[r, :])
        add_vector(FMIXK, diff * by_key)
        add_vector(FMIXG, diff * by_gate)
        add_vector(GAIN2, grad * hat)
        add_vector(BIAS2, grad)
        total = upstream(i) + norm_back(hat, scale, grad, vector(GAIN2))
        t.mid[r, :] = total
        t.xall[pl.ds(multiple(p * 256 + i * 32, 32), 32), :] = total.astype(BF16)

    agview = xview
    sp_out(4, agview)

    arrive(t.fgcr.at[0], t.rsr.at[4, 0])
    there = pl.ds(multiple(p_y * 32, 32), 32)

    @pl.loop(0, 8)
    def _(i):
        t.wfg[i, there, :] = (t.wfg[i, there, :].astype(F32) + t.fgcr[0, i].astype(F32)).astype(BF16)

    send(fgview(p_y), t.fgyr, t.rss.at[4, 2], t.rsr.at[4, 2], ydev)
    grad_x_in(FV, 0)
    grad_x_in(FK, 1)
    sp_pass(4, agview)
    sp_sib(4, agview)
    sp_diag(4, agview)

    @pl.loop(0, 4)
    def _(i):
        r = pl.ds(multiple(i * 256, 256), 256)
        grad = nt(t.xall[r, :], t.wo[...])
        gate = t.gate[r, :]
        t.hidden[r, 0:256] = (grad * gate).astype(BF16)
        t.hidden[r, 256:512] = (grad * t.mixed[r, :].astype(BF16).astype(F32) * gate * (1.0 - gate)).astype(BF16)

    settle(B)
    t.wo[...] = tn(t.gated[...], t.xall[...]).astype(BF16)
    for k in (1, 2, 3, 0):
        grad_x_out(O, zs[k])
    grad_x_in(FK, 2)

    def backward_block(k, held):
        b = 7 - k
        d_top, d_bottom, d_first, d_rate = held
        r = pl.ds(multiple(b * 128, 128), 128)
        alike, keep, memory, tail = block_parts(b)
        later = (alike & (iota((128, 128), 1) > iota((128, 128), 0))).astype(F32).astype(BF16)
        top, bottom = t.carry[b, 0:1, :], t.carry[b, 1:2, :]
        v = t.vv[r, :].astype(F32)
        weight = jnp.exp(t.kk[r, :].astype(F32))
        d_high = t.hidden[r, 0:256].astype(F32) * t.inverse[r, :]
        d_low = -d_high * t.mixed[r, :]
        shrink = t.tables[1]
        sums = exact_dot(later, jnp.concatenate([shrink * d_high, shrink * d_low], axis=1))
        scaled = t.tables[0] * weight
        own = t.small[1:2, :] * weight
        tail = tail * weight
        by_sum = scaled * (v * sums[:, :256] + sums[:, 256:])
        by_own = own * (v * d_high + d_low)
        by_tail = tail * (v * d_top + d_bottom)
        by_memory = memory * (top * d_high + bottom * d_low)
        t.vv[r, :] = (scaled * sums[:, :256] + own * d_high + tail * d_top).astype(BF16)
        t.kk[r, :] = (by_sum + by_own + by_tail).astype(BF16)
        place = iota((128, 1), 0).astype(F32)
        d_rate = d_rate + column_sum(
            place * by_sum + (place - 1.0) * by_own - by_memory - (127.0 - place) * by_tail
        )
        d_rate = d_rate - 128.0 * keep * (top * d_top + bottom * d_bottom)
        d_first = d_first + column_sum(by_own)
        d_top = keep * d_top + column_sum(memory * d_high)
        d_bottom = keep * d_bottom + column_sum(memory * d_low)
        return d_top, d_bottom, d_first, d_rate

    held = lax.fori_loop(0, 4, backward_block, (zero, zero, zero, zero))
    held = lax.fori_loop(4, 8, backward_block, held)
    t.vgc[DECAY : DECAY + 1, :] = held[3] * t.small[2:3, :]
    t.vgc[FIRST : FIRST + 1, :] = held[2]

    t.last[...] = jnp.zeros_like(t.last)

    @pl.loop(0, 8)
    def _(k):
        i = 7 - k
        r = pl.ds(multiple(i * 128, 128), 128)
        t.acca[0:128, :] = nt(t.kk[r, :], t.wkvg[:, 0:256])
        t.acca[128:256, :] = nt(t.vv[r, :], t.wkvg[:, 256:512])
        t.fgg[0:128, :] = nt(t.hidden[r, 256:512], t.wkvg[:, 512:768])

        @pl.loop(0, 4)
        def _(kk):
            j = 3 - kk
            u = multiple(j * 32, 32)
            base = i * 128 + j * 32
            here = pl.ds(multiple(base, 32), 32)
            by_key, by_value, by_gate = t.acca[pl.ds(u, 32), :], t.acca[pl.ds(128 + u, 32), :], t.fgg[pl.ds(u, 32), :]
            diff = t.spread[here, :].astype(F32)
            add_vector(MIXK, diff * by_key)
            add_vector(MIXV, diff * by_value)
            add_vector(MIXG, diff * by_gate)
            current = by_key * vector(MIXK) + by_value * vector(MIXV) + by_gate * vector(MIXG)
            row = iota((32, 1), 0)
            through = (by_key + by_value + by_gate - current) * same_at(base + row)
            after = jnp.where(row == 31, t.last[0:1, :], pltpu.roll(through, 31, 0))
            t.last[0:1, :] = through[0:1, :]
            t.relu[here, :] = (current + after).astype(BF16)

    sum_begin(3, t.csb, t.crb, t.ysb, t.yrb, t.accb, lambda q: quarter(t.relu, q).astype(F32))

    arrive(t.fgcr.at[1], t.rsr.at[4, 1])
    arrive(t.fgyr, t.rsr.at[4, 2])
    mine = pl.ds(multiple(p * 32, 32), 32)

    @pl.loop(0, 8)
    def _(i):
        total = t.wfg[i, mine, :].astype(F32) + t.fgcr[1, i].astype(F32) + t.fgyr[i].astype(F32)
        t.fgin[pl.ds(multiple(i * 32, 32), 32), :] = total.astype(BF16)

    for k in (1, 2, 3, 0):
        grad_x_out(FG, zs[k])
    grad_x_in(FK, 3)

    settle(A)
    for k in (1, 2, 3, 0):
        q = pl.ds(multiple(zs[k] * 256, 256), 256)
        t.wkvg[q, 0:256] = tn(t.kin[:, q], t.kk[...]).astype(BF16)
        t.wkvg[q, 256:512] = tn(t.vin[:, q], t.vv[...]).astype(BF16)
        t.wkvg[q, 512:768] = tn(t.gin[:, q], t.hidden[:, 256:512]).astype(BF16)
        grad_x_out(KVG, zs[k])

    def put_fv(i, r, v):
        t.fv_out[r, :] = v

    def put_fk(i, r, v):
        t.fkpart[i] = v.astype(BF16)

    def put_kvg(i, r, v):
        t.kvgpart[i] = v.astype(BF16)

    def put_o(i, r, v):
        t.o_out[r, :] = v

    def put_fg(i, r, v):
        t.fg_out[r, :] = v

    settle(("a2a", 1), ("a2a", 2))
    grad_z_in(FV, put_fv)
    result(t.fv_out, g_fv)
    grad_x_in(FK, 0)
    for k in (1, 2, 3, 0):
        grad_x_in(O, k)

    sum_end(3, t.yrb, t.accb)

    @pl.loop(0, 8)
    def _(i):
        r = pl.ds(multiple(i * 32, 32), 32)
        hat, scale = spread_rows(t.xo[r, :].astype(F32))
        grad = t.accb[r, :]
        add_vector(GAIN1, grad * hat)
        add_vector(BIAS1, grad)
        t.x_out[r, :] = t.mid[r, :] + norm_back(hat, scale, grad, vector(GAIN1))

    lane = iota((16, 128), 1)
    mine_lanes = (lane >= 32 * p) & (lane < 32 * p + 32)
    for i in range(8):
        tile = t.vgc[:, 128 * (i // 4) : 128 * (i // 4) + 128]
        moved = pltpu.roll(tile, (32 * p + 128 - 32 * (i % 4)) % 128, 1)
        t.vmsg[i] = t.vg[:, 128 * i : 128 * i + 128] + jnp.where(mine_lanes, moved, 0.0)
    for k in range(1, 8):
        send(t.vmsg.at[sqs[k]], t.vrec.at[k], t.vss.at[0, k - 1], t.vsr.at[0, k], (sqs[k], p))
    result(t.x_out, xgrad)
    for k in (1, 2, 3, 0):
        grad_x_in(FG, k)
    grad_x_in(KVG, 1)
    grad_z_in(FK, put_fk)
    hand_back(0, t.fkpart, t.recfk)
    grad_x_in(KVG, 2)
    grad_z_in(O, put_o)
    result(t.o_out, g_o)
    total = t.vmsg[s]
    for k in range(1, 8):
        arrive(t.vrec.at[k], t.vsr.at[0, k])
        total = total + t.vrec[k]
    t.vtwo[...] = total
    for k in range(1, 4):
        send(t.vtwo, t.vrec2.at[k], t.vss.at[1, k - 1], t.vsr.at[1, k], (s, sps[k]))
    grad_x_in(KVG, 3)
    grad_z_in(FG, put_fg)
    result(t.fg_out, g_fg)
    handed_back(0, t.recfk)
    for i in range(8):
        for j in range(4):
            t.fk_out[:, 512 * i + 128 * j : 512 * i + 128 * j + 128] = t.recfk[j, :, 128 * i : 128 * i + 128].astype(F32)
    result(t.fk_out, g_fk)
    total = t.vtwo[...]
    for k in range(1, 4):
        arrive(t.vrec2.at[k], t.vsr.at[1, k])
        total = total + t.vrec2[k]
    t.v_out[...] = pltpu.roll(total, (128 - 32 * p) % 128, 1)
    result(t.v_out, g_vec)
    grad_x_in(KVG, 0)
    grad_z_in(KVG, put_kvg)
    hand_back(1, t.kvgpart, t.reckvg)
    handed_back(1, t.reckvg)
    result(t.reckvg, g_kvg)
    for _, copy in pending:
        copy.wait_send()
    for copy in results:
        copy.wait()


def finish_kernel(
    a_out, a_xgrad, a_o, a_fg, a_fk, a_fv, a_kvg, a_vec,
    out, xgrad, g_o, g_fg, g_fk, g_fv, g_k, g_v, g_g, *rest,
):
    vectors, held, sems = rest[:11], rest[11:17], rest[17]
    pairs = ((a_xgrad, xgrad), (a_out, out), (a_fk, g_fk), (a_fv, g_fv), (a_o, g_o), (a_fg, g_fg))
    inward = [pltpu.make_async_copy(src, mid, sems.at[0, i]) for i, ((src, _), mid) in enumerate(zip(pairs, held))]
    outward = [pltpu.make_async_copy(mid, dst, sems.at[1, i]) for i, ((_, dst), mid) in enumerate(zip(pairs, held))]
    for copy in inward:
        copy.start()
    piece = iota((32, 128), 1) // 32
    for w, ref in enumerate((g_k, g_v, g_g)):
        for h in range(2):
            first = 256 * w + 128 * h
            tiles = [a_kvg[q, :, first : first + 128].astype(F32) for q in range(4)]
            for j in range(4):
                total = jnp.zeros((32, 128), F32)
                for q in range(4):
                    turn = 32 * (q - j) % 128
                    total = jnp.where(piece == q, pltpu.roll(tiles[q], turn, 1) if turn else tiles[q], total)
                ref[:, 512 * h + 128 * j : 512 * h + 128 * j + 128] = total
    for k, ref in enumerate(vectors):
        ref[...] = a_vec[k, 0:32]
    for first, second in zip(inward, outward):
        first.wait()
        second.start()
    for copy in outward:
        copy.wait()


def fast_body(
    incoming_signal,
    document_extents,
    adjoint_signal,
    layernorm_scaling,
    layernorm_offset,
    temporal_blend_lookup,
    temporal_blend_content,
    temporal_blend_receptor,
    temporal_shrinkage_log,
    diagonal_reward,
    lookup_projection,
    content_projection,
    receptor_projection,
    emission_projection,
    latter_scaling,
    latter_offset,
    channel_blend_lookup,
    channel_blend_receptor,
    channel_mixer_lookup,
    channel_mixer_content,
    channel_mixer_receptor,
):
    vecs = jnp.stack(
        [
            layernorm_scaling,
            layernorm_offset,
            temporal_blend_lookup,
            temporal_blend_content,
            temporal_blend_receptor,
            temporal_shrinkage_log,
            diagonal_reward,
            latter_scaling,
            latter_offset,
            channel_blend_lookup,
            channel_blend_receptor,
        ]
    )
    vecs = jnp.pad(vecs, ((0, 5), (0, 96)))
    anywhere = pl.BlockSpec(memory_space=pl.ANY)
    vmem = pl.BlockSpec(memory_space=pltpu.VMEM)
    shape = jax.ShapeDtypeStruct
    whole = (
        shape((256, 1024), BF16),
        shape((256, 1024), F32),
        shape((32, 1024), F32),
        shape((32, 1024), F32),
        shape((32, 4096), F32),
        shape((128, 1024), F32),
    )
    made = pl.pallas_call(
        step_kernel,
        out_shape=(*whole, shape((4, 32, 768), BF16), shape((16, 128), F32)),
        in_specs=[pl.BlockSpec(memory_space=pltpu.SMEM)] + [anywhere] * 10,
        out_specs=[anywhere] * 8,
        scratch_shapes=list(scratch_list().values()),
        compiler_params=pltpu.CompilerParams(
            collective_id=0, has_side_effects=True, vmem_limit_bytes=63 * 1024 * 1024
        ),
    )(
        document_extents,
        incoming_signal,
        adjoint_signal,
        vecs,
        lookup_projection,
        content_projection,
        receptor_projection,
        emission_projection,
        channel_mixer_receptor,
        channel_mixer_lookup,
        channel_mixer_content,
    )
    out, xgrad, g_o, g_fg, g_fk, g_fv, g_k, g_v, g_g, *v = pl.pallas_call(
        finish_kernel,
        out_shape=(*whole, *[shape((32, 1024), F32)] * 3, *[shape((32,), F32)] * 11),
        in_specs=[anywhere] * 6 + [vmem] * 2,
        out_specs=[anywhere] * 6 + [vmem] * 14,
        scratch_shapes=[
            *[pltpu.VMEM(whole[i].shape, whole[i].dtype) for i in (1, 0, 4, 5, 2, 3)],
            pltpu.SemaphoreType.DMA((2, 6)),
        ],
    )(*made)
    return (out, xgrad, *v[:7], g_k, g_v, g_g, g_o, *v[7:], g_fk, g_fv, g_fg)


def solution(mesh):
    fast = (mesh.shape["seq"], mesh.shape["sp"]) == (8, 4)
    flat, wide = P(("seq", "sp")), P(("seq", "sp"), None)
    return jax.shard_map(
        fast_body if fast else plain_body,
        mesh=mesh,
        in_specs=(wide, P("seq", None), wide, *[flat] * 7, *[wide] * 4, *[flat] * 4, *[wide] * 3),
        out_specs=(wide, wide, *[flat] * 7, *[wide] * 4, *[flat] * 4, *[wide] * 3),
        check_vma=False,
    )
```

```python
import functools
import types

import jax
import jax.numpy as jnp
from jax import lax
from jax.experimental import pallas as pl
from jax.experimental.pallas import tpu as pltpu
from jax.sharding import PartitionSpec as P

LOOP_LENGTH = 128


HIGHEST = lax.Precision.HIGHEST
EPSILON = 1e-05


def shifted(value, axis, steps):
    count = lax.axis_size(axis)
    first, last = (max(0, -steps), min(count, count - steps))
    return lax.ppermute(value, axis, [(source, source + steps) for source in range(first, last)])


def norm_rows(content_vectors, gain, bias):
    centered = content_vectors - jnp.mean(content_vectors, axis=1, keepdims=True)
    scale = lax.rsqrt(jnp.mean(centered * centered, axis=1, keepdims=True) + EPSILON)
    return centered * scale * gain + bias


def running(lengths_row):
    ends = [lengths_row[0]]
    for i in range(1, lengths_row.shape[0]):
        ends.append(ends[-1] + lengths_row[i])
    return ends


def segment_ids(lengths_row, positions):
    ends = jnp.stack(running(lengths_row))
    bounds = jnp.concatenate([ends - lengths_row, ends[-1:]])
    document_tags = jnp.sum((positions[:, None] >= bounds[None, :]).astype(jnp.int32), axis=1) - 1
    return (document_tags, positions < ends[-1])


def weighted_attention_loop(
    lookup_vectors,
    content_vectors,
    temporal_shrinkage_log,
    diagonal_reward,
    document_tags,
    segment_piece,
):
    count, feature_dimension = lookup_vectors.shape
    blocks = count // segment_piece
    rate = jnp.exp(temporal_shrinkage_log)
    offsets = jnp.arange(segment_piece, dtype=jnp.float32)[:, None]
    grow = jnp.exp(offsets * rate)
    shrink_multiplier = jnp.exp(-(offsets - 1.0) * rate)
    fade = jnp.exp(-offsets * rate)
    tail_fade = jnp.exp(-(segment_piece - 1.0 - offsets) * rate)
    whole_fade = jnp.exp(-1.0 * segment_piece * rate)
    order = jnp.arange(segment_piece, dtype=jnp.int32)
    lower = order[None, :] < order[:, None]
    key_blocks = lookup_vectors.reshape(blocks, segment_piece, feature_dimension)
    value_blocks = content_vectors.reshape(blocks, segment_piece, feature_dimension)
    label_blocks = document_tags.reshape(blocks, segment_piece)
    before = jnp.concatenate([jnp.full((1,), -1, jnp.int32), label_blocks[:-1, -1]])

    @jax.checkpoint
    def advance(carry, items):
        dividend_total, divisor_total = carry
        lookup_portion, content_portion, label_part, last_label = items
        weight_key = jnp.exp(lookup_portion)
        links = ((label_part[:, None] == label_part[None, :]) & lower).astype(jnp.float32)
        scaled = grow * weight_key
        cumulative_totals = jnp.dot(
            links, jnp.concatenate([scaled * content_portion, scaled], axis=1), precision=HIGHEST
        )
        recurrent_memory = (label_part == last_label).astype(jnp.float32)[:, None] * fade
        initial_reward = jnp.exp(diagonal_reward + lookup_portion)
        highest_line_entry = (
            shrink_multiplier * cumulative_totals[:, :feature_dimension]
            + recurrent_memory * dividend_total
            + initial_reward * content_portion
        )
        lowest_line_entry = (
            shrink_multiplier * cumulative_totals[:, feature_dimension:]
            + recurrent_memory * divisor_total
            + initial_reward
        )
        end_label = label_part[-1]
        keep = (end_label == last_label).astype(jnp.float32) * whole_fade
        tail = (label_part == end_label).astype(jnp.float32)[:, None] * tail_fade * weight_key
        dividend_total = keep * dividend_total + jnp.sum(tail * content_portion, axis=0)
        divisor_total = keep * divisor_total + jnp.sum(tail, axis=0)
        return ((dividend_total, divisor_total), highest_line_entry / lowest_line_entry)

    zeros = jnp.zeros((feature_dimension,), jnp.float32)
    _, blended_signal = lax.scan(
        advance, (zeros, zeros), (key_blocks, value_blocks, label_blocks, before)
    )
    return blended_signal.reshape(count, feature_dimension)


def product(left, right):
    return jnp.dot(left, right, preferred_element_type=jnp.float32)


def times_transposed(left, right):
    return lax.dot_general(
        left, right, (((1,), (1,)), ((), ())), preferred_element_type=jnp.float32
    )


def outer_sum(left, right):
    return lax.dot_general(
        left, right, (((0,), (0,)), ((), ())), preferred_element_type=jnp.float32
    )


def blend(current, prior, share):
    return current * share + prior * (1.0 - share)


def blend_back(current, prior, shares, grads):
    current_grad = jnp.zeros_like(current)
    prior_grad = jnp.zeros_like(current)
    spread = current - prior
    share_grads = []
    for share, grad in zip(shares, grads):
        current_grad = current_grad + grad * share
        prior_grad = prior_grad + grad * (1.0 - share)
        share_grads.append(jnp.sum(spread * grad, axis=0))
    return (current_grad, prior_grad, share_grads)


def plain_body(
    incoming_signal,
    document_extents,
    adjoint_signal,
    layernorm_scaling,
    layernorm_offset,
    temporal_blend_lookup,
    temporal_blend_content,
    temporal_blend_receptor,
    temporal_shrinkage_log,
    diagonal_reward,
    lookup_projection,
    content_projection,
    receptor_projection,
    emission_projection,
    latter_scaling,
    latter_offset,
    channel_blend_lookup,
    channel_blend_receptor,
    channel_mixer_lookup,
    channel_mixer_content,
    channel_mixer_receptor,
):
    rows = incoming_signal.shape[0]
    feature_dimension = incoming_signal.shape[1]
    parts = lax.axis_size("sp")
    place = lax.axis_index("sp")
    group_rows = rows * parts
    channels = feature_dimension // parts
    lengths_row = document_extents[0]
    positions = place * rows + jnp.arange(rows, dtype=jnp.int32)
    document_tags, live = segment_ids(lengths_row, positions)
    earlier, _ = segment_ids(lengths_row, positions - 1)
    same = (document_tags == earlier).astype(jnp.float32)[:, None]
    live_rows = live.astype(jnp.float32)[:, None]
    group_labels, _ = segment_ids(lengths_row, jnp.arange(group_rows, dtype=jnp.int32))
    fetched = [
        lax.all_gather(piece, ("seq", "sp"), axis=0, tiled=True)
        for piece in (
            layernorm_scaling,
            layernorm_offset,
            temporal_blend_lookup,
            temporal_blend_content,
            temporal_blend_receptor,
            temporal_shrinkage_log,
            diagonal_reward,
            lookup_projection,
            content_projection,
            receptor_projection,
            emission_projection,
            latter_scaling,
            latter_offset,
            channel_blend_lookup,
            channel_blend_receptor,
            channel_mixer_lookup,
            channel_mixer_content,
            channel_mixer_receptor,
        )
    ]
    vectors = [fetched[i].astype(jnp.float32) for i in (0, 1, 2, 3, 4, 5, 6, 11, 12, 13, 14)]
    gain_one, bias_one, share_key, share_value, share_gate, decay_all, first_all = vectors[:7]
    gain_two, bias_two, feed_share_key, feed_share_gate = vectors[7:]
    key_matrix, value_matrix, gate_matrix, output_matrix = (
        fetched[7],
        fetched[8],
        fetched[9],
        fetched[10],
    )
    feed_key_matrix, feed_value_matrix, feed_gate_matrix = (fetched[15], fetched[16], fetched[17])
    source = incoming_signal.astype(jnp.float32)
    normed, norm_pull = jax.vjp(norm_rows, source, gain_one, bias_one)
    edge = shifted(normed[-1:], "sp", 1)
    prior = jnp.concatenate([edge, normed[:-1]], axis=0) * same
    key_in = blend(normed, prior, share_key).astype(jnp.bfloat16)
    value_in = blend(normed, prior, share_value).astype(jnp.bfloat16)
    gate_in = blend(normed, prior, share_gate).astype(jnp.bfloat16)
    lookup_vectors = product(key_in, key_matrix).astype(jnp.bfloat16)
    content_vectors = product(value_in, value_matrix).astype(jnp.bfloat16)
    gate = jax.nn.sigmoid(product(gate_in, gate_matrix))
    arrived = lax.all_to_all(
        jnp.stack([lookup_vectors, content_vectors]), "sp", split_axis=2, concat_axis=1, tiled=True
    )
    decay_part = lax.dynamic_slice_in_dim(decay_all, place * channels, channels)
    first_part = lax.dynamic_slice_in_dim(first_all, place * channels, channels)

    def recurrence(key_full, value_full, decay_here, first_here):
        return weighted_attention_loop(
            key_full, value_full, decay_here, first_here, group_labels, LOOP_LENGTH
        )

    blended_signal, scan_pull = jax.vjp(
        recurrence,
        arrived[0].astype(jnp.float32),
        arrived[1].astype(jnp.float32),
        decay_part,
        first_part,
    )
    mixed_rows = lax.all_to_all(
        blended_signal.astype(jnp.bfloat16), "sp", split_axis=0, concat_axis=1, tiled=True
    ).astype(jnp.float32)
    gated = (gate * mixed_rows).astype(jnp.bfloat16)
    middle = source + product(gated, output_matrix)
    second, second_pull = jax.vjp(norm_rows, middle, gain_two, bias_two)
    second_edge = shifted(second[-1:], "sp", 1)
    prior_second = jnp.concatenate([second_edge, second[:-1]], axis=0) * same
    feed_key_in = blend(second, prior_second, feed_share_key).astype(jnp.bfloat16)
    feed_gate_in = blend(second, prior_second, feed_share_gate).astype(jnp.bfloat16)
    raised = product(feed_key_in, feed_key_matrix)
    hidden = jnp.square(jax.nn.relu(raised)).astype(jnp.bfloat16)
    recurrent_memory = product(hidden, feed_value_matrix)
    feed_sig = jax.nn.sigmoid(product(feed_gate_in, feed_gate_matrix))
    block_out = (live_rows * (middle + feed_sig * recurrent_memory)).astype(jnp.bfloat16)
    upstream = adjoint_signal.astype(jnp.float32) * live_rows
    carried_grad = (upstream * feed_sig).astype(jnp.bfloat16)
    feed_pre_grad = (upstream * recurrent_memory * feed_sig * (1.0 - feed_sig)).astype(jnp.bfloat16)
    grad_feed_value = outer_sum(hidden, carried_grad)
    grad_feed_gate = outer_sum(feed_gate_in, feed_pre_grad)
    raised_grad = (
        times_transposed(carried_grad, feed_value_matrix) * 2.0 * jax.nn.relu(raised)
    ).astype(jnp.bfloat16)
    grad_feed_key = outer_sum(feed_key_in, raised_grad)
    second_grad, second_prior_grad, feed_share_grads = blend_back(
        second,
        prior_second,
        (feed_share_key, feed_share_gate),
        (
            times_transposed(raised_grad, feed_key_matrix),
            times_transposed(feed_pre_grad, feed_gate_matrix),
        ),
    )
    moved = second_prior_grad * same
    incoming = shifted(moved[:1], "sp", -1)
    second_grad = second_grad + jnp.concatenate([moved[1:], incoming], axis=0)
    middle_norm_grad, grad_second_gain, grad_second_bias = second_pull(second_grad)
    middle_grad = upstream + middle_norm_grad
    attended_grad = middle_grad.astype(jnp.bfloat16)
    grad_output_weight = outer_sum(gated, attended_grad)
    gated_grad = times_transposed(attended_grad, output_matrix)
    mixed_grad = (gated_grad * gate).astype(jnp.bfloat16)
    gate_pre_grad = (gated_grad * mixed_rows * gate * (1.0 - gate)).astype(jnp.bfloat16)
    channel_grad = lax.all_to_all(mixed_grad, "sp", split_axis=1, concat_axis=0, tiled=True)
    key_grad_here, value_grad_here, decay_grad_here, first_grad_here = scan_pull(
        channel_grad.astype(jnp.float32)
    )
    returned = lax.all_to_all(
        jnp.stack([key_grad_here, value_grad_here]).astype(jnp.bfloat16),
        "sp",
        split_axis=1,
        concat_axis=2,
        tiled=True,
    )
    key_grad = returned[0]
    value_grad = returned[1]
    grad_key_weight = outer_sum(key_in, key_grad)
    grad_value_weight = outer_sum(value_in, value_grad)
    grad_gate_weight = outer_sum(gate_in, gate_pre_grad)
    normed_grad, normed_prior_grad, share_grads = blend_back(
        normed,
        prior,
        (share_key, share_value, share_gate),
        (
            times_transposed(key_grad, key_matrix),
            times_transposed(value_grad, value_matrix),
            times_transposed(gate_pre_grad, gate_matrix),
        ),
    )
    moved_first = normed_prior_grad * same
    incoming_first = shifted(moved_first[:1], "sp", -1)
    normed_grad = normed_grad + jnp.concatenate([moved_first[1:], incoming_first], axis=0)
    source_norm_grad, grad_norm_gain, grad_norm_bias = norm_pull(normed_grad)
    input_grad = middle_grad + source_norm_grad
    decay_grad = lax.dynamic_update_slice_in_dim(
        jnp.zeros((feature_dimension,), jnp.float32), decay_grad_here, place * channels, 0
    )
    first_grad = lax.dynamic_update_slice_in_dim(
        jnp.zeros((feature_dimension,), jnp.float32), first_grad_here, place * channels, 0
    )
    grads = (
        grad_norm_gain,
        grad_norm_bias,
        *share_grads,
        decay_grad,
        first_grad,
        grad_key_weight,
        grad_value_weight,
        grad_gate_weight,
        grad_output_weight,
        grad_second_gain,
        grad_second_bias,
        *feed_share_grads,
        grad_feed_key,
        grad_feed_value,
        grad_feed_gate,
    )
    shares = []
    for grad in grads:
        for axis in ("seq", "sp"):
            grad = lax.psum_scatter(
                grad.astype(jnp.bfloat16), axis, scatter_dimension=0, tiled=True
            ).astype(jnp.float32)
        shares.append(grad)
    return (block_out, input_grad, *shares)


MESH = pl.DeviceIdType.MESH
F32 = jnp.float32
BF16 = jnp.bfloat16
GAIN1, BIAS1, MIXK, MIXV, MIXG, DECAY, FIRST, GAIN2, BIAS2, FMIXK, FMIXG = range(11)


def multiple(value, step):
    return pl.multiple_of(value, step)


def nn(a, b):
    return jnp.dot(a, b, preferred_element_type=F32)


def nt(a, b):
    return lax.dot_general(a, b, (((1,), (1,)), ((), ())), preferred_element_type=F32)


def tn(a, b):
    return lax.dot_general(a, b, (((0,), (0,)), ((), ())), preferred_element_type=F32)


def exact_dot(links, right):
    high = right.astype(BF16)
    rest = right - high.astype(F32)
    middle = rest.astype(BF16)
    low = (rest - middle.astype(F32)).astype(BF16)
    return nn(links, high) + nn(links, middle) + nn(links, low)


def iota(shape, axis):
    return lax.broadcasted_iota(jnp.int32, shape, axis)


def spread_rows(v):
    centered = v - jnp.mean(v, axis=1, keepdims=True)
    scale = lax.rsqrt(jnp.mean(centered * centered, axis=1, keepdims=True) + EPSILON)
    return centered * scale, scale


def column_sum(v):
    return jnp.sum(v, axis=0, keepdims=True)


def scratch_list():
    vm = pltpu.VMEM
    sem = pltpu.SemaphoreType.DMA
    return dict(
        xall=vm((1024, 1024), BF16),
        kin=vm((1024, 1024), BF16),
        vin=vm((1024, 1024), BF16),
        gin=vm((1024, 1024), BF16),
        spread=vm((1024, 1024), BF16),
        wkvg=vm((1024, 768), BF16),
        wo=vm((256, 1024), BF16),
        wfg=vm((8, 128, 1024), BF16),
        wfk=vm((1024, 1024), BF16),
        wfv=vm((1024, 1024), BF16),
        kk=vm((1024, 256), BF16),
        vv=vm((1024, 256), BF16),
        gate=vm((1024, 256), F32),
        mixed=vm((1024, 256), F32),
        inverse=vm((1024, 256), F32),
        gated=vm((1024, 256), BF16),
        carry=vm((8, 8, 256), F32),
        tables=vm((4, 128, 256), F32),
        small=vm((8, 256), F32),
        last=vm((8, 1024), F32),
        xo=vm((256, 1024), BF16),
        adj=vm((256, 1024), BF16),
        mid=vm((256, 1024), F32),
        sec=vm((256, 1024), F32),
        edge=vm((4, 16, 1024), BF16),
        sig=vm((256, 1024), F32),
        fgin=vm((256, 1024), BF16),
        fpg=vm((256, 1024), BF16),
        fkall=vm((1024, 1024), BF16),
        cgall=vm((1024, 1024), BF16),
        hidden=vm((1024, 1024), BF16),
        gfv=vm((1024, 1024), BF16),
        rgrad=vm((1024, 1024), BF16),
        acca=vm((256, 1024), F32),
        accb=vm((256, 1024), F32),
        fgg=vm((256, 1024), F32),
        moved=vm((264, 1024), F32),
        csa=vm((2, 256, 1024), BF16),
        cra=vm((2, 256, 1024), BF16),
        ysa=vm((256, 1024), BF16),
        yra=vm((256, 1024), BF16),
        csb=vm((2, 256, 1024), BF16),
        crb=vm((2, 256, 1024), BF16),
        ysb=vm((256, 1024), BF16),
        yrb=vm((256, 1024), BF16),
        fgcr=vm((2, 8, 32, 1024), BF16),
        fgyr=vm((8, 32, 1024), BF16),
        xrfv=vm((4, 128, 1024), BF16),
        xrfk=vm((4, 128, 1024), BF16),
        xrfg=vm((4, 32, 1024), BF16),
        xro=vm((4, 32, 1024), BF16),
        xrkvg=vm((4, 128, 768), BF16),
        zrfv=vm((3, 128, 1024), BF16),
        zrfk=vm((3, 128, 1024), BF16),
        zrfg=vm((3, 32, 1024), BF16),
        zro=vm((3, 32, 1024), BF16),
        zrkvg=vm((3, 128, 768), BF16),
        kvgraw=vm((3, 32, 1024), BF16),
        fkraw=vm((32, 4096), BF16),
        kvgpart=vm((4, 32, 768), BF16),
        fkpart=vm((4, 32, 1024), BF16),
        o_out=vm((32, 1024), F32),
        fg_out=vm((32, 1024), F32),
        fk_out=vm((32, 4096), F32),
        b_out=vm((256, 1024), BF16),
        v_out=vm((16, 128), F32),
        recfk=vm((4, 32, 1024), BF16),
        reckvg=vm((4, 32, 768), BF16),
        vraw=vm((8, 4, 16, 128), BF16),
        nat=vm((16, 1024), F32),
        chan=vm((16, 256), F32),
        vg=vm((16, 8, 1024), F32),
        vgc=vm((16, 256), F32),
        vmsg=vm((8, 16, 128), F32),
        vrec=vm((8, 16, 128), F32),
        vtwo=vm((16, 128), F32),
        vrec2=vm((4, 16, 128), F32),
        ags=sem((6, 9)),
        agr=sem((6, 8)),
        a2s=sem((3, 3)),
        a2r=sem((3, 4)),
        sps=sem((5, 3)),
        spr=sem((5, 3)),
        rss=sem((5, 3)),
        rsr=sem((5, 3)),
        qxs=sem((5, 4)),
        qxr=sem((5, 4)),
        qzs=sem((5, 3)),
        qzr=sem((5, 3)),
        fas=sem((2, 3)),
        far=sem((2, 4)),
        vss=sem((2, 7)),
        vsr=sem((2, 8)),
        eds=sem((4,)),
        edr=sem((5,)),
        loc=sem((24,)),
    )


def step_kernel(
    lengths, xin, adjoint, vecs, k_in, v_in, g_in, o_in, fg_in, fk_in, fv_in,
    out, xgrad, g_o, g_fg, g_fk, g_fv, g_kvg, g_vec,
    *scratch,
):
    t = types.SimpleNamespace(**dict(zip(scratch_list(), scratch)))
    s, p = lax.axis_index("seq"), lax.axis_index("sp")
    z, x, y, c = s // 2, s % 2, p // 2, p % 2
    zs = [(z + k) % 4 for k in range(4)]
    xdev = (z * 2 + 1 - x, p)
    ydev, sib = (s, (1 - y) * 2 + c), (s, y * 2 + 1 - c)
    sps = [(p + k) % 4 for k in range(4)]
    sqs = [(s + k) % 8 for k in range(8)]
    p_sib, p_y, p_diag = y * 2 + 1 - c, (1 - y) * 2 + c, (1 - y) * 2 + 1 - c

    pending = []

    def remote(src, dst, send_sem, recv_sem, device):
        return pltpu.make_async_remote_copy(
            src_ref=src, dst_ref=dst, send_sem=send_sem, recv_sem=recv_sem,
            device_id=device, device_id_type=MESH,
        )

    def send(src, dst, send_sem, recv_sem, device, tag=None):
        copy = remote(src, dst, send_sem, recv_sem, device)
        copy.start()
        pending.append((tag, copy, None))
        return copy

    def left(copy, cond):
        if cond is None:
            copy.wait_send()
        else:
            pl.when(cond)(copy.wait_send)

    def settle(*tags):
        for tag, copy, cond in pending:
            if tag in tags:
                left(copy, cond)
        pending[:] = [entry for entry in pending if entry[0] not in tags]

    def arrive(dst, recv_sem):
        remote(dst, dst, recv_sem, recv_sem, sib).wait_recv()

    def local(src, dst, k):
        copy = pltpu.make_async_copy(src, dst, t.loc.at[k])
        copy.start()
        return copy

    loads = []

    def load(src, dst):
        copy = pltpu.make_async_copy(src, dst, t.loc.at[len(loads)])
        copy.start()
        loads.append(copy)

    def own_rows(ref, size):
        return ref.at[pl.ds(multiple(s * size, size), size)]

    load(k_in, t.kvgraw.at[0])
    load(v_in, t.kvgraw.at[1])
    load(g_in, t.kvgraw.at[2])
    load(vecs, t.vraw.at[s, p])
    load(fk_in, t.fkraw)
    early = len(loads)
    load(xin, t.xall.at[pl.ds(multiple(p * 256, 256), 256)])
    load(o_in, own_rows(t.wo, 32))
    load(fg_in, t.wfg.at[s, pl.ds(multiple(p * 32, 32), 32)])
    load(fv_in, own_rows(t.wfv, 128))
    load(xin, t.xo)
    load(adjoint, t.adj)
    load(adjoint, t.rgrad.at[pl.ds(multiple(p * 256, 256), 256)])
    for copy in loads[:4]:
        copy.wait()
    piece = iota((32, 128), 1) // 32
    for w in range(3):
        for h in range(2):
            tiles = [t.kvgraw[w, :, 512 * h + 128 * j : 512 * h + 128 * j + 128].astype(F32) for j in range(4)]
            for q in range(4):
                total = jnp.zeros((32, 128), F32)
                for j in range(4):
                    turn = 32 * (j - q) % 128
                    total = jnp.where(piece == j, pltpu.roll(tiles[j], turn, 1) if turn else tiles[j], total)
                t.kvgpart[q, :, 256 * w + 128 * h : 256 * w + 128 * h + 128] = total.astype(BF16)
    loads[4].wait()
    for i in range(8):
        for q in range(4):
            t.fkpart[q, :, 128 * i : 128 * i + 128] = t.fkraw[:, 512 * i + 128 * q : 512 * i + 128 * q + 128]

    barrier = pltpu.get_barrier_semaphore()
    for k in range(1, 8):
        pl.semaphore_signal(barrier, inc=1, device_id=(sqs[k], p), device_id_type=MESH)
    for k in range(1, 4):
        pl.semaphore_signal(barrier, inc=1, device_id=(s, sps[k]), device_id_type=MESH)
    pl.semaphore_wait(barrier, 10)

    def rows(ref, size):
        return lambda i: ref.at[pl.ds(multiple(i * size, size), size)]

    V, A, B, C, D, E = range(6)
    block = {
        V: lambda i: t.vraw.at[i],
        A: rows(t.wkvg, 128),
        B: rows(t.wo, 32),
        C: lambda i: t.wfg.at[i, pl.ds(multiple(p * 32, 32), 32)],
        D: rows(t.wfk, 128),
        E: rows(t.wfv, 128),
    }

    inner = (z == 1) | (z == 2)
    far = (z + 2) % 4
    beside = 1 + z % 2
    outer = 3 * (z // 2)

    def pick(*values):
        return sum((z == i).astype(jnp.int32) * v for i, v in enumerate(values))

    sources = (pick(1, 3, 0, 2), pick(2, 0, 3, 1), pick(3, 2, 1, 0))

    def send_if(cond, src, dst, send_sem, recv_sem, device, tag=None):
        copy = remote(src, dst, send_sem, recv_sem, device)
        pl.when(cond)(copy.start)
        pending.append((tag, copy, cond))

    def along_z(item, i, src, first):
        there = block[item](i)
        send(src, there, t.ags.at[item, first], t.agr.at[item, i], (far * 2 + x, p), item)
        send(src, there, t.ags.at[item, first + 1], t.agr.at[item, i], (beside * 2 + x, p), item)
        send_if(inner, src, there, t.ags.at[item, first + 2], t.agr.at[item, i], (outer * 2 + x, p), item)

    def hand_on(item, i, sem):
        send_if(inner, block[item](i), block[item](i), t.ags.at[item, sem], t.agr.at[item, i], (outer * 2 + x, p), item)

    def own_out(item, src):
        send(src, block[item](s), t.ags.at[item, 0], t.agr.at[item, s], xdev, item)
        if item == V:
            for k in range(1, 4):
                send(src, block[V](s), t.ags.at[V, k], t.agr.at[V, s], (zs[k] * 2 + x, p), V)
        else:
            along_z(item, s, src, 1)

    def pass_on(item, j):
        i = sources[j] * 2 + x
        arrive(block[item](i), t.agr.at[item, i])
        send(block[item](i), block[item](i), t.ags.at[item, 4 + j], t.agr.at[item, i], xdev, item)
        if j == 0 and item != V:
            hand_on(item, i, 7)

    def all_in(item):
        for k in range(4):
            i = zs[k] * 2 + 1 - x
            arrive(block[item](i), t.agr.at[item, i])

    def sp_out(n, view):
        send(view(p), view(p), t.sps.at[n, 0], t.spr.at[n, 0], ydev, ("sp", n))
        send(view(p), view(p), t.sps.at[n, 1], t.spr.at[n, 1], sib, ("sp", n))

    def sp_pass(n, view):
        arrive(view(p_y), t.spr.at[n, 0])
        send(view(p_y), view(p_y), t.sps.at[n, 2], t.spr.at[n, 2], sib, ("sp", n))

    def sp_sib(n, view):
        arrive(view(p_sib), t.spr.at[n, 1])

    def sp_diag(n, view):
        arrive(view(p_diag), t.spr.at[n, 2])

    def add_rows(n, fn):
        @pl.loop(0, n // 32)
        def _(i):
            fn(pl.ds(multiple(i * 32, 32), 32))

    def sum_begin(n, cs, cr, ys, yr, acc, compute):
        def to_sibling(j, q):
            cs[j] = compute(q).astype(BF16)
            send(cs.at[j], cr.at[j], t.rss.at[n, j], t.rsr.at[n, j], sib, ("sum", n))

        def to_other(r):
            ys[r, :] = (acc[r, :] + cr[0, r, :].astype(F32)).astype(BF16)

        def to_own(r):
            acc[r, :] += cr[1, r, :].astype(F32)

        to_sibling(0, p_diag)
        acc[...] = compute(p_y)
        arrive(cr.at[0], t.rsr.at[n, 0])
        add_rows(256, to_other)
        send(ys, yr, t.rss.at[n, 2], t.rsr.at[n, 2], ydev, ("sum", n))
        to_sibling(1, p_sib)
        acc[...] = compute(p)
        arrive(cr.at[1], t.rsr.at[n, 1])
        add_rows(256, to_own)

    def sum_end(n, yr, acc):
        arrive(yr, t.rsr.at[n, 2])

        def add(r):
            acc[r, :] += yr[r, :].astype(F32)

        add_rows(256, add)
        settle(("sum", n))

    FV, FK, FG, O, KVG = range(5)
    grads = {
        FV: (t.gfv, t.xrfv, t.zrfv, 128),
        FK: (t.wfk, t.xrfk, t.zrfk, 128),
        FG: (t.fgin, t.xrfg, t.zrfg, 32),
        O: (t.wo, t.xro, t.zro, 32),
        KVG: (t.rgrad, t.xrkvg, t.zrkvg, 128),
    }

    def piece_of(item, i):
        ref, xr, _, size = grads[item]
        return ref.at[pl.ds(multiple(i * size, size), size), pl.ds(0, xr.shape[2])]

    def grad_x_out(item, zz):
        _, xr, _, _ = grads[item]
        send(piece_of(item, zz * 2 + 1 - x), xr.at[zz], t.qxs.at[item, zz], t.qxr.at[item, zz], xdev)

    def grad_x_in(item, k):
        ref, xr, zr, size = grads[item]
        zz = zs[k]
        arrive(xr.at[zz], t.qxr.at[item, zz])
        if k == 0:
            return
        base = (zz * 2 + x) * size

        def add(r):
            here = pl.ds(multiple(base + r.start, 32), 32)
            w = pl.ds(0, xr.shape[2])
            ref[here, w] = (ref[here, w].astype(F32) + xr[zz, r, :].astype(F32)).astype(BF16)

        add_rows(size, add)
        send(piece_of(item, zz * 2 + x), zr.at[k - 1], t.qzs.at[item, k - 1], t.qzr.at[item, k - 1], (zz * 2 + x, p))

    def grad_z_in(item, put):
        ref, xr, zr, size = grads[item]
        for k in range(1, 4):
            arrive(zr.at[k - 1], t.qzr.at[item, k - 1])

        @pl.loop(0, size // 32)
        def _(i):
            r = pl.ds(multiple(i * 32, 32), 32)
            here = pl.ds(multiple(s * size + i * 32, 32), 32)
            total = ref[here, pl.ds(0, xr.shape[2])].astype(F32) + xr[z, r, :].astype(F32)
            total = total + zr[0, r, :].astype(F32) + zr[1, r, :].astype(F32) + zr[2, r, :].astype(F32)
            put(i, r, total)

    def hand_back(n, fin, rec):
        for k in range(1, 4):
            send(fin.at[sps[k]], rec.at[p], t.fas.at[n, k - 1], t.far.at[n, p], (s, sps[k]))
        rec[p] = fin[p]

    def handed_back(n, rec):
        for k in range(1, 4):
            arrive(rec.at[sps[k]], t.far.at[n, sps[k]])

    e0 = lengths[0, 0]
    e1 = e0 + lengths[0, 1]
    e2 = e1 + lengths[0, 2]
    e3 = e2 + lengths[0, 3]

    def label(pos):
        total = (pos >= 0).astype(jnp.int32)
        for edge in (e0, e1, e2, e3):
            total = total + (pos >= edge).astype(jnp.int32)
        return total - 1

    def same_at(pos):
        return (label(pos) == label(pos - 1)).astype(F32)

    xview = rows(t.xall, 256)

    def a2a_out(n, src, dst):
        for k in (2, 1, 3):
            send(src(sps[k]), dst(p), t.a2s.at[n, k - 1], t.a2r.at[n, p], (s, sps[k]), ("a2a", n))

    def a2a_in(n, dst):
        for k in range(1, 4):
            arrive(dst(sps[k]), t.a2r.at[n, sps[k]])

    vec_dst = lambda i: t.vraw.at[s, i]
    kvg_dst = lambda i: t.wkvg.at[pl.ds(multiple(s * 128 + i * 32, 32), 32)]
    fk_dst = lambda i: t.wfk.at[pl.ds(multiple(s * 128 + i * 32, 32), 32)]
    a2a_out(0, lambda i: vecs, vec_dst)
    a2a_out(1, lambda i: t.kvgpart.at[i], kvg_dst)
    a2a_out(2, lambda i: t.fkpart.at[i], fk_dst)
    send(xin, xview(p), t.sps.at[0, 0], t.spr.at[0, 0], ydev)
    send(xin, xview(p), t.sps.at[0, 1], t.spr.at[0, 1], sib)
    adjview = rows(t.rgrad, 256)
    send(adjoint, adjview(p), t.sps.at[3, 0], t.spr.at[3, 0], ydev, ("sp", 3))
    send(adjoint, adjview(p), t.sps.at[3, 1], t.spr.at[3, 1], sib, ("sp", 3))
    t.wkvg[pl.ds(multiple(s * 128 + p * 32, 32), 32), :] = t.kvgpart[p]
    t.wfk[pl.ds(multiple(s * 128 + p * 32, 32), 32), :] = t.fkpart[p]
    a2a_in(0, vec_dst)
    own_out(V, t.vraw.at[s])
    a2a_in(1, kvg_dst)
    own_out(A, block[A](s))
    own_out(C, fg_in)
    own_out(B, o_in)
    for copy in loads[early:]:
        copy.wait()
    for j in range(3):
        pass_on(V, j)
    a2a_in(2, fk_dst)
    all_in(V)

    t.last[...] = jnp.zeros_like(t.last)
    t.vg[...] = jnp.zeros_like(t.vg)
    t.vgc[...] = jnp.zeros_like(t.vgc)
    for i in range(8):
        total = t.vraw[i, 0].astype(F32)
        for j in range(1, 4):
            total = total + pltpu.roll(t.vraw[i, j].astype(F32), 32 * j, 1)
        t.nat[:, 128 * i : 128 * i + 128] = total
    for i in range(2):
        total = t.vraw[4 * i, p].astype(F32)
        for j in range(1, 4):
            total = total + pltpu.roll(t.vraw[4 * i + j, p].astype(F32), 32 * j, 1)
        t.chan[:, 128 * i : 128 * i + 128] = total

    def vector(k):
        return t.nat[k : k + 1, :]

    rate = jnp.exp(t.chan[DECAY : DECAY + 1, :])
    offset = iota((128, 1), 0).astype(F32)
    t.tables[0] = jnp.exp(offset * rate)
    t.tables[1] = jnp.exp(-(offset - 1.0) * rate)
    t.tables[2] = jnp.exp(-offset * rate)
    t.tables[3] = jnp.exp(-(127.0 - offset) * rate)
    t.small[0:1, :] = jnp.exp(-128.0 * rate)
    t.small[1:2, :] = jnp.exp(t.chan[FIRST : FIRST + 1, :])
    t.small[2:3, :] = rate

    pass_on(A, 0)
    pass_on(C, 0)
    pass_on(B, 0)
    pass_on(A, 1)
    pass_on(C, 1)
    sp_pass(0, xview)
    sp_sib(0, xview)
    pass_on(A, 2)
    own_out(D, block[D](s))
    sp_diag(0, xview)

    def norm_quarter(q):
        @pl.loop(0, 8)
        def _(i):
            base = q * 256 + i * 32
            r = pl.ds(multiple(base, 32), 32)
            hat, _ = spread_rows(t.xall[r, :].astype(F32))
            normed = hat * vector(GAIN1) + vector(BIAS1)
            row = iota((32, 1), 0)
            prior = jnp.where(row == 0, t.last[0:1, :], pltpu.roll(normed, 1, 0))
            prior = prior * same_at(base + row)
            t.last[0:1, :] = normed[31:32, :]
            diff = normed - prior
            t.spread[r, :] = diff.astype(BF16)
            t.kin[r, :] = (prior + diff * vector(MIXK)).astype(BF16)
            t.vin[r, :] = (prior + diff * vector(MIXV)).astype(BF16)
            t.gin[r, :] = (prior + diff * vector(MIXG)).astype(BF16)

    norm_quarter(0)
    pass_on(C, 2)
    pass_on(B, 1)
    norm_quarter(1)
    pass_on(B, 2)
    own_out(E, fv_in)
    norm_quarter(2)
    norm_quarter(3)
    all_in(C)
    fgview = lambda i: t.wfg.at[:, pl.ds(multiple(i * 32, 32), 32)]
    sp_out(1, fgview)
    all_in(A)
    settle(("sp", 0))

    @pl.loop(0, 4)
    def _(i):
        r = pl.ds(multiple(i * 256, 256), 256)
        t.kk[r, :] = nn(t.kin[r, :], t.wkvg[:, 0:256]).astype(BF16)
        t.vv[r, :] = nn(t.vin[r, :], t.wkvg[:, 256:512]).astype(BF16)
        t.gate[r, :] = jax.nn.sigmoid(nn(t.gin[r, :], t.wkvg[:, 512:768]))

    def block_parts(b):
        base = b * 128
        column = label(base + iota((128, 1), 0))
        row = label(base + iota((1, 128), 1))
        before, end = label(base - 1), label(base + 127)
        alike = column == row
        keep = (before == end).astype(F32) * t.small[0:1, :]
        memory = (column == before).astype(F32) * t.tables[2]
        tail = (column == end).astype(F32) * t.tables[3]
        return alike, keep, memory, tail

    def forward_block(b, held):
        top, bottom = held
        r = pl.ds(multiple(b * 128, 128), 128)
        alike, keep, memory, tail = block_parts(b)
        links = (alike & (iota((128, 128), 1) < iota((128, 128), 0))).astype(F32).astype(BF16)
        v = t.vv[r, :].astype(F32)
        weight = jnp.exp(t.kk[r, :].astype(F32))
        scaled = t.tables[0] * weight
        sums = exact_dot(links, jnp.concatenate([scaled * v, scaled], axis=1))
        own = t.small[1:2, :] * weight
        high = t.tables[1] * sums[:, :256] + memory * top + own * v
        low = t.tables[1] * sums[:, 256:] + memory * bottom + own
        inverse = 1.0 / low
        mixed = high * inverse
        t.inverse[r, :] = inverse
        t.mixed[r, :] = mixed
        t.gated[r, :] = (t.gate[r, :] * mixed.astype(BF16).astype(F32)).astype(BF16)
        t.carry[b, 0:1, :] = top
        t.carry[b, 1:2, :] = bottom
        tail = tail * weight
        return keep * top + column_sum(tail * v), keep * bottom + column_sum(tail)

    zero = jnp.zeros((1, 256), F32)
    held = lax.fori_loop(0, 4, forward_block, (zero, zero))
    held = lax.fori_loop(4, 8, forward_block, held)

    pass_on(D, 0)
    all_in(B)

    def quarter(ref, q):
        return ref[pl.ds(multiple(q * 256, 256), 256), :]

    sum_begin(0, t.csa, t.cra, t.ysa, t.yra, t.acca, lambda q: nn(quarter(t.gated, q), t.wo[...]))
    pass_on(D, 1)
    sp_pass(3, adjview)
    sp_sib(3, adjview)
    sp_pass(1, fgview)
    sp_sib(1, fgview)
    pass_on(D, 2)
    sp_diag(3, adjview)
    sum_end(0, t.yra, t.acca)

    secview = rows(t.gfv, 256)

    def second_tile(i):
        r = pl.ds(multiple(i * 32, 32), 32)
        middle = t.xo[r, :].astype(F32) + t.acca[r, :]
        t.mid[r, :] = middle
        hat, _ = spread_rows(middle)
        second = (hat * vector(GAIN2) + vector(BIAS2)).astype(BF16)
        t.gfv[pl.ds(multiple(p * 256 + i * 32, 32), 32), :] = second
        return second

    t.edge[p] = second_tile(7)[16:32]
    for k in range(1, 4):
        send(t.edge.at[p], t.edge.at[p], t.eds.at[k], t.edr.at[p], (s, sps[k]))

    @pl.loop(0, 7)
    def _(i):
        second_tile(i)

    sp_out(2, secview)
    pass_on(E, 0)
    sp_diag(1, fgview)

    def feed_gate_weight():
        return t.wfg[...].reshape(1024, 1024)

    def live_rows(r, base):
        pos = base + iota((32, 1), 0)
        return t.rgrad[r, :].astype(F32) * (pos < e3).astype(F32)

    def feed_rows(q, fgin, mine):
        before = (q + 3) % 4
        t.last[0:1, :] = t.edge[before, 15:16, :].astype(F32)

        @pl.loop(0, 8)
        def _(i):
            base = q * 256 + i * 32
            r, u = pl.ds(multiple(base, 32), 32), pl.ds(multiple(i * 32, 32), 32)
            second = t.gfv[r, :].astype(F32)
            row = iota((32, 1), 0)
            prior = jnp.where(row == 0, t.last[0:1, :], pltpu.roll(second, 1, 0)) * same_at(base + row)
            t.last[0:1, :] = second[31:32, :]
            diff = second - prior
            if mine:
                t.sec[u, :] = diff
            t.fkall[r, :] = (prior + diff * vector(FMIXK)).astype(BF16)
            fgin[u, :] = (prior + diff * vector(FMIXG)).astype(BF16)

        gate = t.sig if mine else t.fgg
        gate[...] = jax.nn.sigmoid(nn(fgin[...], feed_gate_weight()))

        @pl.loop(0, 8)
        def _(i):
            base = q * 256 + i * 32
            r, u = pl.ds(multiple(base, 32), 32), pl.ds(multiple(i * 32, 32), 32)
            t.cgall[r, :] = (live_rows(r, base) * gate[u, :]).astype(BF16)

    def upstream(i):
        pos = p * 256 + i * 32 + iota((32, 1), 0)
        return t.adj[pl.ds(multiple(i * 32, 32), 32), :].astype(F32) * (pos < e3).astype(F32)

    def raise_rows(q):
        r = pl.ds(multiple(q * 256, 256), 256)
        relu = jnp.maximum(nn(t.fkall[r, :], t.wfk[...]), 0.0)
        t.hidden[r, :] = (relu * relu).astype(BF16)

    for k in range(1, 4):
        arrive(t.edge.at[sps[k]], t.edr.at[sps[k]])
    feed_rows(p, t.fgin, True)
    pass_on(E, 1)
    sp_sib(2, secview)
    feed_rows(p_sib, t.fpg, False)
    all_in(D)
    raise_rows(p)
    raise_rows(p_sib)
    sp_pass(2, secview)
    feed_rows(p_y, t.fpg, False)
    raise_rows(p_y)
    pass_on(E, 2)
    sp_diag(2, secview)
    feed_rows(p_diag, t.fpg, False)
    raise_rows(p_diag)
    settle(("sp", 2), ("sp", 3))
    for k in (1, 2, 3, 0):
        q = pl.ds(multiple(zs[k] * 256, 256), 256)
        t.gfv[q, :] = tn(t.hidden[:, q], t.cgall[...]).astype(BF16)
        grad_x_out(FV, zs[k])
    all_in(E)
    sum_begin(1, t.csb, t.crb, t.ysb, t.yrb, t.accb, lambda q: nn(quarter(t.hidden, q), t.wfv[...]))

    def lower_rows(q):
        r = pl.ds(multiple(q * 256, 256), 256)
        t.rgrad[r, :] = (nt(t.cgall[r, :], t.wfv[...]) * 2.0 * jnp.sqrt(t.hidden[r, :].astype(F32))).astype(BF16)

    for q in (p_diag, p_sib, p_y, p):
        lower_rows(q)
    grad_x_in(FV, 1)
    sum_begin(2, t.csa, t.cra, t.ysa, t.yra, t.acca, lambda q: nt(quarter(t.rgrad, q), t.wfk[...]))

    settle(D)
    for k in (1, 2, 3, 0):
        q = pl.ds(multiple(zs[k] * 256, 256), 256)
        t.wfk[q, :] = tn(t.fkall[:, q], t.rgrad[...]).astype(BF16)
        grad_x_out(FK, zs[k])

    sum_end(1, t.yrb, t.accb)

    @pl.loop(0, 8)
    def _(i):
        r = pl.ds(multiple(i * 32, 32), 32)
        pos = p * 256 + i * 32 + iota((32, 1), 0)
        live = (pos < e3).astype(F32)
        sig, total, up = t.sig[r, :], t.accb[r, :], upstream(i)
        t.b_out[r, :] = (live * (t.mid[r, :] + sig * total)).astype(BF16)
        t.fpg[r, :] = (up * total * sig * (1.0 - sig)).astype(BF16)

    t.fgg[...] = nt(t.fpg[...], feed_gate_weight())
    settle(C, ("sp", 1))
    for k in range(4):
        part = tn(t.fgin[:, 256 * k : 256 * k + 256], t.fpg[...]).astype(BF16)
        t.wfg[2 * k : 2 * k + 2] = part.reshape(2, 128, 1024)
    for j, q in enumerate((p_diag, p_sib)):
        send(fgview(q), t.fgcr.at[j], t.rss.at[4, j], t.rsr.at[4, j], sib)
    results = []

    def result(src, dst):
        copy = pltpu.make_async_copy(src, dst, t.loc.at[12 + len(results)])
        copy.start()
        results.append(copy)

    result(t.b_out, out)
    grad_x_in(FV, 2)
    sum_end(2, t.yra, t.acca)

    @pl.loop(0, 8)
    def _(i):
        r = pl.ds(multiple(i * 32, 32), 32)
        pos = p * 256 + i * 32 + iota((32, 1), 0)
        through = t.acca[r, :] * (1.0 - vector(FMIXK)) + t.fgg[r, :] * (1.0 - vector(FMIXG))
        t.moved[r, :] = through * same_at(pos)

    down_edge = remote(t.moved.at[pl.ds(0, 8)], t.moved.at[pl.ds(256, 8)], t.eds.at[0], t.edr.at[4], (s, sps[3]))

    @pl.when(p > 0)
    def _():
        down_edge.start()

    @pl.when(p == 3)
    def _():
        t.moved[256:264, :] = jnp.zeros((8, 1024), F32)

    @pl.when(p < 3)
    def _():
        remote(t.moved.at[pl.ds(256, 8)], t.moved.at[pl.ds(256, 8)], t.eds.at[0], t.edr.at[4], sib).wait_recv()

    @pl.when(p > 0)
    def _():
        down_edge.wait_send()

    grad_x_in(FV, 3)

    def norm_back(hat, scale, grad, gain):
        grad = grad * gain
        return scale * (
            grad - jnp.mean(grad, axis=1, keepdims=True) - hat * jnp.mean(grad * hat, axis=1, keepdims=True)
        )

    def add_vector(k, v):
        t.vg[k] += v[0:8] + v[8:16] + v[16:24] + v[24:32]

    @pl.loop(0, 8)
    def _(i):
        r = pl.ds(multiple(i * 32, 32), 32)
        after = pltpu.roll(t.moved[pl.ds(multiple(i * 32, 32), 40), :], 39, 0)[0:32]
        by_key, by_gate = t.acca[r, :], t.fgg[r, :]
        grad = by_key * vector(FMIXK) + by_gate * vector(FMIXG) + after
        diff = t.sec[r, :]
        hat, scale = spread_rows(t.mid[r, :])
        add_vector(FMIXK, diff * by_key)
        add_vector(FMIXG, diff * by_gate)
        add_vector(GAIN2, grad * hat)
        add_vector(BIAS2, grad)
        total = upstream(i) + norm_back(hat, scale, grad, vector(GAIN2))
        t.mid[r, :] = total
        t.xall[pl.ds(multiple(p * 256 + i * 32, 32), 32), :] = total.astype(BF16)

    agview = xview
    sp_out(4, agview)

    arrive(t.fgcr.at[0], t.rsr.at[4, 0])
    there = pl.ds(multiple(p_y * 32, 32), 32)

    @pl.loop(0, 8)
    def _(i):
        t.wfg[i, there, :] = (t.wfg[i, there, :].astype(F32) + t.fgcr[0, i].astype(F32)).astype(BF16)

    send(fgview(p_y), t.fgyr, t.rss.at[4, 2], t.rsr.at[4, 2], ydev)
    grad_x_in(FK, 1)
    grad_x_in(FV, 0)
    sp_pass(4, agview)
    sp_sib(4, agview)
    sp_diag(4, agview)

    @pl.loop(0, 4)
    def _(i):
        r = pl.ds(multiple(i * 256, 256), 256)
        grad = nt(t.xall[r, :], t.wo[...])
        gate = t.gate[r, :]
        t.hidden[r, 0:256] = (grad * gate).astype(BF16)
        t.hidden[r, 256:512] = (grad * t.mixed[r, :].astype(BF16).astype(F32) * gate * (1.0 - gate)).astype(BF16)

    settle(B)
    t.wo[...] = tn(t.gated[...], t.xall[...]).astype(BF16)
    for k in (1, 2, 3, 0):
        grad_x_out(O, zs[k])
    grad_x_in(FK, 2)

    def backward_block(k, held):
        b = 7 - k
        d_top, d_bottom, d_first, d_rate = held
        r = pl.ds(multiple(b * 128, 128), 128)
        alike, keep, memory, tail = block_parts(b)
        later = (alike & (iota((128, 128), 1) > iota((128, 128), 0))).astype(F32).astype(BF16)
        top, bottom = t.carry[b, 0:1, :], t.carry[b, 1:2, :]
        v = t.vv[r, :].astype(F32)
        weight = jnp.exp(t.kk[r, :].astype(F32))
        d_high = t.hidden[r, 0:256].astype(F32) * t.inverse[r, :]
        d_low = -d_high * t.mixed[r, :]
        shrink = t.tables[1]
        sums = exact_dot(later, jnp.concatenate([shrink * d_high, shrink * d_low], axis=1))
        scaled = t.tables[0] * weight
        own = t.small[1:2, :] * weight
        tail = tail * weight
        by_sum = scaled * (v * sums[:, :256] + sums[:, 256:])
        by_own = own * (v * d_high + d_low)
        by_tail = tail * (v * d_top + d_bottom)
        by_memory = memory * (top * d_high + bottom * d_low)
        t.vv[r, :] = (scaled * sums[:, :256] + own * d_high + tail * d_top).astype(BF16)
        t.kk[r, :] = (by_sum + by_own + by_tail).astype(BF16)
        place = iota((128, 1), 0).astype(F32)
        d_rate = d_rate + column_sum(
            place * by_sum + (place - 1.0) * by_own - by_memory - (127.0 - place) * by_tail
        )
        d_rate = d_rate - 128.0 * keep * (top * d_top + bottom * d_bottom)
        d_first = d_first + column_sum(by_own)
        d_top = keep * d_top + column_sum(memory * d_high)
        d_bottom = keep * d_bottom + column_sum(memory * d_low)
        return d_top, d_bottom, d_first, d_rate

    held = lax.fori_loop(0, 4, backward_block, (zero, zero, zero, zero))
    held = lax.fori_loop(4, 8, backward_block, held)
    t.vgc[DECAY : DECAY + 1, :] = held[3] * t.small[2:3, :]
    t.vgc[FIRST : FIRST + 1, :] = held[2]

    for k in (1, 2, 3, 0):
        q = pl.ds(multiple(zs[k] * 256, 256), 256)
        t.rgrad[q, 0:256] = tn(t.kin[:, q], t.kk[...]).astype(BF16)
        t.rgrad[q, 256:512] = tn(t.vin[:, q], t.vv[...]).astype(BF16)
        t.rgrad[q, 512:768] = tn(t.gin[:, q], t.hidden[:, 256:512]).astype(BF16)
        grad_x_out(KVG, zs[k])
    grad_x_in(FK, 3)

    t.last[...] = jnp.zeros_like(t.last)

    def rows_back(i):
        r = pl.ds(256 * i, 256)
        t.acca[...] = nt(t.kk[r, :], t.wkvg[:, 0:256])
        t.accb[...] = nt(t.vv[r, :], t.wkvg[:, 256:512])
        t.fgg[...] = nt(t.hidden[r, 256:512], t.wkvg[:, 512:768])

        @pl.loop(0, 8)
        def _(k):
            j = 7 - k
            u = pl.ds(multiple(j * 32, 32), 32)
            base = i * 256 + j * 32
            here = pl.ds(multiple(base, 32), 32)
            by_key, by_value, by_gate = t.acca[u, :], t.accb[u, :], t.fgg[u, :]
            diff = t.spread[here, :].astype(F32)
            add_vector(MIXK, diff * by_key)
            add_vector(MIXV, diff * by_value)
            add_vector(MIXG, diff * by_gate)
            current = by_key * vector(MIXK) + by_value * vector(MIXV) + by_gate * vector(MIXG)
            row = iota((32, 1), 0)
            through = (by_key + by_value + by_gate - current) * same_at(base + row)
            after = jnp.where(row == 31, t.last[0:1, :], pltpu.roll(through, 31, 0))
            t.last[0:1, :] = through[0:1, :]
            t.cgall[here, :] = (current + after).astype(BF16)

    rows_back(3)
    grad_x_in(FK, 0)
    rows_back(2)
    grad_x_in(O, 1)
    grad_x_in(O, 2)
    rows_back(1)
    grad_x_in(O, 3)
    grad_x_in(O, 0)
    rows_back(0)
    sum_begin(3, t.csb, t.crb, t.ysb, t.yrb, t.accb, lambda q: quarter(t.cgall, q).astype(F32))

    arrive(t.fgcr.at[1], t.rsr.at[4, 1])
    arrive(t.fgyr, t.rsr.at[4, 2])
    mine = pl.ds(multiple(p * 32, 32), 32)

    @pl.loop(0, 8)
    def _(i):
        total = t.wfg[i, mine, :].astype(F32) + t.fgcr[1, i].astype(F32) + t.fgyr[i].astype(F32)
        t.fgin[pl.ds(multiple(i * 32, 32), 32), :] = total.astype(BF16)

    for k in (1, 2, 3, 0):
        grad_x_out(FG, zs[k])
    grad_x_in(KVG, 1)
    grad_x_in(KVG, 2)

    def put_fv(i, r, v):
        t.moved[r, :] = v

    def put_fk(i, r, v):
        t.fkpart[i] = v.astype(BF16)

    def put_kvg(i, r, v):
        t.kvgpart[i] = v.astype(BF16)

    def put_o(i, r, v):
        t.o_out[r, :] = v

    def put_fg(i, r, v):
        t.fg_out[r, :] = v

    settle(("a2a", 1), ("a2a", 2))
    grad_z_in(FV, put_fv)
    result(t.moved.at[pl.ds(0, 128)], g_fv)
    grad_x_in(KVG, 3)
    grad_z_in(FK, put_fk)
    hand_back(0, t.fkpart, t.recfk)

    sum_end(3, t.yrb, t.accb)

    @pl.loop(0, 8)
    def _(i):
        r = pl.ds(multiple(i * 32, 32), 32)
        hat, scale = spread_rows(t.xo[r, :].astype(F32))
        grad = t.accb[r, :]
        add_vector(GAIN1, grad * hat)
        add_vector(BIAS1, grad)
        t.mid[r, :] = t.mid[r, :] + norm_back(hat, scale, grad, vector(GAIN1))

    lane = iota((16, 128), 1)
    mine_lanes = (lane >= 32 * p) & (lane < 32 * p + 32)
    for i in range(8):
        tile = t.vgc[:, 128 * (i // 4) : 128 * (i // 4) + 128]
        moved = pltpu.roll(tile, (32 * p + 128 - 32 * (i % 4)) % 128, 1)
        t.vmsg[i] = jnp.sum(t.vg[:, :, 128 * i : 128 * i + 128], axis=1) + jnp.where(mine_lanes, moved, 0.0)
    for k in range(1, 8):
        send(t.vmsg.at[sqs[k]], t.vrec.at[k], t.vss.at[0, k - 1], t.vsr.at[0, k], (sqs[k], p))
    result(t.mid, xgrad)
    for k in (1, 2, 3, 0):
        grad_x_in(FG, k)
    grad_z_in(O, put_o)
    result(t.o_out, g_o)
    total = t.vmsg[s]
    for k in range(1, 8):
        arrive(t.vrec.at[k], t.vsr.at[0, k])
        total = total + t.vrec[k]
    t.vtwo[...] = total
    for k in range(1, 4):
        send(t.vtwo, t.vrec2.at[k], t.vss.at[1, k - 1], t.vsr.at[1, k], (s, sps[k]))
    grad_z_in(FG, put_fg)
    result(t.fg_out, g_fg)
    handed_back(0, t.recfk)
    for i in range(8):
        for j in range(4):
            t.fk_out[:, 512 * i + 128 * j : 512 * i + 128 * j + 128] = t.recfk[j, :, 128 * i : 128 * i + 128].astype(F32)
    result(t.fk_out, g_fk)
    total = t.vtwo[...]
    for k in range(1, 4):
        arrive(t.vrec2.at[k], t.vsr.at[1, k])
        total = total + t.vrec2[k]
    t.v_out[...] = pltpu.roll(total, (128 - 32 * p) % 128, 1)
    result(t.v_out, g_vec)
    grad_x_in(KVG, 0)
    grad_z_in(KVG, put_kvg)
    hand_back(1, t.kvgpart, t.reckvg)
    handed_back(1, t.reckvg)
    result(t.reckvg, g_kvg)
    for _, copy, cond in pending:
        left(copy, cond)
    for copy in results:
        copy.wait()


def finish_kernel(
    a_out, a_xgrad, a_o, a_fg, a_fk, a_fv, a_kvg, a_vec,
    out, xgrad, g_o, g_fg, g_fk, g_fv, g_k, g_v, g_g, *rest,
):
    vectors, held, sems = rest[:11], rest[11:17], rest[17]
    pairs = ((a_xgrad, xgrad), (a_out, out), (a_fk, g_fk), (a_fv, g_fv), (a_o, g_o), (a_fg, g_fg))
    inward = [pltpu.make_async_copy(src, mid, sems.at[0, i]) for i, ((src, _), mid) in enumerate(zip(pairs, held))]
    outward = [pltpu.make_async_copy(mid, dst, sems.at[1, i]) for i, ((_, dst), mid) in enumerate(zip(pairs, held))]
    for copy in inward:
        copy.start()
    piece = iota((32, 128), 1) // 32
    for w, ref in enumerate((g_k, g_v, g_g)):
        for h in range(2):
            first = 256 * w + 128 * h
            tiles = [a_kvg[q, :, first : first + 128].astype(F32) for q in range(4)]
            for j in range(4):
                total = jnp.zeros((32, 128), F32)
                for q in range(4):
                    turn = 32 * (q - j) % 128
                    total = jnp.where(piece == q, pltpu.roll(tiles[q], turn, 1) if turn else tiles[q], total)
                ref[:, 512 * h + 128 * j : 512 * h + 128 * j + 128] = total
    for k, ref in enumerate(vectors):
        ref[...] = a_vec[k, 0:32]
    for first, second in zip(inward, outward):
        first.wait()
        second.start()
    for copy in outward:
        copy.wait()


def fast_body(
    incoming_signal,
    document_extents,
    adjoint_signal,
    layernorm_scaling,
    layernorm_offset,
    temporal_blend_lookup,
    temporal_blend_content,
    temporal_blend_receptor,
    temporal_shrinkage_log,
    diagonal_reward,
    lookup_projection,
    content_projection,
    receptor_projection,
    emission_projection,
    latter_scaling,
    latter_offset,
    channel_blend_lookup,
    channel_blend_receptor,
    channel_mixer_lookup,
    channel_mixer_content,
    channel_mixer_receptor,
):
    vecs = jnp.stack(
        [
            layernorm_scaling,
            layernorm_offset,
            temporal_blend_lookup,
            temporal_blend_content,
            temporal_blend_receptor,
            temporal_shrinkage_log,
            diagonal_reward,
            latter_scaling,
            latter_offset,
            channel_blend_lookup,
            channel_blend_receptor,
        ]
    )
    vecs = jnp.pad(vecs, ((0, 5), (0, 96)))
    anywhere = pl.BlockSpec(memory_space=pl.ANY)
    vmem = pl.BlockSpec(memory_space=pltpu.VMEM)
    shape = jax.ShapeDtypeStruct
    whole = (
        shape((256, 1024), BF16),
        shape((256, 1024), F32),
        shape((32, 1024), F32),
        shape((32, 1024), F32),
        shape((32, 4096), F32),
        shape((128, 1024), F32),
    )
    made = pl.pallas_call(
        step_kernel,
        out_shape=(*whole, shape((4, 32, 768), BF16), shape((16, 128), F32)),
        in_specs=[pl.BlockSpec(memory_space=pltpu.SMEM)] + [anywhere] * 10,
        out_specs=[anywhere] * 8,
        scratch_shapes=list(scratch_list().values()),
        compiler_params=pltpu.CompilerParams(
            collective_id=0, has_side_effects=True, vmem_limit_bytes=63 * 1024 * 1024
        ),
    )(
        document_extents,
        incoming_signal,
        adjoint_signal,
        vecs,
        lookup_projection,
        content_projection,
        receptor_projection,
        emission_projection,
        channel_mixer_receptor,
        channel_mixer_lookup,
        channel_mixer_content,
    )
    out, xgrad, g_o, g_fg, g_fk, g_fv, g_k, g_v, g_g, *v = pl.pallas_call(
        finish_kernel,
        out_shape=(*whole, *[shape((32, 1024), F32)] * 3, *[shape((32,), F32)] * 11),
        in_specs=[anywhere] * 6 + [vmem] * 2,
        out_specs=[anywhere] * 6 + [vmem] * 14,
        scratch_shapes=[
            *[pltpu.VMEM(whole[i].shape, whole[i].dtype) for i in (1, 0, 4, 5, 2, 3)],
            pltpu.SemaphoreType.DMA((2, 6)),
        ],
    )(*made)
    return (out, xgrad, *v[:7], g_k, g_v, g_g, g_o, *v[7:], g_fk, g_fv, g_fg)


def solution(mesh):
    fast = (mesh.shape["seq"], mesh.shape["sp"]) == (8, 4)
    flat, wide = P(("seq", "sp")), P(("seq", "sp"), None)
    return jax.shard_map(
        fast_body if fast else plain_body,
        mesh=mesh,
        in_specs=(wide, P("seq", None), wide, *[flat] * 7, *[wide] * 4, *[flat] * 4, *[wide] * 3),
        out_specs=(wide, wide, *[flat] * 7, *[wide] * 4, *[flat] * 4, *[wide] * 3),
        check_vma=False,
    )
```

```python
import functools
import types

import jax
import jax.numpy as jnp
from jax import lax
from jax.experimental import pallas as pl
from jax.experimental.pallas import tpu as pltpu
from jax.sharding import PartitionSpec as P

LOOP_LENGTH = 128


HIGHEST = lax.Precision.HIGHEST
EPSILON = 1e-05


def shifted(value, axis, steps):
    count = lax.axis_size(axis)
    first, last = (max(0, -steps), min(count, count - steps))
    return lax.ppermute(value, axis, [(source, source + steps) for source in range(first, last)])


def norm_rows(content_vectors, gain, bias):
    centered = content_vectors - jnp.mean(content_vectors, axis=1, keepdims=True)
    scale = lax.rsqrt(jnp.mean(centered * centered, axis=1, keepdims=True) + EPSILON)
    return centered * scale * gain + bias


def running(lengths_row):
    ends = [lengths_row[0]]
    for i in range(1, lengths_row.shape[0]):
        ends.append(ends[-1] + lengths_row[i])
    return ends


def segment_ids(lengths_row, positions):
    ends = jnp.stack(running(lengths_row))
    bounds = jnp.concatenate([ends - lengths_row, ends[-1:]])
    document_tags = jnp.sum((positions[:, None] >= bounds[None, :]).astype(jnp.int32), axis=1) - 1
    return (document_tags, positions < ends[-1])


def weighted_attention_loop(
    lookup_vectors,
    content_vectors,
    temporal_shrinkage_log,
    diagonal_reward,
    document_tags,
    segment_piece,
):
    count, feature_dimension = lookup_vectors.shape
    blocks = count // segment_piece
    rate = jnp.exp(temporal_shrinkage_log)
    offsets = jnp.arange(segment_piece, dtype=jnp.float32)[:, None]
    grow = jnp.exp(offsets * rate)
    shrink_multiplier = jnp.exp(-(offsets - 1.0) * rate)
    fade = jnp.exp(-offsets * rate)
    tail_fade = jnp.exp(-(segment_piece - 1.0 - offsets) * rate)
    whole_fade = jnp.exp(-1.0 * segment_piece * rate)
    order = jnp.arange(segment_piece, dtype=jnp.int32)
    lower = order[None, :] < order[:, None]
    key_blocks = lookup_vectors.reshape(blocks, segment_piece, feature_dimension)
    value_blocks = content_vectors.reshape(blocks, segment_piece, feature_dimension)
    label_blocks = document_tags.reshape(blocks, segment_piece)
    before = jnp.concatenate([jnp.full((1,), -1, jnp.int32), label_blocks[:-1, -1]])

    @jax.checkpoint
    def advance(carry, items):
        dividend_total, divisor_total = carry
        lookup_portion, content_portion, label_part, last_label = items
        weight_key = jnp.exp(lookup_portion)
        links = ((label_part[:, None] == label_part[None, :]) & lower).astype(jnp.float32)
        scaled = grow * weight_key
        cumulative_totals = jnp.dot(
            links, jnp.concatenate([scaled * content_portion, scaled], axis=1), precision=HIGHEST
        )
        recurrent_memory = (label_part == last_label).astype(jnp.float32)[:, None] * fade
        initial_reward = jnp.exp(diagonal_reward + lookup_portion)
        highest_line_entry = (
            shrink_multiplier * cumulative_totals[:, :feature_dimension]
            + recurrent_memory * dividend_total
            + initial_reward * content_portion
        )
        lowest_line_entry = (
            shrink_multiplier * cumulative_totals[:, feature_dimension:]
            + recurrent_memory * divisor_total
            + initial_reward
        )
        end_label = label_part[-1]
        keep = (end_label == last_label).astype(jnp.float32) * whole_fade
        tail = (label_part == end_label).astype(jnp.float32)[:, None] * tail_fade * weight_key
        dividend_total = keep * dividend_total + jnp.sum(tail * content_portion, axis=0)
        divisor_total = keep * divisor_total + jnp.sum(tail, axis=0)
        return ((dividend_total, divisor_total), highest_line_entry / lowest_line_entry)

    zeros = jnp.zeros((feature_dimension,), jnp.float32)
    _, blended_signal = lax.scan(
        advance, (zeros, zeros), (key_blocks, value_blocks, label_blocks, before)
    )
    return blended_signal.reshape(count, feature_dimension)


def product(left, right):
    return jnp.dot(left, right, preferred_element_type=jnp.float32)


def times_transposed(left, right):
    return lax.dot_general(
        left, right, (((1,), (1,)), ((), ())), preferred_element_type=jnp.float32
    )


def outer_sum(left, right):
    return lax.dot_general(
        left, right, (((0,), (0,)), ((), ())), preferred_element_type=jnp.float32
    )


def blend(current, prior, share):
    return current * share + prior * (1.0 - share)


def blend_back(current, prior, shares, grads):
    current_grad = jnp.zeros_like(current)
    prior_grad = jnp.zeros_like(current)
    spread = current - prior
    share_grads = []
    for share, grad in zip(shares, grads):
        current_grad = current_grad + grad * share
        prior_grad = prior_grad + grad * (1.0 - share)
        share_grads.append(jnp.sum(spread * grad, axis=0))
    return (current_grad, prior_grad, share_grads)


def plain_body(
    incoming_signal,
    document_extents,
    adjoint_signal,
    layernorm_scaling,
    layernorm_offset,
    temporal_blend_lookup,
    temporal_blend_content,
    temporal_blend_receptor,
    temporal_shrinkage_log,
    diagonal_reward,
    lookup_projection,
    content_projection,
    receptor_projection,
    emission_projection,
    latter_scaling,
    latter_offset,
    channel_blend_lookup,
    channel_blend_receptor,
    channel_mixer_lookup,
    channel_mixer_content,
    channel_mixer_receptor,
):
    rows = incoming_signal.shape[0]
    feature_dimension = incoming_signal.shape[1]
    parts = lax.axis_size("sp")
    place = lax.axis_index("sp")
    group_rows = rows * parts
    channels = feature_dimension // parts
    lengths_row = document_extents[0]
    positions = place * rows + jnp.arange(rows, dtype=jnp.int32)
    document_tags, live = segment_ids(lengths_row, positions)
    earlier, _ = segment_ids(lengths_row, positions - 1)
    same = (document_tags == earlier).astype(jnp.float32)[:, None]
    live_rows = live.astype(jnp.float32)[:, None]
    group_labels, _ = segment_ids(lengths_row, jnp.arange(group_rows, dtype=jnp.int32))
    fetched = [
        lax.all_gather(piece, ("seq", "sp"), axis=0, tiled=True)
        for piece in (
            layernorm_scaling,
            layernorm_offset,
            temporal_blend_lookup,
            temporal_blend_content,
            temporal_blend_receptor,
            temporal_shrinkage_log,
            diagonal_reward,
            lookup_projection,
            content_projection,
            receptor_projection,
            emission_projection,
            latter_scaling,
            latter_offset,
            channel_blend_lookup,
            channel_blend_receptor,
            channel_mixer_lookup,
            channel_mixer_content,
            channel_mixer_receptor,
        )
    ]
    vectors = [fetched[i].astype(jnp.float32) for i in (0, 1, 2, 3, 4, 5, 6, 11, 12, 13, 14)]
    gain_one, bias_one, share_key, share_value, share_gate, decay_all, first_all = vectors[:7]
    gain_two, bias_two, feed_share_key, feed_share_gate = vectors[7:]
    key_matrix, value_matrix, gate_matrix, output_matrix = (
        fetched[7],
        fetched[8],
        fetched[9],
        fetched[10],
    )
    feed_key_matrix, feed_value_matrix, feed_gate_matrix = (fetched[15], fetched[16], fetched[17])
    source = incoming_signal.astype(jnp.float32)
    normed, norm_pull = jax.vjp(norm_rows, source, gain_one, bias_one)
    edge = shifted(normed[-1:], "sp", 1)
    prior = jnp.concatenate([edge, normed[:-1]], axis=0) * same
    key_in = blend(normed, prior, share_key).astype(jnp.bfloat16)
    value_in = blend(normed, prior, share_value).astype(jnp.bfloat16)
    gate_in = blend(normed, prior, share_gate).astype(jnp.bfloat16)
    lookup_vectors = product(key_in, key_matrix).astype(jnp.bfloat16)
    content_vectors = product(value_in, value_matrix).astype(jnp.bfloat16)
    gate = jax.nn.sigmoid(product(gate_in, gate_matrix))
    arrived = lax.all_to_all(
        jnp.stack([lookup_vectors, content_vectors]), "sp", split_axis=2, concat_axis=1, tiled=True
    )
    decay_part = lax.dynamic_slice_in_dim(decay_all, place * channels, channels)
    first_part = lax.dynamic_slice_in_dim(first_all, place * channels, channels)

    def recurrence(key_full, value_full, decay_here, first_here):
        return weighted_attention_loop(
            key_full, value_full, decay_here, first_here, group_labels, LOOP_LENGTH
        )

    blended_signal, scan_pull = jax.vjp(
        recurrence,
        arrived[0].astype(jnp.float32),
        arrived[1].astype(jnp.float32),
        decay_part,
        first_part,
    )
    mixed_rows = lax.all_to_all(
        blended_signal.astype(jnp.bfloat16), "sp", split_axis=0, concat_axis=1, tiled=True
    ).astype(jnp.float32)
    gated = (gate * mixed_rows).astype(jnp.bfloat16)
    middle = source + product(gated, output_matrix)
    second, second_pull = jax.vjp(norm_rows, middle, gain_two, bias_two)
    second_edge = shifted(second[-1:], "sp", 1)
    prior_second = jnp.concatenate([second_edge, second[:-1]], axis=0) * same
    feed_key_in = blend(second, prior_second, feed_share_key).astype(jnp.bfloat16)
    feed_gate_in = blend(second, prior_second, feed_share_gate).astype(jnp.bfloat16)
    raised = product(feed_key_in, feed_key_matrix)
    hidden = jnp.square(jax.nn.relu(raised)).astype(jnp.bfloat16)
    recurrent_memory = product(hidden, feed_value_matrix)
    feed_sig = jax.nn.sigmoid(product(feed_gate_in, feed_gate_matrix))
    block_out = (live_rows * (middle + feed_sig * recurrent_memory)).astype(jnp.bfloat16)
    upstream = adjoint_signal.astype(jnp.float32) * live_rows
    carried_grad = (upstream * feed_sig).astype(jnp.bfloat16)
    feed_pre_grad = (upstream * recurrent_memory * feed_sig * (1.0 - feed_sig)).astype(jnp.bfloat16)
    grad_feed_value = outer_sum(hidden, carried_grad)
    grad_feed_gate = outer_sum(feed_gate_in, feed_pre_grad)
    raised_grad = (
        times_transposed(carried_grad, feed_value_matrix) * 2.0 * jax.nn.relu(raised)
    ).astype(jnp.bfloat16)
    grad_feed_key = outer_sum(feed_key_in, raised_grad)
    second_grad, second_prior_grad, feed_share_grads = blend_back(
        second,
        prior_second,
        (feed_share_key, feed_share_gate),
        (
            times_transposed(raised_grad, feed_key_matrix),
            times_transposed(feed_pre_grad, feed_gate_matrix),
        ),
    )
    moved = second_prior_grad * same
    incoming = shifted(moved[:1], "sp", -1)
    second_grad = second_grad + jnp.concatenate([moved[1:], incoming], axis=0)
    middle_norm_grad, grad_second_gain, grad_second_bias = second_pull(second_grad)
    middle_grad = upstream + middle_norm_grad
    attended_grad = middle_grad.astype(jnp.bfloat16)
    grad_output_weight = outer_sum(gated, attended_grad)
    gated_grad = times_transposed(attended_grad, output_matrix)
    mixed_grad = (gated_grad * gate).astype(jnp.bfloat16)
    gate_pre_grad = (gated_grad * mixed_rows * gate * (1.0 - gate)).astype(jnp.bfloat16)
    channel_grad = lax.all_to_all(mixed_grad, "sp", split_axis=1, concat_axis=0, tiled=True)
    key_grad_here, value_grad_here, decay_grad_here, first_grad_here = scan_pull(
        channel_grad.astype(jnp.float32)
    )
    returned = lax.all_to_all(
        jnp.stack([key_grad_here, value_grad_here]).astype(jnp.bfloat16),
        "sp",
        split_axis=1,
        concat_axis=2,
        tiled=True,
    )
    key_grad = returned[0]
    value_grad = returned[1]
    grad_key_weight = outer_sum(key_in, key_grad)
    grad_value_weight = outer_sum(value_in, value_grad)
    grad_gate_weight = outer_sum(gate_in, gate_pre_grad)
    normed_grad, normed_prior_grad, share_grads = blend_back(
        normed,
        prior,
        (share_key, share_value, share_gate),
        (
            times_transposed(key_grad, key_matrix),
            times_transposed(value_grad, value_matrix),
            times_transposed(gate_pre_grad, gate_matrix),
        ),
    )
    moved_first = normed_prior_grad * same
    incoming_first = shifted(moved_first[:1], "sp", -1)
    normed_grad = normed_grad + jnp.concatenate([moved_first[1:], incoming_first], axis=0)
    source_norm_grad, grad_norm_gain, grad_norm_bias = norm_pull(normed_grad)
    input_grad = middle_grad + source_norm_grad
    decay_grad = lax.dynamic_update_slice_in_dim(
        jnp.zeros((feature_dimension,), jnp.float32), decay_grad_here, place * channels, 0
    )
    first_grad = lax.dynamic_update_slice_in_dim(
        jnp.zeros((feature_dimension,), jnp.float32), first_grad_here, place * channels, 0
    )
    grads = (
        grad_norm_gain,
        grad_norm_bias,
        *share_grads,
        decay_grad,
        first_grad,
        grad_key_weight,
        grad_value_weight,
        grad_gate_weight,
        grad_output_weight,
        grad_second_gain,
        grad_second_bias,
        *feed_share_grads,
        grad_feed_key,
        grad_feed_value,
        grad_feed_gate,
    )
    shares = []
    for grad in grads:
        for axis in ("seq", "sp"):
            grad = lax.psum_scatter(
                grad.astype(jnp.bfloat16), axis, scatter_dimension=0, tiled=True
            ).astype(jnp.float32)
        shares.append(grad)
    return (block_out, input_grad, *shares)


MESH = pl.DeviceIdType.MESH
F32 = jnp.float32
BF16 = jnp.bfloat16
GAIN1, BIAS1, MIXK, MIXV, MIXG, DECAY, FIRST, GAIN2, BIAS2, FMIXK, FMIXG = range(11)


def multiple(value, step):
    return pl.multiple_of(value, step)


def nn(a, b):
    return jnp.dot(a, b, preferred_element_type=F32)


def nt(a, b):
    return lax.dot_general(a, b, (((1,), (1,)), ((), ())), preferred_element_type=F32)


def tn(a, b):
    return lax.dot_general(a, b, (((0,), (0,)), ((), ())), preferred_element_type=F32)


def exact_dot(links, right):
    high = right.astype(BF16)
    rest = right - high.astype(F32)
    middle = rest.astype(BF16)
    low = (rest - middle.astype(F32)).astype(BF16)
    return nn(links, high) + nn(links, middle) + nn(links, low)


def iota(shape, axis):
    return lax.broadcasted_iota(jnp.int32, shape, axis)


def spread_rows(v):
    centered = v - jnp.mean(v, axis=1, keepdims=True)
    scale = lax.rsqrt(jnp.mean(centered * centered, axis=1, keepdims=True) + EPSILON)
    return centered * scale, scale


def column_sum(v):
    return jnp.sum(v, axis=0, keepdims=True)


def scratch_list():
    vm = pltpu.VMEM
    sem = pltpu.SemaphoreType.DMA
    return dict(
        xall=vm((1024, 1024), BF16),
        kin=vm((1024, 1024), BF16),
        vin=vm((1024, 1024), BF16),
        gin=vm((1024, 1024), BF16),
        spread=vm((1024, 1024), BF16),
        wkvg=vm((1024, 768), BF16),
        wo=vm((256, 1024), BF16),
        wfg=vm((8, 128, 1024), BF16),
        wfk=vm((1024, 1024), BF16),
        wfv=vm((1024, 1024), BF16),
        kk=vm((1024, 256), BF16),
        vv=vm((1024, 256), BF16),
        gate=vm((1024, 256), F32),
        mixed=vm((1024, 256), F32),
        inverse=vm((1024, 256), F32),
        gated=vm((1024, 256), BF16),
        carry=vm((8, 8, 256), F32),
        tables=vm((4, 128, 256), F32),
        small=vm((8, 256), F32),
        last=vm((8, 1024), F32),
        xo=vm((256, 1024), BF16),
        adj=vm((256, 1024), BF16),
        mid=vm((256, 1024), F32),
        sec=vm((256, 1024), F32),
        edge=vm((4, 16, 1024), BF16),
        sig=vm((256, 1024), F32),
        fgin=vm((256, 1024), BF16),
        fpg=vm((256, 1024), BF16),
        fkall=vm((1024, 1024), BF16),
        cgall=vm((1024, 1024), BF16),
        hidden=vm((1024, 1024), BF16),
        gfv=vm((1024, 1024), BF16),
        rgrad=vm((1024, 1024), BF16),
        acca=vm((256, 1024), F32),
        accb=vm((256, 1024), F32),
        fgg=vm((256, 1024), F32),
        moved=vm((264, 1024), F32),
        csa=vm((2, 256, 1024), BF16),
        cra=vm((2, 256, 1024), BF16),
        ysa=vm((256, 1024), BF16),
        yra=vm((256, 1024), BF16),
        csb=vm((2, 256, 1024), BF16),
        crb=vm((2, 256, 1024), BF16),
        ysb=vm((256, 1024), BF16),
        yrb=vm((256, 1024), BF16),
        fgcr=vm((2, 8, 32, 1024), BF16),
        fgyr=vm((8, 32, 1024), BF16),
        xrfv=vm((4, 128, 1024), BF16),
        xrfk=vm((4, 128, 1024), BF16),
        xrfg=vm((4, 32, 1024), BF16),
        xro=vm((4, 32, 1024), BF16),
        xrkv=vm((4, 128, 512), BF16),
        xrg=vm((4, 128, 256), BF16),
        zrfv=vm((3, 128, 1024), BF16),
        zrfk=vm((3, 128, 1024), BF16),
        zrfg=vm((3, 32, 1024), BF16),
        zro=vm((3, 32, 1024), BF16),
        zrkv=vm((3, 128, 512), BF16),
        zrg=vm((3, 128, 256), BF16),
        kvgraw=vm((3, 32, 1024), BF16),
        fkraw=vm((32, 4096), BF16),
        kvgpart=vm((4, 32, 768), BF16),
        fkpart=vm((4, 32, 1024), BF16),
        o_out=vm((32, 1024), F32),
        fg_out=vm((32, 1024), F32),
        mrfv=vm((128, 1024), BF16),
        mrfk=vm((128, 1024), BF16),
        mrfg=vm((32, 1024), BF16),
        mro=vm((32, 1024), BF16),
        mrkv=vm((128, 512), BF16),
        mrg=vm((128, 256), BF16),
        b_out=vm((256, 1024), BF16),
        v_out=vm((16, 128), F32),
        recfk=vm((4, 32, 1024), BF16),
        reckvg=vm((4, 32, 768), BF16),
        vraw=vm((8, 4, 16, 128), BF16),
        nat=vm((16, 1024), F32),
        chan=vm((16, 256), F32),
        vg=vm((16, 8, 1024), F32),
        vgc=vm((16, 256), F32),
        vmsg=vm((8, 16, 128), F32),
        vrec=vm((8, 16, 128), F32),
        vtwo=vm((16, 128), F32),
        vrec2=vm((4, 16, 128), F32),
        ags=sem((7, 9)),
        agr=sem((7, 8)),
        a2s=sem((3, 3)),
        a2r=sem((3, 4)),
        sps=sem((6, 3)),
        spr=sem((6, 3)),
        rss=sem((5, 3)),
        rsr=sem((5, 3)),
        qxs=sem((6, 4)),
        qxr=sem((6, 4)),
        qzs=sem((6, 3)),
        qzr=sem((6, 3)),
        qmr=sem((6,)),
        fas=sem((2, 3)),
        far=sem((2, 4)),
        vss=sem((2, 7)),
        vsr=sem((2, 8)),
        eds=sem((4,)),
        edr=sem((5,)),
        loc=sem((24,)),
    )


def step_kernel(
    lengths, xin, adjoint, vecs, k_in, v_in, g_in, o_in, fg_in, fk_in, fv_in,
    out, xgrad, g_o, g_fg, g_fk, g_fv, g_kvg, g_vec,
    *scratch,
):
    t = types.SimpleNamespace(**dict(zip(scratch_list(), scratch)))
    s, p = lax.axis_index("seq"), lax.axis_index("sp")
    z, x, y, c = s // 2, s % 2, p // 2, p % 2
    zs = [(z + k) % 4 for k in range(4)]
    xdev = (z * 2 + 1 - x, p)
    ydev, sib = (s, (1 - y) * 2 + c), (s, y * 2 + 1 - c)
    sps = [(p + k) % 4 for k in range(4)]
    sqs = [(s + k) % 8 for k in range(8)]
    p_sib, p_y, p_diag = y * 2 + 1 - c, (1 - y) * 2 + c, (1 - y) * 2 + 1 - c

    pending = []

    def remote(src, dst, send_sem, recv_sem, device):
        return pltpu.make_async_remote_copy(
            src_ref=src, dst_ref=dst, send_sem=send_sem, recv_sem=recv_sem,
            device_id=device, device_id_type=MESH,
        )

    def send(src, dst, send_sem, recv_sem, device, tag=None):
        copy = remote(src, dst, send_sem, recv_sem, device)
        copy.start()
        pending.append((tag, copy, None))
        return copy

    def left(copy, cond):
        if cond is None:
            copy.wait_send()
        else:
            pl.when(cond)(copy.wait_send)

    def settle(*tags):
        for tag, copy, cond in pending:
            if tag in tags:
                left(copy, cond)
        pending[:] = [entry for entry in pending if entry[0] not in tags]

    def arrive(dst, recv_sem):
        remote(dst, dst, recv_sem, recv_sem, sib).wait_recv()

    def local(src, dst, k):
        copy = pltpu.make_async_copy(src, dst, t.loc.at[k])
        copy.start()
        return copy

    loads = []

    def load(src, dst):
        copy = pltpu.make_async_copy(src, dst, t.loc.at[len(loads)])
        copy.start()
        loads.append(copy)

    def own_rows(ref, size):
        return ref.at[pl.ds(multiple(s * size, size), size)]

    load(k_in, t.kvgraw.at[0])
    load(v_in, t.kvgraw.at[1])
    load(g_in, t.kvgraw.at[2])
    load(vecs, t.vraw.at[s, p])
    load(fk_in, t.fkraw)
    early = len(loads)
    load(xin, t.xall.at[pl.ds(multiple(p * 256, 256), 256)])
    load(o_in, own_rows(t.wo, 32))
    load(fg_in, t.wfg.at[s, pl.ds(multiple(p * 32, 32), 32)])
    load(fv_in, own_rows(t.wfv, 128))
    load(xin, t.xo)
    load(adjoint, t.adj)
    load(adjoint, t.rgrad.at[pl.ds(multiple(p * 256, 256), 256)])
    for copy in loads[:4]:
        copy.wait()
    piece = iota((32, 128), 1) // 32
    for w in range(3):
        for h in range(2):
            tiles = [t.kvgraw[w, :, 512 * h + 128 * j : 512 * h + 128 * j + 128].astype(F32) for j in range(4)]
            for q in range(4):
                total = jnp.zeros((32, 128), F32)
                for j in range(4):
                    turn = 32 * (j - q) % 128
                    total = jnp.where(piece == j, pltpu.roll(tiles[j], turn, 1) if turn else tiles[j], total)
                t.kvgpart[q, :, 256 * w + 128 * h : 256 * w + 128 * h + 128] = total.astype(BF16)
    loads[4].wait()
    for i in range(8):
        for q in range(4):
            t.fkpart[q, :, 128 * i : 128 * i + 128] = t.fkraw[:, 512 * i + 128 * q : 512 * i + 128 * q + 128]

    barrier = pltpu.get_barrier_semaphore()
    for k in range(1, 8):
        pl.semaphore_signal(barrier, inc=1, device_id=(sqs[k], p), device_id_type=MESH)
    for k in range(1, 4):
        pl.semaphore_signal(barrier, inc=1, device_id=(s, sps[k]), device_id_type=MESH)
    pl.semaphore_wait(barrier, 10)

    def rows(ref, size):
        return lambda i: ref.at[pl.ds(multiple(i * size, size), size)]

    V, A, B, C, D, E, H = range(7)
    block = {
        V: lambda i: t.vraw.at[i],
        A: rows(t.wkvg, 128),
        B: rows(t.wo, 32),
        C: lambda i: t.wfg.at[i, pl.ds(multiple(p * 32, 32), 32)],
        D: rows(t.wfk, 128),
        E: lambda i: t.wfv.at[pl.ds(multiple(i * 128, 64), 64)],
        H: lambda i: t.wfv.at[pl.ds(multiple(i * 128 + 64, 64), 64)],
    }

    inner = (z == 1) | (z == 2)
    far = (z + 2) % 4
    beside = 1 + z % 2
    outer = 3 * (z // 2)

    def pick(*values):
        return sum((z == i).astype(jnp.int32) * v for i, v in enumerate(values))

    sources = (pick(1, 3, 0, 2), pick(2, 0, 3, 1), pick(3, 2, 1, 0))

    def send_if(cond, src, dst, send_sem, recv_sem, device, tag=None):
        copy = remote(src, dst, send_sem, recv_sem, device)
        pl.when(cond)(copy.start)
        pending.append((tag, copy, cond))

    def along_z(item, i, src, first):
        there = block[item](i)
        send(src, there, t.ags.at[item, first], t.agr.at[item, i], (far * 2 + x, p), item)
        send(src, there, t.ags.at[item, first + 1], t.agr.at[item, i], (beside * 2 + x, p), item)
        send_if(inner, src, there, t.ags.at[item, first + 2], t.agr.at[item, i], (outer * 2 + x, p), item)

    def hand_on(item, i, sem):
        send_if(inner, block[item](i), block[item](i), t.ags.at[item, sem], t.agr.at[item, i], (outer * 2 + x, p), item)

    def x_out(item, src):
        send(src, block[item](s), t.ags.at[item, 0], t.agr.at[item, s], xdev, item)

    def z_out(item, src):
        if item == V:
            for k in range(1, 4):
                send(src, block[V](s), t.ags.at[V, k], t.agr.at[V, s], (zs[k] * 2 + x, p), V)
        else:
            along_z(item, s, src, 1)

    def pass_on(item, j):
        i = sources[j] * 2 + x
        arrive(block[item](i), t.agr.at[item, i])
        send(block[item](i), block[item](i), t.ags.at[item, 4 + j], t.agr.at[item, i], xdev, item)
        if j == 0 and item != V:
            hand_on(item, i, 7)

    def all_in(item):
        for k in range(4):
            i = zs[k] * 2 + 1 - x
            arrive(block[item](i), t.agr.at[item, i])

    def neighbour_in(item):
        i = z * 2 + 1 - x
        arrive(block[item](i), t.agr.at[item, i])
        along_z(item, i, block[item](i), 4)

    def pass_outwards(item):
        for xx, sem in ((x, 7), (1 - x, 8)):
            i = sources[0] * 2 + xx
            arrive(block[item](i), t.agr.at[item, i])
            hand_on(item, i, sem)

    def rest_in(item):
        for j in (1, 2):
            for xx in (x, 1 - x):
                i = sources[j] * 2 + xx
                arrive(block[item](i), t.agr.at[item, i])

    def sp_out(n, view):
        send(view(p), view(p), t.sps.at[n, 0], t.spr.at[n, 0], ydev, ("sp", n))
        send(view(p), view(p), t.sps.at[n, 1], t.spr.at[n, 1], sib, ("sp", n))

    def sp_pass(n, view):
        arrive(view(p_y), t.spr.at[n, 0])
        send(view(p_y), view(p_y), t.sps.at[n, 2], t.spr.at[n, 2], sib, ("sp", 3 if n == 5 else n))

    def sp_sib(n, view):
        arrive(view(p_sib), t.spr.at[n, 1])

    def sp_diag(n, view):
        arrive(view(p_diag), t.spr.at[n, 2])

    def add_rows(n, fn):
        @pl.loop(0, n // 32)
        def _(i):
            fn(pl.ds(multiple(i * 32, 32), 32))

    def sum_begin(n, cs, cr, ys, yr, acc, compute):
        def to_sibling(j, q):
            cs[j] = compute(q).astype(BF16)
            send(cs.at[j], cr.at[j], t.rss.at[n, j], t.rsr.at[n, j], sib, ("sum", n))

        def to_other(r):
            ys[r, :] = (acc[r, :] + cr[0, r, :].astype(F32)).astype(BF16)

        def to_own(r):
            acc[r, :] += cr[1, r, :].astype(F32)

        to_sibling(0, p_diag)
        acc[...] = compute(p_y)
        arrive(cr.at[0], t.rsr.at[n, 0])
        add_rows(256, to_other)
        send(ys, yr, t.rss.at[n, 2], t.rsr.at[n, 2], ydev, ("sum", n))
        to_sibling(1, p_sib)
        acc[...] = compute(p)
        arrive(cr.at[1], t.rsr.at[n, 1])
        add_rows(256, to_own)

    def sum_end(n, yr, acc):
        arrive(yr, t.rsr.at[n, 2])

        def add(r):
            acc[r, :] += yr[r, :].astype(F32)

        add_rows(256, add)
        settle(("sum", n))

    FV, FK, FG, O, KV, G = range(6)
    grads = {
        FV: (t.gfv, t.xrfv, t.zrfv, t.mrfv, 128),
        FK: (t.wfk, t.xrfk, t.zrfk, t.mrfk, 128),
        FG: (t.fgin, t.xrfg, t.zrfg, t.mrfg, 32),
        O: (t.wo, t.xro, t.zro, t.mro, 32),
        KV: (t.rgrad.at[:, pl.ds(0, 512)], t.xrkv, t.zrkv, t.mrkv, 128),
        G: (t.rgrad.at[:, pl.ds(512, 256)], t.xrg, t.zrg, t.mrg, 128),
    }
    dests = (z, pick(3, 0, 3, 0), pick(2, 2, 1, 1), pick(1, 3, 0, 2))

    def piece_of(item, i):
        ref, xr, _, _, size = grads[item]
        return ref.at[pl.ds(multiple(i * size, size), size), pl.ds(0, xr.shape[2])]

    def grad_x_out(item, zz):
        xr = grads[item][1]
        send(piece_of(item, zz * 2 + 1 - x), xr.at[zz], t.qxs.at[item, zz], t.qxr.at[item, zz], xdev)

    def grad_x_in(item, j):
        ref, xr, zr, mr, size = grads[item]
        zz = dests[j]
        arrive(xr.at[zz], t.qxr.at[item, zz])
        if j == 0:
            return
        base = (zz * 2 + x) * size
        w = pl.ds(0, xr.shape[2])

        def add(r):
            here = pl.ds(multiple(base + r.start, 32), 32)
            ref[here, w] = (ref[here, w].astype(F32) + xr[zz, r, :].astype(F32)).astype(BF16)

        def add_both(r):
            here = pl.ds(multiple(base + r.start, 32), 32)
            total = ref[here, w].astype(F32) + xr[zz, r, :].astype(F32)
            ref[here, w] = (total + mr[r, :].astype(F32)).astype(BF16)

        if j == 3:

            @pl.when(inner)
            def _():
                arrive(mr, t.qmr.at[item])
                add_rows(size, add_both)

            @pl.when(jnp.logical_not(inner))
            def _():
                add_rows(size, add)
        else:
            add_rows(size, add)
        piece, slot = piece_of(item, zz * 2 + x), (z - zz + 3) % 4
        straight = (zr.at[slot], t.qzs.at[item, j - 1], t.qzr.at[item, slot], (zz * 2 + x, p))
        if j == 1:
            send_if(inner, piece, *straight)
            send_if(jnp.logical_not(inner), piece, mr, t.qzs.at[item, 0], t.qmr.at[item], (beside * 2 + x, p))
        else:
            send(piece, *straight)

    def grad_z_in(item, put):
        ref, xr, zr, _, size = grads[item]
        for slot in range(3):
            both = (z + slot + 1) % 4 == 3 - z
            opposite = jnp.logical_and(both, jnp.logical_not(inner))

            @pl.when(jnp.logical_not(opposite))
            def _():
                arrive(zr.at[slot], t.qzr.at[item, slot])

            @pl.when(opposite)
            def _():
                zr[slot] = jnp.zeros(zr.shape[1:], BF16)

        @pl.loop(0, size // 32)
        def _(i):
            r = pl.ds(multiple(i * 32, 32), 32)
            here = pl.ds(multiple(s * size + i * 32, 32), 32)
            total = ref[here, pl.ds(0, xr.shape[2])].astype(F32) + xr[z, r, :].astype(F32)
            total = total + zr[0, r, :].astype(F32) + zr[1, r, :].astype(F32) + zr[2, r, :].astype(F32)
            put(i, r, total)

    def hand_back(n, fin, rec):
        for k in range(1, 4):
            send(fin.at[sps[k]], rec.at[p], t.fas.at[n, k - 1], t.far.at[n, p], (s, sps[k]))
        rec[p] = fin[p]

    def handed_back(n, rec):
        for k in range(1, 4):
            arrive(rec.at[sps[k]], t.far.at[n, sps[k]])

    e0 = lengths[0, 0]
    e1 = e0 + lengths[0, 1]
    e2 = e1 + lengths[0, 2]
    e3 = e2 + lengths[0, 3]

    def label(pos):
        total = (pos >= 0).astype(jnp.int32)
        for edge in (e0, e1, e2, e3):
            total = total + (pos >= edge).astype(jnp.int32)
        return total - 1

    def same_at(pos):
        return (label(pos) == label(pos - 1)).astype(F32)

    xview = rows(t.xall, 256)

    def a2a_out(n, src, dst):
        for k in (2, 1, 3):
            send(src(sps[k]), dst(p), t.a2s.at[n, k - 1], t.a2r.at[n, p], (s, sps[k]), ("a2a", n))

    def a2a_in(n, dst):
        for k in range(1, 4):
            arrive(dst(sps[k]), t.a2r.at[n, sps[k]])

    vec_dst = lambda i: t.vraw.at[s, i]
    kvg_dst = lambda i: t.wkvg.at[pl.ds(multiple(s * 128 + i * 32, 32), 32)]
    fk_dst = lambda i: t.wfk.at[pl.ds(multiple(s * 128 + i * 32, 32), 32)]
    a2a_out(0, lambda i: vecs, vec_dst)
    a2a_out(1, lambda i: t.kvgpart.at[i], kvg_dst)
    a2a_out(2, lambda i: t.fkpart.at[i], fk_dst)
    send(xin, xview(p), t.sps.at[0, 0], t.spr.at[0, 0], ydev)
    send(xin, xview(p), t.sps.at[0, 1], t.spr.at[0, 1], sib)
    adjviews = [lambda i, h=h: t.rgrad.at[pl.ds(multiple(i * 256 + 128 * h, 128), 128)] for h in range(2)]

    def adjoint_out(h):
        piece = adjoint.at[pl.ds(128 * h, 128)]
        send(piece, adjviews[h](p), t.sps.at[3 + 2 * h, 0], t.spr.at[3 + 2 * h, 0], ydev, ("sp", 3))
        send(piece, adjviews[h](p), t.sps.at[3 + 2 * h, 1], t.spr.at[3 + 2 * h, 1], sib, ("sp", 3))

    t.wkvg[pl.ds(multiple(s * 128 + p * 32, 32), 32), :] = t.kvgpart[p]
    t.wfk[pl.ds(multiple(s * 128 + p * 32, 32), 32), :] = t.fkpart[p]
    a2a_in(0, vec_dst)
    x_out(V, t.vraw.at[s])
    z_out(V, t.vraw.at[s])
    x_out(C, fg_in)
    z_out(C, fg_in)
    a2a_in(1, kvg_dst)
    z_out(A, block[A](s))
    for j in range(3):
        pass_on(V, j)
    x_out(A, block[A](s))
    for copy in loads[early:]:
        copy.wait()
    a2a_in(2, fk_dst)
    pass_on(C, 0)
    pass_on(C, 1)
    z_out(B, o_in)
    all_in(V)

    t.last[...] = jnp.zeros_like(t.last)
    t.vg[...] = jnp.zeros_like(t.vg)
    t.vgc[...] = jnp.zeros_like(t.vgc)
    for i in range(8):
        total = t.vraw[i, 0].astype(F32)
        for j in range(1, 4):
            total = total + pltpu.roll(t.vraw[i, j].astype(F32), 32 * j, 1)
        t.nat[:, 128 * i : 128 * i + 128] = total
    for i in range(2):
        total = t.vraw[4 * i, p].astype(F32)
        for j in range(1, 4):
            total = total + pltpu.roll(t.vraw[4 * i + j, p].astype(F32), 32 * j, 1)
        t.chan[:, 128 * i : 128 * i + 128] = total

    def vector(k):
        return t.nat[k : k + 1, :]

    rate = jnp.exp(t.chan[DECAY : DECAY + 1, :])
    offset = iota((128, 1), 0).astype(F32)
    t.tables[0] = jnp.exp(offset * rate)
    t.tables[1] = jnp.exp(-(offset - 1.0) * rate)
    t.tables[2] = jnp.exp(-offset * rate)
    t.tables[3] = jnp.exp(-(127.0 - offset) * rate)
    t.small[0:1, :] = jnp.exp(-128.0 * rate)
    t.small[1:2, :] = jnp.exp(t.chan[FIRST : FIRST + 1, :])
    t.small[2:3, :] = rate

    pass_on(A, 0)
    pass_on(C, 2)
    pass_on(A, 1)
    x_out(B, o_in)
    sp_pass(0, xview)
    all_in(C)
    fgview = lambda i: t.wfg.at[:, pl.ds(multiple(i * 32, 32), 32)]
    sp_out(1, fgview)
    adjoint_out(0)
    adjoint_out(1)
    sp_sib(0, xview)
    sp_diag(0, xview)

    def norm_quarter(q):
        @pl.loop(0, 8)
        def _(i):
            base = q * 256 + i * 32
            r = pl.ds(multiple(base, 32), 32)
            hat, _ = spread_rows(t.xall[r, :].astype(F32))
            normed = hat * vector(GAIN1) + vector(BIAS1)
            row = iota((32, 1), 0)
            prior = jnp.where(row == 0, t.last[0:1, :], pltpu.roll(normed, 1, 0))
            prior = prior * same_at(base + row)
            t.last[0:1, :] = normed[31:32, :]
            diff = normed - prior
            t.spread[r, :] = diff.astype(BF16)
            t.kin[r, :] = (prior + diff * vector(MIXK)).astype(BF16)
            t.vin[r, :] = (prior + diff * vector(MIXV)).astype(BF16)
            t.gin[r, :] = (prior + diff * vector(MIXG)).astype(BF16)

    norm_quarter(0)
    pass_on(A, 2)
    pass_on(B, 0)
    norm_quarter(1)
    z_out(D, block[D](s))
    norm_quarter(2)
    norm_quarter(3)
    pass_on(B, 1)
    x_out(D, block[D](s))
    all_in(A)
    settle(("sp", 0))

    @pl.loop(0, 4)
    def _(i):
        r = pl.ds(multiple(i * 256, 256), 256)
        t.kk[r, :] = nn(t.kin[r, :], t.wkvg[:, 0:256]).astype(BF16)
        t.vv[r, :] = nn(t.vin[r, :], t.wkvg[:, 256:512]).astype(BF16)
        t.gate[r, :] = jax.nn.sigmoid(nn(t.gin[r, :], t.wkvg[:, 512:768]))

    def block_parts(b):
        base = b * 128
        column = label(base + iota((128, 1), 0))
        row = label(base + iota((1, 128), 1))
        before, end = label(base - 1), label(base + 127)
        alike = column == row
        keep = (before == end).astype(F32) * t.small[0:1, :]
        memory = (column == before).astype(F32) * t.tables[2]
        tail = (column == end).astype(F32) * t.tables[3]
        return alike, keep, memory, tail

    def forward_block(b, held):
        top, bottom = held
        r = pl.ds(multiple(b * 128, 128), 128)
        alike, keep, memory, tail = block_parts(b)
        links = (alike & (iota((128, 128), 1) < iota((128, 128), 0))).astype(F32).astype(BF16)
        v = t.vv[r, :].astype(F32)
        weight = jnp.exp(t.kk[r, :].astype(F32))
        scaled = t.tables[0] * weight
        sums = exact_dot(links, jnp.concatenate([scaled * v, scaled], axis=1))
        own = t.small[1:2, :] * weight
        high = t.tables[1] * sums[:, :256] + memory * top + own * v
        low = t.tables[1] * sums[:, 256:] + memory * bottom + own
        inverse = 1.0 / low
        mixed = high * inverse
        t.inverse[r, :] = inverse
        t.mixed[r, :] = mixed
        t.gated[r, :] = (t.gate[r, :] * mixed.astype(BF16).astype(F32)).astype(BF16)
        t.carry[b, 0:1, :] = top
        t.carry[b, 1:2, :] = bottom
        tail = tail * weight
        return keep * top + column_sum(tail * v), keep * bottom + column_sum(tail)

    zero = jnp.zeros((1, 256), F32)
    held = lax.fori_loop(0, 4, forward_block, (zero, zero))
    pass_on(B, 2)
    z_out(E, fv_in.at[pl.ds(0, 64)])
    x_out(H, fv_in.at[pl.ds(64, 64)])
    held = lax.fori_loop(4, 8, forward_block, held)

    pass_on(D, 0)
    sp_pass(1, fgview)
    sp_sib(1, fgview)
    all_in(B)

    def quarter(ref, q):
        return ref[pl.ds(multiple(q * 256, 256), 256), :]

    sum_begin(0, t.csa, t.cra, t.ysa, t.yra, t.acca, lambda q: nn(quarter(t.gated, q), t.wo[...]))
    pass_on(D, 1)
    x_out(E, fv_in.at[pl.ds(0, 64)])
    z_out(H, fv_in.at[pl.ds(64, 64)])
    neighbour_in(H)
    for h, n in ((0, 3), (1, 5)):
        sp_pass(n, adjviews[h])
        sp_sib(n, adjviews[h])
    pass_on(D, 2)
    sp_diag(1, fgview)
    sum_end(0, t.yra, t.acca)

    secview = rows(t.gfv, 256)

    def second_tile(i):
        r = pl.ds(multiple(i * 32, 32), 32)
        middle = t.xo[r, :].astype(F32) + t.acca[r, :]
        t.mid[r, :] = middle
        hat, _ = spread_rows(middle)
        second = (hat * vector(GAIN2) + vector(BIAS2)).astype(BF16)
        t.gfv[pl.ds(multiple(p * 256 + i * 32, 32), 32), :] = second
        return second

    t.edge[p] = second_tile(7)[16:32]
    for k in range(1, 4):
        send(t.edge.at[p], t.edge.at[p], t.eds.at[k], t.edr.at[p], (s, sps[k]))

    @pl.loop(0, 7)
    def _(i):
        second_tile(i)

    sp_out(2, secview)
    pass_on(E, 0)

    def feed_gate_weight():
        return t.wfg[...].reshape(1024, 1024)

    def live_rows(r, base):
        pos = base + iota((32, 1), 0)
        return t.rgrad[r, :].astype(F32) * (pos < e3).astype(F32)

    def feed_rows(q, fgin, mine):
        before = (q + 3) % 4
        t.last[0:1, :] = t.edge[before, 15:16, :].astype(F32)

        @pl.loop(0, 8)
        def _(i):
            base = q * 256 + i * 32
            r, u = pl.ds(multiple(base, 32), 32), pl.ds(multiple(i * 32, 32), 32)
            second = t.gfv[r, :].astype(F32)
            row = iota((32, 1), 0)
            prior = jnp.where(row == 0, t.last[0:1, :], pltpu.roll(second, 1, 0)) * same_at(base + row)
            t.last[0:1, :] = second[31:32, :]
            diff = second - prior
            if mine:
                t.sec[u, :] = diff
            t.fkall[r, :] = (prior + diff * vector(FMIXK)).astype(BF16)
            fgin[u, :] = (prior + diff * vector(FMIXG)).astype(BF16)

        gate = t.sig if mine else t.fgg
        gate[...] = jax.nn.sigmoid(nn(fgin[...], feed_gate_weight()))

        @pl.loop(0, 8)
        def _(i):
            base = q * 256 + i * 32
            r, u = pl.ds(multiple(base, 32), 32), pl.ds(multiple(i * 32, 32), 32)
            t.cgall[r, :] = (live_rows(r, base) * gate[u, :]).astype(BF16)

    def upstream(i):
        pos = p * 256 + i * 32 + iota((32, 1), 0)
        return t.adj[pl.ds(multiple(i * 32, 32), 32), :].astype(F32) * (pos < e3).astype(F32)

    def raise_rows(q):
        r = pl.ds(multiple(q * 256, 256), 256)
        relu = jnp.maximum(nn(t.fkall[r, :], t.wfk[...]), 0.0)
        t.hidden[r, :] = (relu * relu).astype(BF16)

    for k in range(1, 4):
        arrive(t.edge.at[sps[k]], t.edr.at[sps[k]])
    feed_rows(p, t.fgin, True)
    pass_on(E, 1)
    sp_sib(2, secview)
    feed_rows(p_sib, t.fpg, False)
    sp_diag(3, adjviews[0])
    sp_diag(5, adjviews[1])
    all_in(D)
    raise_rows(p)
    raise_rows(p_sib)
    pass_on(E, 2)
    pass_outwards(H)
    sp_pass(2, secview)
    feed_rows(p_y, t.fpg, False)
    raise_rows(p_y)
    sp_diag(2, secview)
    feed_rows(p_diag, t.fpg, False)
    raise_rows(p_diag)
    settle(("sp", 2), ("sp", 3))

    def value_tile(k):
        q = pl.ds(multiple(dests[k] * 256, 256), 256)
        t.gfv[q, :] = tn(t.hidden[:, q], t.cgall[...]).astype(BF16)
        grad_x_out(FV, dests[k])

    value_tile(1)
    rest_in(H)
    all_in(E)
    sum_begin(1, t.csb, t.crb, t.ysb, t.yrb, t.accb, lambda q: nn(quarter(t.hidden, q), t.wfv[...]))

    def lower_rows(q):
        r = pl.ds(multiple(q * 256, 256), 256)
        t.rgrad[r, :] = (nt(t.cgall[r, :], t.wfv[...]) * 2.0 * jnp.sqrt(t.hidden[r, :].astype(F32))).astype(BF16)

    value_tile(2)
    for q in (p_diag, p_sib, p_y, p):
        lower_rows(q)
    grad_x_in(FV, 1)
    value_tile(3)
    sum_begin(2, t.csa, t.cra, t.ysa, t.yra, t.acca, lambda q: nt(quarter(t.rgrad, q), t.wfk[...]))

    value_tile(0)
    grad_x_in(FV, 2)
    settle(D)
    for k in (1, 2, 3, 0):
        q = pl.ds(multiple(dests[k] * 256, 256), 256)
        t.wfk[q, :] = tn(t.fkall[:, q], t.rgrad[...]).astype(BF16)
        grad_x_out(FK, dests[k])

    sum_end(1, t.yrb, t.accb)

    @pl.loop(0, 8)
    def _(i):
        r = pl.ds(multiple(i * 32, 32), 32)
        pos = p * 256 + i * 32 + iota((32, 1), 0)
        live = (pos < e3).astype(F32)
        sig, total, up = t.sig[r, :], t.accb[r, :], upstream(i)
        t.b_out[r, :] = (live * (t.mid[r, :] + sig * total)).astype(BF16)
        t.fpg[r, :] = (up * total * sig * (1.0 - sig)).astype(BF16)

    t.fgg[...] = nt(t.fpg[...], feed_gate_weight())
    settle(C, ("sp", 1))
    for k in range(4):
        part = tn(t.fgin[:, 256 * k : 256 * k + 256], t.fpg[...]).astype(BF16)
        t.wfg[2 * k : 2 * k + 2] = part.reshape(2, 128, 1024)
    for j, q in enumerate((p_diag, p_sib)):
        send(fgview(q), t.fgcr.at[j], t.rss.at[4, j], t.rsr.at[4, j], sib)
    results = []

    def result(src, dst):
        copy = pltpu.make_async_copy(src, dst, t.loc.at[12 + len(results)])
        copy.start()
        results.append(copy)

    result(t.b_out, out)
    grad_x_in(FV, 3)
    sum_end(2, t.yra, t.acca)

    @pl.loop(0, 8)
    def _(i):
        r = pl.ds(multiple(i * 32, 32), 32)
        pos = p * 256 + i * 32 + iota((32, 1), 0)
        through = t.acca[r, :] * (1.0 - vector(FMIXK)) + t.fgg[r, :] * (1.0 - vector(FMIXG))
        t.moved[r, :] = through * same_at(pos)

    down_edge = remote(t.moved.at[pl.ds(0, 8)], t.moved.at[pl.ds(256, 8)], t.eds.at[0], t.edr.at[4], (s, sps[3]))

    @pl.when(p > 0)
    def _():
        down_edge.start()

    @pl.when(p == 3)
    def _():
        t.moved[256:264, :] = jnp.zeros((8, 1024), F32)

    @pl.when(p < 3)
    def _():
        remote(t.moved.at[pl.ds(256, 8)], t.moved.at[pl.ds(256, 8)], t.eds.at[0], t.edr.at[4], sib).wait_recv()

    @pl.when(p > 0)
    def _():
        down_edge.wait_send()

    def norm_back(hat, scale, grad, gain):
        grad = grad * gain
        return scale * (
            grad - jnp.mean(grad, axis=1, keepdims=True) - hat * jnp.mean(grad * hat, axis=1, keepdims=True)
        )

    def add_vector(k, v):
        t.vg[k] += v[0:8] + v[8:16] + v[16:24] + v[24:32]

    @pl.loop(0, 8)
    def _(i):
        r = pl.ds(multiple(i * 32, 32), 32)
        after = pltpu.roll(t.moved[pl.ds(multiple(i * 32, 32), 40), :], 39, 0)[0:32]
        by_key, by_gate = t.acca[r, :], t.fgg[r, :]
        grad = by_key * vector(FMIXK) + by_gate * vector(FMIXG) + after
        diff = t.sec[r, :]
        hat, scale = spread_rows(t.mid[r, :])
        add_vector(FMIXK, diff * by_key)
        add_vector(FMIXG, diff * by_gate)
        add_vector(GAIN2, grad * hat)
        add_vector(BIAS2, grad)
        total = upstream(i) + norm_back(hat, scale, grad, vector(GAIN2))
        t.mid[r, :] = total
        t.xall[pl.ds(multiple(p * 256 + i * 32, 32), 32), :] = total.astype(BF16)

    agview = xview
    sp_out(4, agview)
    grad_x_in(FK, 1)
    grad_x_in(FV, 0)

    arrive(t.fgcr.at[0], t.rsr.at[4, 0])
    there = pl.ds(multiple(p_y * 32, 32), 32)

    @pl.loop(0, 8)
    def _(i):
        t.wfg[i, there, :] = (t.wfg[i, there, :].astype(F32) + t.fgcr[0, i].astype(F32)).astype(BF16)

    send(fgview(p_y), t.fgyr, t.rss.at[4, 2], t.rsr.at[4, 2], ydev)
    grad_x_in(FK, 2)
    grad_x_in(FK, 3)
    sp_pass(4, agview)
    sp_sib(4, agview)
    sp_diag(4, agview)

    @pl.loop(0, 4)
    def _(i):
        r = pl.ds(multiple(i * 256, 256), 256)
        grad = nt(t.xall[r, :], t.wo[...])
        gate = t.gate[r, :]
        t.hidden[r, 0:256] = (grad * gate).astype(BF16)
        t.hidden[r, 256:512] = (grad * t.mixed[r, :].astype(BF16).astype(F32) * gate * (1.0 - gate)).astype(BF16)

    for k in (1, 2, 3, 0):
        q = pl.ds(multiple(dests[k] * 256, 256), 256)
        t.rgrad[q, 512:768] = tn(t.gin[:, q], t.hidden[:, 256:512]).astype(BF16)
        grad_x_out(G, dests[k])

    def backward_block(k, held):
        b = 7 - k
        d_top, d_bottom, d_first, d_rate = held
        r = pl.ds(multiple(b * 128, 128), 128)
        alike, keep, memory, tail = block_parts(b)
        later = (alike & (iota((128, 128), 1) > iota((128, 128), 0))).astype(F32).astype(BF16)
        top, bottom = t.carry[b, 0:1, :], t.carry[b, 1:2, :]
        v = t.vv[r, :].astype(F32)
        weight = jnp.exp(t.kk[r, :].astype(F32))
        d_high = t.hidden[r, 0:256].astype(F32) * t.inverse[r, :]
        d_low = -d_high * t.mixed[r, :]
        shrink = t.tables[1]
        sums = exact_dot(later, jnp.concatenate([shrink * d_high, shrink * d_low], axis=1))
        scaled = t.tables[0] * weight
        own = t.small[1:2, :] * weight
        tail = tail * weight
        by_sum = scaled * (v * sums[:, :256] + sums[:, 256:])
        by_own = own * (v * d_high + d_low)
        by_tail = tail * (v * d_top + d_bottom)
        by_memory = memory * (top * d_high + bottom * d_low)
        t.vv[r, :] = (scaled * sums[:, :256] + own * d_high + tail * d_top).astype(BF16)
        t.kk[r, :] = (by_sum + by_own + by_tail).astype(BF16)
        place = iota((128, 1), 0).astype(F32)
        d_rate = d_rate + column_sum(
            place * by_sum + (place - 1.0) * by_own - by_memory - (127.0 - place) * by_tail
        )
        d_rate = d_rate - 128.0 * keep * (top * d_top + bottom * d_bottom)
        d_first = d_first + column_sum(by_own)
        d_top = keep * d_top + column_sum(memory * d_high)
        d_bottom = keep * d_bottom + column_sum(memory * d_low)
        return d_top, d_bottom, d_first, d_rate

    held = lax.fori_loop(0, 4, backward_block, (zero, zero, zero, zero))
    held = lax.fori_loop(4, 8, backward_block, held)
    t.vgc[DECAY : DECAY + 1, :] = held[3] * t.small[2:3, :]
    t.vgc[FIRST : FIRST + 1, :] = held[2]

    for k in (1, 2, 3, 0):
        q = pl.ds(multiple(dests[k] * 256, 256), 256)
        t.rgrad[q, 0:256] = tn(t.kin[:, q], t.kk[...]).astype(BF16)
        t.rgrad[q, 256:512] = tn(t.vin[:, q], t.vv[...]).astype(BF16)
        grad_x_out(KV, dests[k])

    t.last[...] = jnp.zeros_like(t.last)

    xbview = rows(t.cgall, 256)

    def rows_back(i):
        r = pl.ds(multiple(256 * i, 256), 256)
        t.acca[...] = nt(t.kk[r, :], t.wkvg[:, 0:256])
        t.accb[...] = nt(t.vv[r, :], t.wkvg[:, 256:512])
        t.fgg[...] = nt(t.hidden[r, 256:512], t.wkvg[:, 512:768])

        @pl.loop(0, 8)
        def _(k):
            j = 7 - k
            u = pl.ds(multiple(j * 32, 32), 32)
            base = i * 256 + j * 32
            here = pl.ds(multiple(base, 32), 32)
            by_key, by_value, by_gate = t.acca[u, :], t.accb[u, :], t.fgg[u, :]
            diff = t.spread[here, :].astype(F32)
            add_vector(MIXK, diff * by_key)
            add_vector(MIXV, diff * by_value)
            add_vector(MIXG, diff * by_gate)
            current = by_key * vector(MIXK) + by_value * vector(MIXV) + by_gate * vector(MIXG)
            row = iota((32, 1), 0)
            through = (by_key + by_value + by_gate - current) * same_at(base + row)
            after = jnp.where(row == 31, t.last[0:1, :], pltpu.roll(through, 31, 0))
            t.last[0:1, :] = through[0:1, :]
            t.cgall[here, :] = (current + after).astype(BF16)

    def first_row(r):
        by = [nt(t.kk[r, :], t.wkvg[:, 0:256]), nt(t.vv[r, :], t.wkvg[:, 256:512])]
        by.append(nt(t.hidden[r, 256:512], t.wkvg[:, 512:768]))
        through = sum(b * (1.0 - vector(k)) for b, k in zip(by, (MIXK, MIXV, MIXG)))
        return through[0:1, :] * same_at(512 + iota((1, 1), 0))

    lower = (y == 1).astype(F32)
    t.last[0:1, :] = first_row(pl.ds(512, 16)) * lower
    other, mine_too = 2 * (1 - y), 2 * y
    rows_back(other + 1)
    rows_back(other)
    t.last[0:1, :] = t.last[0:1, :] * (1.0 - lower)

    send(xbview(p_diag), t.crb.at[0], t.rss.at[3, 0], t.rsr.at[3, 0], sib, ("sum", 3))
    grad_x_in(FK, 0)
    grad_x_in(G, 1)
    arrive(t.crb.at[0], t.rsr.at[3, 0])

    def to_other(r):
        there = pl.ds(multiple(p_y * 256 + r.start, 32), 32)
        t.ysb[r, :] = (t.cgall[there, :].astype(F32) + t.crb[0, r, :].astype(F32)).astype(BF16)

    add_rows(256, to_other)
    send(t.ysb, t.yrb, t.rss.at[3, 2], t.rsr.at[3, 2], ydev, ("sum", 3))
    rows_back(mine_too + 1)
    rows_back(mine_too)
    send(xbview(p_sib), t.crb.at[1], t.rss.at[3, 1], t.rsr.at[3, 1], sib, ("sum", 3))
    settle(B)
    t.wo[...] = tn(t.gated[...], t.xall[...]).astype(BF16)
    for k in (1, 2, 3, 0):
        grad_x_out(O, dests[k])
    arrive(t.crb.at[1], t.rsr.at[3, 1])

    def to_own(r):
        there = pl.ds(multiple(p * 256 + r.start, 32), 32)
        t.accb[r, :] = t.cgall[there, :].astype(F32) + t.crb[1, r, :].astype(F32)

    add_rows(256, to_own)
    grad_x_in(G, 2)
    grad_x_in(KV, 1)

    arrive(t.fgcr.at[1], t.rsr.at[4, 1])
    arrive(t.fgyr, t.rsr.at[4, 2])
    mine = pl.ds(multiple(p * 32, 32), 32)

    @pl.loop(0, 8)
    def _(i):
        total = t.wfg[i, mine, :].astype(F32) + t.fgcr[1, i].astype(F32) + t.fgyr[i].astype(F32)
        t.fgin[pl.ds(multiple(i * 32, 32), 32), :] = total.astype(BF16)

    for k in (1, 2, 3, 0):
        grad_x_out(FG, dests[k])
    grad_x_in(G, 3)
    grad_x_in(KV, 2)

    def put_fv(i, r, v):
        t.moved[r, :] = v

    def put_fk(i, r, v):
        t.fkpart[i] = v.astype(BF16)

    def put_kv(i, r, v):
        t.kvgpart[i, :, 0:512] = v.astype(BF16)

    def put_g(i, r, v):
        t.kvgpart[i, :, 512:768] = v.astype(BF16)

    def put_o(i, r, v):
        t.o_out[r, :] = v

    def put_fg(i, r, v):
        t.fg_out[r, :] = v

    settle(("a2a", 1), ("a2a", 2))
    grad_z_in(FV, put_fv)
    result(t.moved.at[pl.ds(0, 128)], g_fv)
    grad_x_in(KV, 3)
    grad_z_in(FK, put_fk)
    hand_back(0, t.fkpart, t.recfk)

    sum_end(3, t.yrb, t.accb)

    @pl.loop(0, 8)
    def _(i):
        r = pl.ds(multiple(i * 32, 32), 32)
        hat, scale = spread_rows(t.xo[r, :].astype(F32))
        grad = t.accb[r, :]
        add_vector(GAIN1, grad * hat)
        add_vector(BIAS1, grad)
        t.mid[r, :] = t.mid[r, :] + norm_back(hat, scale, grad, vector(GAIN1))

    lane = iota((16, 128), 1)
    mine_lanes = (lane >= 32 * p) & (lane < 32 * p + 32)
    for i in range(8):
        tile = t.vgc[:, 128 * (i // 4) : 128 * (i // 4) + 128]
        moved = pltpu.roll(tile, (32 * p + 128 - 32 * (i % 4)) % 128, 1)
        t.vmsg[i] = jnp.sum(t.vg[:, :, 128 * i : 128 * i + 128], axis=1) + jnp.where(mine_lanes, moved, 0.0)
    for k in range(1, 8):
        send(t.vmsg.at[sqs[k]], t.vrec.at[k], t.vss.at[0, k - 1], t.vsr.at[0, k], (sqs[k], p))
    result(t.mid, xgrad)
    for k in (1, 2, 3, 0):
        grad_x_in(O, k)
    for k in (1, 2, 3, 0):
        grad_x_in(FG, k)
    grad_x_in(G, 0)
    grad_z_in(G, put_g)
    total = t.vmsg[s]
    for k in range(1, 8):
        arrive(t.vrec.at[k], t.vsr.at[0, k])
        total = total + t.vrec[k]
    t.vtwo[...] = total
    for k in range(1, 4):
        send(t.vtwo, t.vrec2.at[k], t.vss.at[1, k - 1], t.vsr.at[1, k], (s, sps[k]))
    grad_x_in(KV, 0)
    grad_z_in(KV, put_kv)
    hand_back(1, t.kvgpart, t.reckvg)
    grad_z_in(O, put_o)
    result(t.o_out, g_o)
    grad_z_in(FG, put_fg)
    result(t.fg_out, g_fg)
    handed_back(0, t.recfk)
    for i in range(8):
        for j in range(4):
            first = 512 * (i % 2) + 128 * j
            part = t.recfk[j, :, 128 * i : 128 * i + 128].astype(F32)
            t.acca[32 * (i // 2) : 32 * (i // 2) + 32, first : first + 128] = part
    for i in range(4):
        result(t.acca.at[pl.ds(32 * i, 32)], g_fk.at[:, pl.ds(1024 * i, 1024)])
    total = t.vtwo[...]
    for k in range(1, 4):
        arrive(t.vrec2.at[k], t.vsr.at[1, k])
        total = total + t.vrec2[k]
    t.v_out[...] = pltpu.roll(total, (128 - 32 * p) % 128, 1)
    result(t.v_out, g_vec)
    handed_back(1, t.reckvg)
    result(t.reckvg, g_kvg)
    for _, copy, cond in pending:
        left(copy, cond)
    for copy in results:
        copy.wait()


def finish_kernel(
    a_out, a_xgrad, a_o, a_fg, a_fk, a_fv, a_kvg, a_vec,
    out, xgrad, g_o, g_fg, g_fk, g_fv, g_k, g_v, g_g, *rest,
):
    vectors, held, sems = rest[:11], rest[11:17], rest[17]
    pairs = ((a_xgrad, xgrad), (a_out, out), (a_fk, g_fk), (a_fv, g_fv), (a_o, g_o), (a_fg, g_fg))
    inward = [pltpu.make_async_copy(src, mid, sems.at[0, i]) for i, ((src, _), mid) in enumerate(zip(pairs, held))]
    outward = [pltpu.make_async_copy(mid, dst, sems.at[1, i]) for i, ((_, dst), mid) in enumerate(zip(pairs, held))]
    for copy in inward:
        copy.start()
    piece = iota((32, 128), 1) // 32
    for w, ref in enumerate((g_k, g_v, g_g)):
        for h in range(2):
            first = 256 * w + 128 * h
            tiles = [a_kvg[q, :, first : first + 128].astype(F32) for q in range(4)]
            for j in range(4):
                total = jnp.zeros((32, 128), F32)
                for q in range(4):
                    turn = 32 * (q - j) % 128
                    total = jnp.where(piece == q, pltpu.roll(tiles[q], turn, 1) if turn else tiles[q], total)
                ref[:, 512 * h + 128 * j : 512 * h + 128 * j + 128] = total
    for k, ref in enumerate(vectors):
        ref[...] = a_vec[k, 0:32]
    for first, second in zip(inward, outward):
        first.wait()
        second.start()
    for copy in outward:
        copy.wait()


def fast_body(
    incoming_signal,
    document_extents,
    adjoint_signal,
    layernorm_scaling,
    layernorm_offset,
    temporal_blend_lookup,
    temporal_blend_content,
    temporal_blend_receptor,
    temporal_shrinkage_log,
    diagonal_reward,
    lookup_projection,
    content_projection,
    receptor_projection,
    emission_projection,
    latter_scaling,
    latter_offset,
    channel_blend_lookup,
    channel_blend_receptor,
    channel_mixer_lookup,
    channel_mixer_content,
    channel_mixer_receptor,
):
    vecs = jnp.stack(
        [
            layernorm_scaling,
            layernorm_offset,
            temporal_blend_lookup,
            temporal_blend_content,
            temporal_blend_receptor,
            temporal_shrinkage_log,
            diagonal_reward,
            latter_scaling,
            latter_offset,
            channel_blend_lookup,
            channel_blend_receptor,
        ]
    )
    vecs = jnp.pad(vecs, ((0, 5), (0, 96)))
    anywhere = pl.BlockSpec(memory_space=pl.ANY)
    vmem = pl.BlockSpec(memory_space=pltpu.VMEM)
    shape = jax.ShapeDtypeStruct
    whole = (
        shape((256, 1024), BF16),
        shape((256, 1024), F32),
        shape((32, 1024), F32),
        shape((32, 1024), F32),
        shape((32, 4096), F32),
        shape((128, 1024), F32),
    )
    made = pl.pallas_call(
        step_kernel,
        out_shape=(*whole, shape((4, 32, 768), BF16), shape((16, 128), F32)),
        in_specs=[pl.BlockSpec(memory_space=pltpu.SMEM)] + [anywhere] * 10,
        out_specs=[anywhere] * 8,
        scratch_shapes=list(scratch_list().values()),
        compiler_params=pltpu.CompilerParams(
            collective_id=0, has_side_effects=True, vmem_limit_bytes=63 * 1024 * 1024
        ),
    )(
        document_extents,
        incoming_signal,
        adjoint_signal,
        vecs,
        lookup_projection,
        content_projection,
        receptor_projection,
        emission_projection,
        channel_mixer_receptor,
        channel_mixer_lookup,
        channel_mixer_content,
    )
    out, xgrad, g_o, g_fg, g_fk, g_fv, g_k, g_v, g_g, *v = pl.pallas_call(
        finish_kernel,
        out_shape=(*whole, *[shape((32, 1024), F32)] * 3, *[shape((32,), F32)] * 11),
        in_specs=[anywhere] * 6 + [vmem] * 2,
        out_specs=[anywhere] * 6 + [vmem] * 14,
        scratch_shapes=[
            *[pltpu.VMEM(whole[i].shape, whole[i].dtype) for i in (1, 0, 4, 5, 2, 3)],
            pltpu.SemaphoreType.DMA((2, 6)),
        ],
    )(*made)
    return (out, xgrad, *v[:7], g_k, g_v, g_g, g_o, *v[7:], g_fk, g_fv, g_fg)


def solution(mesh):
    fast = (mesh.shape["seq"], mesh.shape["sp"]) == (8, 4)
    flat, wide = P(("seq", "sp")), P(("seq", "sp"), None)
    return jax.shard_map(
        fast_body if fast else plain_body,
        mesh=mesh,
        in_specs=(wide, P("seq", None), wide, *[flat] * 7, *[wide] * 4, *[flat] * 4, *[wide] * 3),
        out_specs=(wide, wide, *[flat] * 7, *[wide] * 4, *[flat] * 4, *[wide] * 3),
        check_vma=False,
    )
```

```python
import functools
import types

import jax
import jax.numpy as jnp
from jax import lax
from jax.experimental import pallas as pl
from jax.experimental.pallas import tpu as pltpu
from jax.sharding import PartitionSpec as P

LOOP_LENGTH = 128


HIGHEST = lax.Precision.HIGHEST
EPSILON = 1e-05


def shifted(value, axis, steps):
    count = lax.axis_size(axis)
    first, last = (max(0, -steps), min(count, count - steps))
    return lax.ppermute(value, axis, [(source, source + steps) for source in range(first, last)])


def norm_rows(content_vectors, gain, bias):
    centered = content_vectors - jnp.mean(content_vectors, axis=1, keepdims=True)
    scale = lax.rsqrt(jnp.mean(centered * centered, axis=1, keepdims=True) + EPSILON)
    return centered * scale * gain + bias


def running(lengths_row):
    ends = [lengths_row[0]]
    for i in range(1, lengths_row.shape[0]):
        ends.append(ends[-1] + lengths_row[i])
    return ends


def segment_ids(lengths_row, positions):
    ends = jnp.stack(running(lengths_row))
    bounds = jnp.concatenate([ends - lengths_row, ends[-1:]])
    document_tags = jnp.sum((positions[:, None] >= bounds[None, :]).astype(jnp.int32), axis=1) - 1
    return (document_tags, positions < ends[-1])


def weighted_attention_loop(
    lookup_vectors,
    content_vectors,
    temporal_shrinkage_log,
    diagonal_reward,
    document_tags,
    segment_piece,
):
    count, feature_dimension = lookup_vectors.shape
    blocks = count // segment_piece
    rate = jnp.exp(temporal_shrinkage_log)
    offsets = jnp.arange(segment_piece, dtype=jnp.float32)[:, None]
    grow = jnp.exp(offsets * rate)
    shrink_multiplier = jnp.exp(-(offsets - 1.0) * rate)
    fade = jnp.exp(-offsets * rate)
    tail_fade = jnp.exp(-(segment_piece - 1.0 - offsets) * rate)
    whole_fade = jnp.exp(-1.0 * segment_piece * rate)
    order = jnp.arange(segment_piece, dtype=jnp.int32)
    lower = order[None, :] < order[:, None]
    key_blocks = lookup_vectors.reshape(blocks, segment_piece, feature_dimension)
    value_blocks = content_vectors.reshape(blocks, segment_piece, feature_dimension)
    label_blocks = document_tags.reshape(blocks, segment_piece)
    before = jnp.concatenate([jnp.full((1,), -1, jnp.int32), label_blocks[:-1, -1]])

    @jax.checkpoint
    def advance(carry, items):
        dividend_total, divisor_total = carry
        lookup_portion, content_portion, label_part, last_label = items
        weight_key = jnp.exp(lookup_portion)
        links = ((label_part[:, None] == label_part[None, :]) & lower).astype(jnp.float32)
        scaled = grow * weight_key
        cumulative_totals = jnp.dot(
            links, jnp.concatenate([scaled * content_portion, scaled], axis=1), precision=HIGHEST
        )
        recurrent_memory = (label_part == last_label).astype(jnp.float32)[:, None] * fade
        initial_reward = jnp.exp(diagonal_reward + lookup_portion)
        highest_line_entry = (
            shrink_multiplier * cumulative_totals[:, :feature_dimension]
            + recurrent_memory * dividend_total
            + initial_reward * content_portion
        )
        lowest_line_entry = (
            shrink_multiplier * cumulative_totals[:, feature_dimension:]
            + recurrent_memory * divisor_total
            + initial_reward
        )
        end_label = label_part[-1]
        keep = (end_label == last_label).astype(jnp.float32) * whole_fade
        tail = (label_part == end_label).astype(jnp.float32)[:, None] * tail_fade * weight_key
        dividend_total = keep * dividend_total + jnp.sum(tail * content_portion, axis=0)
        divisor_total = keep * divisor_total + jnp.sum(tail, axis=0)
        return ((dividend_total, divisor_total), highest_line_entry / lowest_line_entry)

    zeros = jnp.zeros((feature_dimension,), jnp.float32)
    _, blended_signal = lax.scan(
        advance, (zeros, zeros), (key_blocks, value_blocks, label_blocks, before)
    )
    return blended_signal.reshape(count, feature_dimension)


def product(left, right):
    return jnp.dot(left, right, preferred_element_type=jnp.float32)


def times_transposed(left, right):
    return lax.dot_general(
        left, right, (((1,), (1,)), ((), ())), preferred_element_type=jnp.float32
    )


def outer_sum(left, right):
    return lax.dot_general(
        left, right, (((0,), (0,)), ((), ())), preferred_element_type=jnp.float32
    )


def blend(current, prior, share):
    return current * share + prior * (1.0 - share)


def blend_back(current, prior, shares, grads):
    current_grad = jnp.zeros_like(current)
    prior_grad = jnp.zeros_like(current)
    spread = current - prior
    share_grads = []
    for share, grad in zip(shares, grads):
        current_grad = current_grad + grad * share
        prior_grad = prior_grad + grad * (1.0 - share)
        share_grads.append(jnp.sum(spread * grad, axis=0))
    return (current_grad, prior_grad, share_grads)


def plain_body(
    incoming_signal,
    document_extents,
    adjoint_signal,
    layernorm_scaling,
    layernorm_offset,
    temporal_blend_lookup,
    temporal_blend_content,
    temporal_blend_receptor,
    temporal_shrinkage_log,
    diagonal_reward,
    lookup_projection,
    content_projection,
    receptor_projection,
    emission_projection,
    latter_scaling,
    latter_offset,
    channel_blend_lookup,
    channel_blend_receptor,
    channel_mixer_lookup,
    channel_mixer_content,
    channel_mixer_receptor,
):
    rows = incoming_signal.shape[0]
    feature_dimension = incoming_signal.shape[1]
    parts = lax.axis_size("sp")
    place = lax.axis_index("sp")
    group_rows = rows * parts
    channels = feature_dimension // parts
    lengths_row = document_extents[0]
    positions = place * rows + jnp.arange(rows, dtype=jnp.int32)
    document_tags, live = segment_ids(lengths_row, positions)
    earlier, _ = segment_ids(lengths_row, positions - 1)
    same = (document_tags == earlier).astype(jnp.float32)[:, None]
    live_rows = live.astype(jnp.float32)[:, None]
    group_labels, _ = segment_ids(lengths_row, jnp.arange(group_rows, dtype=jnp.int32))
    fetched = [
        lax.all_gather(piece, ("seq", "sp"), axis=0, tiled=True)
        for piece in (
            layernorm_scaling,
            layernorm_offset,
            temporal_blend_lookup,
            temporal_blend_content,
            temporal_blend_receptor,
            temporal_shrinkage_log,
            diagonal_reward,
            lookup_projection,
            content_projection,
            receptor_projection,
            emission_projection,
            latter_scaling,
            latter_offset,
            channel_blend_lookup,
            channel_blend_receptor,
            channel_mixer_lookup,
            channel_mixer_content,
            channel_mixer_receptor,
        )
    ]
    vectors = [fetched[i].astype(jnp.float32) for i in (0, 1, 2, 3, 4, 5, 6, 11, 12, 13, 14)]
    gain_one, bias_one, share_key, share_value, share_gate, decay_all, first_all = vectors[:7]
    gain_two, bias_two, feed_share_key, feed_share_gate = vectors[7:]
    key_matrix, value_matrix, gate_matrix, output_matrix = (
        fetched[7],
        fetched[8],
        fetched[9],
        fetched[10],
    )
    feed_key_matrix, feed_value_matrix, feed_gate_matrix = (fetched[15], fetched[16], fetched[17])
    source = incoming_signal.astype(jnp.float32)
    normed, norm_pull = jax.vjp(norm_rows, source, gain_one, bias_one)
    edge = shifted(normed[-1:], "sp", 1)
    prior = jnp.concatenate([edge, normed[:-1]], axis=0) * same
    key_in = blend(normed, prior, share_key).astype(jnp.bfloat16)
    value_in = blend(normed, prior, share_value).astype(jnp.bfloat16)
    gate_in = blend(normed, prior, share_gate).astype(jnp.bfloat16)
    lookup_vectors = product(key_in, key_matrix).astype(jnp.bfloat16)
    content_vectors = product(value_in, value_matrix).astype(jnp.bfloat16)
    gate = jax.nn.sigmoid(product(gate_in, gate_matrix))
    arrived = lax.all_to_all(
        jnp.stack([lookup_vectors, content_vectors]), "sp", split_axis=2, concat_axis=1, tiled=True
    )
    decay_part = lax.dynamic_slice_in_dim(decay_all, place * channels, channels)
    first_part = lax.dynamic_slice_in_dim(first_all, place * channels, channels)

    def recurrence(key_full, value_full, decay_here, first_here):
        return weighted_attention_loop(
            key_full, value_full, decay_here, first_here, group_labels, LOOP_LENGTH
        )

    blended_signal, scan_pull = jax.vjp(
        recurrence,
        arrived[0].astype(jnp.float32),
        arrived[1].astype(jnp.float32),
        decay_part,
        first_part,
    )
    mixed_rows = lax.all_to_all(
        blended_signal.astype(jnp.bfloat16), "sp", split_axis=0, concat_axis=1, tiled=True
    ).astype(jnp.float32)
    gated = (gate * mixed_rows).astype(jnp.bfloat16)
    middle = source + product(gated, output_matrix)
    second, second_pull = jax.vjp(norm_rows, middle, gain_two, bias_two)
    second_edge = shifted(second[-1:], "sp", 1)
    prior_second = jnp.concatenate([second_edge, second[:-1]], axis=0) * same
    feed_key_in = blend(second, prior_second, feed_share_key).astype(jnp.bfloat16)
    feed_gate_in = blend(second, prior_second, feed_share_gate).astype(jnp.bfloat16)
    raised = product(feed_key_in, feed_key_matrix)
    hidden = jnp.square(jax.nn.relu(raised)).astype(jnp.bfloat16)
    recurrent_memory = product(hidden, feed_value_matrix)
    feed_sig = jax.nn.sigmoid(product(feed_gate_in, feed_gate_matrix))
    block_out = (live_rows * (middle + feed_sig * recurrent_memory)).astype(jnp.bfloat16)
    upstream = adjoint_signal.astype(jnp.float32) * live_rows
    carried_grad = (upstream * feed_sig).astype(jnp.bfloat16)
    feed_pre_grad = (upstream * recurrent_memory * feed_sig * (1.0 - feed_sig)).astype(jnp.bfloat16)
    grad_feed_value = outer_sum(hidden, carried_grad)
    grad_feed_gate = outer_sum(feed_gate_in, feed_pre_grad)
    raised_grad = (
        times_transposed(carried_grad, feed_value_matrix) * 2.0 * jax.nn.relu(raised)
    ).astype(jnp.bfloat16)
    grad_feed_key = outer_sum(feed_key_in, raised_grad)
    second_grad, second_prior_grad, feed_share_grads = blend_back(
        second,
        prior_second,
        (feed_share_key, feed_share_gate),
        (
            times_transposed(raised_grad, feed_key_matrix),
            times_transposed(feed_pre_grad, feed_gate_matrix),
        ),
    )
    moved = second_prior_grad * same
    incoming = shifted(moved[:1], "sp", -1)
    second_grad = second_grad + jnp.concatenate([moved[1:], incoming], axis=0)
    middle_norm_grad, grad_second_gain, grad_second_bias = second_pull(second_grad)
    middle_grad = upstream + middle_norm_grad
    attended_grad = middle_grad.astype(jnp.bfloat16)
    grad_output_weight = outer_sum(gated, attended_grad)
    gated_grad = times_transposed(attended_grad, output_matrix)
    mixed_grad = (gated_grad * gate).astype(jnp.bfloat16)
    gate_pre_grad = (gated_grad * mixed_rows * gate * (1.0 - gate)).astype(jnp.bfloat16)
    channel_grad = lax.all_to_all(mixed_grad, "sp", split_axis=1, concat_axis=0, tiled=True)
    key_grad_here, value_grad_here, decay_grad_here, first_grad_here = scan_pull(
        channel_grad.astype(jnp.float32)
    )
    returned = lax.all_to_all(
        jnp.stack([key_grad_here, value_grad_here]).astype(jnp.bfloat16),
        "sp",
        split_axis=1,
        concat_axis=2,
        tiled=True,
    )
    key_grad = returned[0]
    value_grad = returned[1]
    grad_key_weight = outer_sum(key_in, key_grad)
    grad_value_weight = outer_sum(value_in, value_grad)
    grad_gate_weight = outer_sum(gate_in, gate_pre_grad)
    normed_grad, normed_prior_grad, share_grads = blend_back(
        normed,
        prior,
        (share_key, share_value, share_gate),
        (
            times_transposed(key_grad, key_matrix),
            times_transposed(value_grad, value_matrix),
            times_transposed(gate_pre_grad, gate_matrix),
        ),
    )
    moved_first = normed_prior_grad * same
    incoming_first = shifted(moved_first[:1], "sp", -1)
    normed_grad = normed_grad + jnp.concatenate([moved_first[1:], incoming_first], axis=0)
    source_norm_grad, grad_norm_gain, grad_norm_bias = norm_pull(normed_grad)
    input_grad = middle_grad + source_norm_grad
    decay_grad = lax.dynamic_update_slice_in_dim(
        jnp.zeros((feature_dimension,), jnp.float32), decay_grad_here, place * channels, 0
    )
    first_grad = lax.dynamic_update_slice_in_dim(
        jnp.zeros((feature_dimension,), jnp.float32), first_grad_here, place * channels, 0
    )
    grads = (
        grad_norm_gain,
        grad_norm_bias,
        *share_grads,
        decay_grad,
        first_grad,
        grad_key_weight,
        grad_value_weight,
        grad_gate_weight,
        grad_output_weight,
        grad_second_gain,
        grad_second_bias,
        *feed_share_grads,
        grad_feed_key,
        grad_feed_value,
        grad_feed_gate,
    )
    shares = []
    for grad in grads:
        for axis in ("seq", "sp"):
            grad = lax.psum_scatter(
                grad.astype(jnp.bfloat16), axis, scatter_dimension=0, tiled=True
            ).astype(jnp.float32)
        shares.append(grad)
    return (block_out, input_grad, *shares)


MESH = pl.DeviceIdType.MESH
F32 = jnp.float32
BF16 = jnp.bfloat16
GAIN1, BIAS1, MIXK, MIXV, MIXG, DECAY, FIRST, GAIN2, BIAS2, FMIXK, FMIXG = range(11)


def multiple(value, step):
    return pl.multiple_of(value, step)


def nn(a, b):
    return jnp.dot(a, b, preferred_element_type=F32)


def nt(a, b):
    return lax.dot_general(a, b, (((1,), (1,)), ((), ())), preferred_element_type=F32)


def tn(a, b):
    return lax.dot_general(a, b, (((0,), (0,)), ((), ())), preferred_element_type=F32)


def exact_dot(links, right):
    high = right.astype(BF16)
    rest = right - high.astype(F32)
    middle = rest.astype(BF16)
    low = (rest - middle.astype(F32)).astype(BF16)
    return nn(links, high) + nn(links, middle) + nn(links, low)


def iota(shape, axis):
    return lax.broadcasted_iota(jnp.int32, shape, axis)


def spread_rows(v):
    centered = v - jnp.mean(v, axis=1, keepdims=True)
    scale = lax.rsqrt(jnp.mean(centered * centered, axis=1, keepdims=True) + EPSILON)
    return centered * scale, scale


def column_sum(v):
    return jnp.sum(v, axis=0, keepdims=True)


def scratch_list():
    vm = pltpu.VMEM
    sem = pltpu.SemaphoreType.DMA
    return dict(
        xall=vm((1024, 1024), BF16),
        kin=vm((1024, 1024), BF16),
        vin=vm((1024, 1024), BF16),
        gin=vm((1024, 1024), BF16),
        spread=vm((1024, 1024), BF16),
        wkvg=vm((1024, 768), BF16),
        wo=vm((256, 1024), BF16),
        wfg=vm((8, 128, 1024), BF16),
        wfk=vm((1024, 1024), BF16),
        wfv=vm((1024, 1024), BF16),
        kk=vm((1024, 256), BF16),
        vv=vm((1024, 256), BF16),
        gate=vm((1024, 256), F32),
        mixed=vm((1024, 256), F32),
        inverse=vm((1024, 256), F32),
        gated=vm((1024, 256), BF16),
        carry=vm((8, 8, 256), F32),
        tables=vm((4, 128, 256), F32),
        small=vm((8, 256), F32),
        last=vm((8, 1024), F32),
        xo=vm((256, 1024), BF16),
        adj=vm((256, 1024), BF16),
        mid=vm((256, 1024), F32),
        sec=vm((256, 1024), F32),
        edge=vm((4, 16, 1024), BF16),
        sig=vm((256, 1024), F32),
        fgin=vm((256, 1024), BF16),
        fpg=vm((256, 1024), BF16),
        fkall=vm((1024, 1024), BF16),
        cgall=vm((1024, 1024), BF16),
        hidden=vm((1024, 1024), BF16),
        gfv=vm((1024, 1024), BF16),
        rgrad=vm((1024, 1024), BF16),
        acca=vm((256, 1024), F32),
        accb=vm((256, 1024), F32),
        fgg=vm((256, 1024), F32),
        moved=vm((264, 1024), F32),
        csa=vm((2, 256, 1024), BF16),
        cra=vm((2, 256, 1024), BF16),
        ysa=vm((256, 1024), BF16),
        yra=vm((256, 1024), BF16),
        csb=vm((2, 256, 1024), BF16),
        crb=vm((2, 256, 1024), BF16),
        ysb=vm((256, 1024), BF16),
        yrb=vm((256, 1024), BF16),
        fgcr=vm((2, 8, 32, 1024), BF16),
        fgyr=vm((8, 32, 1024), BF16),
        xrfv=vm((4, 128, 1024), BF16),
        xrfk=vm((4, 128, 1024), BF16),
        xrfg=vm((4, 32, 1024), BF16),
        xro=vm((32, 1024), BF16),
        xrkv=vm((4, 128, 512), BF16),
        xrg=vm((4, 128, 256), BF16),
        zrfv=vm((3, 128, 1024), BF16),
        zrfk=vm((3, 128, 1024), BF16),
        zrfg=vm((3, 32, 1024), BF16),
        zro=vm((3, 64, 1024), BF16),
        zrkv=vm((3, 128, 512), BF16),
        zrg=vm((3, 128, 256), BF16),
        kvgraw=vm((3, 32, 1024), BF16),
        fkraw=vm((32, 4096), BF16),
        kvgpart=vm((4, 32, 768), BF16),
        fkpart=vm((4, 32, 1024), BF16),
        o_out=vm((32, 1024), F32),
        fg_out=vm((32, 1024), F32),
        mrfv=vm((128, 1024), BF16),
        mrfk=vm((128, 1024), BF16),
        mrfg=vm((32, 1024), BF16),
        mro=vm((64, 1024), BF16),
        mrkv=vm((128, 512), BF16),
        mrg=vm((128, 256), BF16),
        b_out=vm((256, 1024), BF16),
        v_out=vm((16, 128), F32),
        recfk=vm((4, 32, 1024), BF16),
        reckvg=vm((4, 32, 768), BF16),
        vraw=vm((8, 4, 16, 128), BF16),
        nat=vm((16, 1024), F32),
        chan=vm((16, 256), F32),
        vg=vm((16, 8, 1024), F32),
        vgc=vm((16, 256), F32),
        vmsg=vm((8, 16, 128), F32),
        vrec=vm((8, 16, 128), F32),
        vtwo=vm((16, 128), F32),
        vrec2=vm((4, 16, 128), F32),
        ags=sem((7, 9)),
        agr=sem((7, 8)),
        a2s=sem((3, 3)),
        a2r=sem((3, 4)),
        sps=sem((8, 3)),
        spr=sem((8, 3)),
        rss=sem((5, 3)),
        rsr=sem((5, 3)),
        qxs=sem((6, 4)),
        qxr=sem((6, 4)),
        qzs=sem((6, 3)),
        qzr=sem((6, 3)),
        qmr=sem((6,)),
        fas=sem((2, 3)),
        far=sem((2, 4)),
        vss=sem((2, 7)),
        vsr=sem((2, 8)),
        eds=sem((4,)),
        edr=sem((5,)),
        loc=sem((24,)),
    )


def step_kernel(
    lengths, xin, adjoint, vecs, k_in, v_in, g_in, o_in, fg_in, fk_in, fv_in,
    out, xgrad, g_o, g_fg, g_fk, g_fv, g_kvg, g_vec,
    *scratch,
):
    t = types.SimpleNamespace(**dict(zip(scratch_list(), scratch)))
    s, p = lax.axis_index("seq"), lax.axis_index("sp")
    z, x, y, c = s // 2, s % 2, p // 2, p % 2
    zs = [(z + k) % 4 for k in range(4)]
    xdev = (z * 2 + 1 - x, p)
    ydev, sib = (s, (1 - y) * 2 + c), (s, y * 2 + 1 - c)
    sps = [(p + k) % 4 for k in range(4)]
    sqs = [(s + k) % 8 for k in range(8)]
    p_sib, p_y, p_diag = y * 2 + 1 - c, (1 - y) * 2 + c, (1 - y) * 2 + 1 - c

    pending = []

    def remote(src, dst, send_sem, recv_sem, device):
        return pltpu.make_async_remote_copy(
            src_ref=src, dst_ref=dst, send_sem=send_sem, recv_sem=recv_sem,
            device_id=device, device_id_type=MESH,
        )

    def send(src, dst, send_sem, recv_sem, device, tag=None):
        copy = remote(src, dst, send_sem, recv_sem, device)
        copy.start()
        pending.append((tag, copy, None))
        return copy

    def left(copy, cond):
        if cond is None:
            copy.wait_send()
        else:
            pl.when(cond)(copy.wait_send)

    def settle(*tags):
        for tag, copy, cond in pending:
            if tag in tags:
                left(copy, cond)
        pending[:] = [entry for entry in pending if entry[0] not in tags]

    def arrive(dst, recv_sem):
        remote(dst, dst, recv_sem, recv_sem, sib).wait_recv()

    def local(src, dst, k):
        copy = pltpu.make_async_copy(src, dst, t.loc.at[k])
        copy.start()
        return copy

    barrier = pltpu.get_barrier_semaphore()
    for k in range(1, 8):
        pl.semaphore_signal(barrier, inc=1, device_id=(sqs[k], p), device_id_type=MESH)
    for k in range(1, 4):
        pl.semaphore_signal(barrier, inc=1, device_id=(s, sps[k]), device_id_type=MESH)

    loads = []

    def load(src, dst):
        copy = pltpu.make_async_copy(src, dst, t.loc.at[len(loads)])
        copy.start()
        loads.append(copy)

    def own_rows(ref, size):
        return ref.at[pl.ds(multiple(s * size, size), size)]

    load(k_in, t.kvgraw.at[0])
    load(v_in, t.kvgraw.at[1])
    load(g_in, t.kvgraw.at[2])
    load(vecs, t.vraw.at[s, p])
    load(fk_in, t.fkraw)
    early = len(loads)
    load(xin, t.xall.at[pl.ds(multiple(p * 256, 256), 256)])
    load(o_in, own_rows(t.wo, 32))
    load(fg_in, t.wfg.at[s, pl.ds(multiple(p * 32, 32), 32)])
    load(fv_in, own_rows(t.wfv, 128))
    load(xin, t.xo)
    load(adjoint, t.adj)
    load(adjoint, t.rgrad.at[pl.ds(multiple(p * 256, 256), 256)])
    for copy in loads[:4]:
        copy.wait()
    piece = iota((32, 128), 1) // 32
    for w in range(3):
        for h in range(2):
            tiles = [t.kvgraw[w, :, 512 * h + 128 * j : 512 * h + 128 * j + 128].astype(F32) for j in range(4)]
            for q in range(4):
                total = jnp.zeros((32, 128), F32)
                for j in range(4):
                    turn = 32 * (j - q) % 128
                    total = jnp.where(piece == j, pltpu.roll(tiles[j], turn, 1) if turn else tiles[j], total)
                t.kvgpart[q, :, 256 * w + 128 * h : 256 * w + 128 * h + 128] = total.astype(BF16)
    loads[4].wait()
    for i in range(8):
        for q in range(4):
            t.fkpart[q, :, 128 * i : 128 * i + 128] = t.fkraw[:, 512 * i + 128 * q : 512 * i + 128 * q + 128]

    pl.semaphore_wait(barrier, 10)

    def rows(ref, size):
        return lambda i: ref.at[pl.ds(multiple(i * size, size), size)]

    V, A, B, C, D, E, H = range(7)
    block = {
        V: lambda i: t.vraw.at[i],
        A: rows(t.wkvg, 128),
        B: rows(t.wo, 32),
        C: lambda i: t.wfg.at[i, pl.ds(multiple(p * 32, 32), 32)],
        D: rows(t.wfk, 128),
        E: lambda i: t.wfv.at[pl.ds(multiple(i * 128, 64), 64)],
        H: lambda i: t.wfv.at[pl.ds(multiple(i * 128 + 64, 64), 64)],
    }

    inner = (z == 1) | (z == 2)
    far = (z + 2) % 4
    beside = 1 + z % 2
    outer = 3 * (z // 2)

    def pick(*values):
        return sum((z == i).astype(jnp.int32) * v for i, v in enumerate(values))

    sources = (pick(1, 3, 0, 2), pick(2, 0, 3, 1), pick(3, 2, 1, 0))

    def send_if(cond, src, dst, send_sem, recv_sem, device, tag=None):
        copy = remote(src, dst, send_sem, recv_sem, device)
        pl.when(cond)(copy.start)
        pending.append((tag, copy, cond))

    def along_z(item, i, src, first):
        there = block[item](i)
        send(src, there, t.ags.at[item, first], t.agr.at[item, i], (far * 2 + x, p), item)
        send(src, there, t.ags.at[item, first + 1], t.agr.at[item, i], (beside * 2 + x, p), item)
        send_if(inner, src, there, t.ags.at[item, first + 2], t.agr.at[item, i], (outer * 2 + x, p), item)

    def hand_on(item, i, sem):
        send_if(inner, block[item](i), block[item](i), t.ags.at[item, sem], t.agr.at[item, i], (outer * 2 + x, p), item)

    def x_out(item, src):
        send(src, block[item](s), t.ags.at[item, 0], t.agr.at[item, s], xdev, item)

    def z_out(item, src):
        if item == V:
            for k in range(1, 4):
                send(src, block[V](s), t.ags.at[V, k], t.agr.at[V, s], (zs[k] * 2 + x, p), V)
        else:
            along_z(item, s, src, 1)

    def pass_on(item, j):
        i = sources[j] * 2 + x
        arrive(block[item](i), t.agr.at[item, i])
        send(block[item](i), block[item](i), t.ags.at[item, 4 + j], t.agr.at[item, i], xdev, item)
        if j == 0 and item != V:
            hand_on(item, i, 7)

    def all_in(item):
        for k in range(4):
            i = zs[k] * 2 + 1 - x
            arrive(block[item](i), t.agr.at[item, i])

    def neighbour_in(item):
        i = z * 2 + 1 - x
        arrive(block[item](i), t.agr.at[item, i])
        along_z(item, i, block[item](i), 4)

    def pass_outwards(item):
        for xx, sem in ((x, 7), (1 - x, 8)):
            i = sources[0] * 2 + xx
            arrive(block[item](i), t.agr.at[item, i])
            hand_on(item, i, sem)

    def rest_in(item):
        for j in (1, 2):
            for xx in (x, 1 - x):
                i = sources[j] * 2 + xx
                arrive(block[item](i), t.agr.at[item, i])

    def sp_tag(n):
        return ("sp", {5: 3, 6: 2, 7: 4}.get(n, n))

    def sp_out(n, view):
        send(view(p), view(p), t.sps.at[n, 0], t.spr.at[n, 0], ydev, sp_tag(n))
        send(view(p), view(p), t.sps.at[n, 1], t.spr.at[n, 1], sib, sp_tag(n))

    def sp_pass(n, view):
        arrive(view(p_y), t.spr.at[n, 0])
        send(view(p_y), view(p_y), t.sps.at[n, 2], t.spr.at[n, 2], sib, sp_tag(n))

    def sp_sib(n, view):
        arrive(view(p_sib), t.spr.at[n, 1])

    def sp_diag(n, view):
        arrive(view(p_diag), t.spr.at[n, 2])

    def halves(ref):
        return [lambda i, h=h: ref.at[pl.ds(multiple(i * 256 + 128 * h, 128), 128)] for h in range(2)]

    def add_rows(n, fn):
        @pl.loop(0, n // 32)
        def _(i):
            fn(pl.ds(multiple(i * 32, 32), 32))

    def sum_begin(n, cs, cr, ys, yr, acc, compute):
        def to_sibling(j, q):
            cs[j] = compute(q).astype(BF16)
            send(cs.at[j], cr.at[j], t.rss.at[n, j], t.rsr.at[n, j], sib, ("sum", n))

        def to_other(r):
            ys[r, :] = (acc[r, :] + cr[0, r, :].astype(F32)).astype(BF16)

        def to_own(r):
            acc[r, :] += cr[1, r, :].astype(F32)

        to_sibling(0, p_diag)
        acc[...] = compute(p_y)
        arrive(cr.at[0], t.rsr.at[n, 0])
        add_rows(256, to_other)
        send(ys, yr, t.rss.at[n, 2], t.rsr.at[n, 2], ydev, ("sum", n))
        to_sibling(1, p_sib)
        acc[...] = compute(p)
        arrive(cr.at[1], t.rsr.at[n, 1])
        add_rows(256, to_own)

    def sum_end(n, yr, acc):
        arrive(yr, t.rsr.at[n, 2])

        def add(r):
            acc[r, :] += yr[r, :].astype(F32)

        add_rows(256, add)
        settle(("sum", n))

    FV, FK, FG, O, KV, G = range(6)
    grads = {
        FV: (t.gfv, t.xrfv, t.zrfv, t.mrfv, 128),
        FK: (t.wfk, t.xrfk, t.zrfk, t.mrfk, 128),
        FG: (t.fgin, t.xrfg, t.zrfg, t.mrfg, 32),
        O: (t.wo, t.xro, t.zro, t.mro, 32),
        KV: (t.rgrad.at[:, pl.ds(0, 512)], t.xrkv, t.zrkv, t.mrkv, 128),
        G: (t.rgrad.at[:, pl.ds(512, 256)], t.xrg, t.zrg, t.mrg, 128),
    }
    dests = (z, pick(3, 0, 3, 0), pick(2, 2, 1, 1), pick(1, 3, 0, 2))

    def piece_of(item, i):
        ref, xr, _, _, size = grads[item]
        return ref.at[pl.ds(multiple(i * size, size), size), pl.ds(0, xr.shape[2])]

    def grad_x_out(item, zz):
        xr = grads[item][1]
        send(piece_of(item, zz * 2 + 1 - x), xr.at[zz], t.qxs.at[item, zz], t.qxr.at[item, zz], xdev)

    def grad_x_in(item, j):
        ref, xr, zr, mr, size = grads[item]
        zz = dests[j]
        arrive(xr.at[zz], t.qxr.at[item, zz])
        if j == 0:
            return
        base = (zz * 2 + x) * size
        w = pl.ds(0, xr.shape[2])

        def add(r):
            here = pl.ds(multiple(base + r.start, 32), 32)
            ref[here, w] = (ref[here, w].astype(F32) + xr[zz, r, :].astype(F32)).astype(BF16)

        def add_both(r):
            here = pl.ds(multiple(base + r.start, 32), 32)
            total = ref[here, w].astype(F32) + xr[zz, r, :].astype(F32)
            ref[here, w] = (total + mr[r, :].astype(F32)).astype(BF16)

        if j == 3:

            @pl.when(inner)
            def _():
                arrive(mr, t.qmr.at[item])
                add_rows(size, add_both)

            @pl.when(jnp.logical_not(inner))
            def _():
                add_rows(size, add)
        else:
            add_rows(size, add)
        piece, slot = piece_of(item, zz * 2 + x), (z - zz + 3) % 4
        straight = (zr.at[slot], t.qzs.at[item, j - 1], t.qzr.at[item, slot], (zz * 2 + x, p))
        if j == 1:
            send_if(inner, piece, *straight)
            send_if(jnp.logical_not(inner), piece, mr, t.qzs.at[item, 0], t.qmr.at[item], (beside * 2 + x, p))
        else:
            send(piece, *straight)

    def grad_z_in(item, put):
        ref, xr, zr, _, size = grads[item]
        wait_z(item)

        @pl.loop(0, size // 32)
        def _(i):
            r = pl.ds(multiple(i * 32, 32), 32)
            here = pl.ds(multiple(s * size + i * 32, 32), 32)
            total = ref[here, pl.ds(0, xr.shape[2])].astype(F32) + xr[z, r, :].astype(F32)
            total = total + zr[0, r, :].astype(F32) + zr[1, r, :].astype(F32) + zr[2, r, :].astype(F32)
            put(i, r, total)

    def first_z(item, j):
        ref, _, zr, mr, _ = grads[item]
        zz = dests[j]
        piece, slot = rows(ref, 64)(zz), (z - zz + 3) % 4
        straight = (zr.at[slot], t.qzs.at[item, j - 1], t.qzr.at[item, slot], (zz * 2 + x, p))
        if j == 1:
            send_if(inner, piece, *straight)
            send_if(jnp.logical_not(inner), piece, mr, t.qzs.at[item, 0], t.qmr.at[item], (beside * 2 + x, p))
            return
        if j == 3:

            @pl.when(inner)
            def _():
                arrive(mr, t.qmr.at[item])

                def add(r):
                    here = pl.ds(multiple(zz * 64 + r.start, 32), 32)
                    ref[here, :] = (ref[here, :].astype(F32) + mr[r, :].astype(F32)).astype(BF16)

                add_rows(64, add)

        send(piece, *straight)

    def wait_z(item):
        zr = grads[item][2]
        for slot in range(3):
            both = (z + slot + 1) % 4 == 3 - z
            opposite = jnp.logical_and(both, jnp.logical_not(inner))

            @pl.when(jnp.logical_not(opposite))
            def _():
                arrive(zr.at[slot], t.qzr.at[item, slot])

            @pl.when(opposite)
            def _():
                zr[slot] = jnp.zeros(zr.shape[1:], BF16)

    def then_x(item):
        ref, xr, zr, _, _ = grads[item]
        wait_z(item)

        def add(r):
            here = pl.ds(multiple(z * 64 + r.start, 32), 32)
            total = zr[0, r, :].astype(F32) + zr[1, r, :].astype(F32) + zr[2, r, :].astype(F32)
            ref[here, :] = (ref[here, :].astype(F32) + total).astype(BF16)

        add_rows(64, add)
        send(rows(ref, 32)(z * 2 + 1 - x), xr, t.qxs.at[item, 0], t.qxr.at[item, 0], xdev)

    def last_x(item, put):
        ref, xr, _, _, _ = grads[item]
        arrive(xr, t.qxr.at[item, 0])
        put(0, pl.ds(0, 32), ref[pl.ds(multiple(s * 32, 32), 32), :].astype(F32) + xr[...].astype(F32))

    def hand_back(n, fin, rec):
        for k in range(1, 4):
            send(fin.at[sps[k]], rec.at[p], t.fas.at[n, k - 1], t.far.at[n, p], (s, sps[k]))
        rec[p] = fin[p]

    def handed_back(n, rec):
        for k in range(1, 4):
            arrive(rec.at[sps[k]], t.far.at[n, sps[k]])

    e0 = lengths[0, 0]
    e1 = e0 + lengths[0, 1]
    e2 = e1 + lengths[0, 2]
    e3 = e2 + lengths[0, 3]

    def label(pos):
        total = (pos >= 0).astype(jnp.int32)
        for edge in (e0, e1, e2, e3):
            total = total + (pos >= edge).astype(jnp.int32)
        return total - 1

    def same_at(pos):
        return (label(pos) == label(pos - 1)).astype(F32)

    xview = rows(t.xall, 256)

    def a2a_out(n, src, dst):
        for k in (2, 1, 3):
            send(src(sps[k]), dst(p), t.a2s.at[n, k - 1], t.a2r.at[n, p], (s, sps[k]), ("a2a", n))

    def a2a_in(n, dst):
        for k in range(1, 4):
            arrive(dst(sps[k]), t.a2r.at[n, sps[k]])

    vec_dst = lambda i: t.vraw.at[s, i]
    kvg_dst = lambda i: t.wkvg.at[pl.ds(multiple(s * 128 + i * 32, 32), 32)]
    fk_dst = lambda i: t.wfk.at[pl.ds(multiple(s * 128 + i * 32, 32), 32)]
    a2a_out(0, lambda i: vecs, vec_dst)
    a2a_out(1, lambda i: t.kvgpart.at[i], kvg_dst)
    a2a_out(2, lambda i: t.fkpart.at[i], fk_dst)
    send(xin, xview(p), t.sps.at[0, 0], t.spr.at[0, 0], ydev)
    send(xin, xview(p), t.sps.at[0, 1], t.spr.at[0, 1], sib)
    adjviews = halves(t.rgrad)

    def adjoint_out(h):
        piece = adjoint.at[pl.ds(128 * h, 128)]
        send(piece, adjviews[h](p), t.sps.at[3 + 2 * h, 0], t.spr.at[3 + 2 * h, 0], ydev, ("sp", 3))
        send(piece, adjviews[h](p), t.sps.at[3 + 2 * h, 1], t.spr.at[3 + 2 * h, 1], sib, ("sp", 3))

    t.wkvg[pl.ds(multiple(s * 128 + p * 32, 32), 32), :] = t.kvgpart[p]
    t.wfk[pl.ds(multiple(s * 128 + p * 32, 32), 32), :] = t.fkpart[p]
    a2a_in(0, vec_dst)
    x_out(V, t.vraw.at[s])
    z_out(V, t.vraw.at[s])
    x_out(C, fg_in)
    z_out(C, fg_in)
    a2a_in(1, kvg_dst)
    z_out(A, block[A](s))
    for j in range(3):
        pass_on(V, j)
    x_out(A, block[A](s))
    for copy in loads[early:]:
        copy.wait()
    a2a_in(2, fk_dst)
    pass_on(C, 0)
    pass_on(C, 1)
    z_out(B, o_in)
    all_in(V)

    t.last[...] = jnp.zeros_like(t.last)
    t.vg[...] = jnp.zeros_like(t.vg)
    t.vgc[...] = jnp.zeros_like(t.vgc)
    for i in range(8):
        total = t.vraw[i, 0].astype(F32)
        for j in range(1, 4):
            total = total + pltpu.roll(t.vraw[i, j].astype(F32), 32 * j, 1)
        t.nat[:, 128 * i : 128 * i + 128] = total
    for i in range(2):
        total = t.vraw[4 * i, p].astype(F32)
        for j in range(1, 4):
            total = total + pltpu.roll(t.vraw[4 * i + j, p].astype(F32), 32 * j, 1)
        t.chan[:, 128 * i : 128 * i + 128] = total

    def vector(k):
        return t.nat[k : k + 1, :]

    rate = jnp.exp(t.chan[DECAY : DECAY + 1, :])
    offset = iota((128, 1), 0).astype(F32)
    t.tables[0] = jnp.exp(offset * rate)
    t.tables[1] = jnp.exp(-(offset - 1.0) * rate)
    t.tables[2] = jnp.exp(-offset * rate)
    t.tables[3] = jnp.exp(-(127.0 - offset) * rate)
    t.small[0:1, :] = jnp.exp(-128.0 * rate)
    t.small[1:2, :] = jnp.exp(t.chan[FIRST : FIRST + 1, :])
    t.small[2:3, :] = rate

    pass_on(A, 0)
    pass_on(C, 2)
    pass_on(A, 1)
    x_out(B, o_in)
    sp_pass(0, xview)
    all_in(C)
    fgview = lambda i: t.wfg.at[:, pl.ds(multiple(i * 32, 32), 32)]
    sp_out(1, fgview)
    adjoint_out(0)
    sp_sib(0, xview)
    sp_diag(0, xview)

    def norm_quarter(q):
        @pl.loop(0, 8)
        def _(i):
            base = q * 256 + i * 32
            r = pl.ds(multiple(base, 32), 32)
            hat, _ = spread_rows(t.xall[r, :].astype(F32))
            normed = hat * vector(GAIN1) + vector(BIAS1)
            row = iota((32, 1), 0)
            prior = jnp.where(row == 0, t.last[0:1, :], pltpu.roll(normed, 1, 0))
            prior = prior * same_at(base + row)
            t.last[0:1, :] = normed[31:32, :]
            diff = normed - prior
            t.spread[r, :] = diff.astype(BF16)
            t.kin[r, :] = (prior + diff * vector(MIXK)).astype(BF16)
            t.vin[r, :] = (prior + diff * vector(MIXV)).astype(BF16)
            t.gin[r, :] = (prior + diff * vector(MIXG)).astype(BF16)

    norm_quarter(0)
    pass_on(A, 2)
    pass_on(B, 0)
    norm_quarter(1)
    z_out(D, block[D](s))
    norm_quarter(2)
    pass_on(B, 1)
    norm_quarter(3)
    all_in(A)
    settle(("sp", 0))

    @pl.loop(0, 4)
    def _(i):
        r = pl.ds(multiple(i * 256, 256), 256)
        t.kk[r, :] = nn(t.kin[r, :], t.wkvg[:, 0:256]).astype(BF16)
        t.vv[r, :] = nn(t.vin[r, :], t.wkvg[:, 256:512]).astype(BF16)
        t.gate[r, :] = jax.nn.sigmoid(nn(t.gin[r, :], t.wkvg[:, 512:768]))

    def block_parts(b):
        base = b * 128
        column = label(base + iota((128, 1), 0))
        row = label(base + iota((1, 128), 1))
        before, end = label(base - 1), label(base + 127)
        alike = column == row
        keep = (before == end).astype(F32) * t.small[0:1, :]
        memory = (column == before).astype(F32) * t.tables[2]
        tail = (column == end).astype(F32) * t.tables[3]
        return alike, keep, memory, tail

    def forward_block(b, held):
        top, bottom = held
        r = pl.ds(multiple(b * 128, 128), 128)
        alike, keep, memory, tail = block_parts(b)
        links = (alike & (iota((128, 128), 1) < iota((128, 128), 0))).astype(F32).astype(BF16)
        v = t.vv[r, :].astype(F32)
        weight = jnp.exp(t.kk[r, :].astype(F32))
        scaled = t.tables[0] * weight
        sums = exact_dot(links, jnp.concatenate([scaled * v, scaled], axis=1))
        own = t.small[1:2, :] * weight
        high = t.tables[1] * sums[:, :256] + memory * top + own * v
        low = t.tables[1] * sums[:, 256:] + memory * bottom + own
        inverse = 1.0 / low
        mixed = high * inverse
        t.inverse[r, :] = inverse
        t.mixed[r, :] = mixed
        t.gated[r, :] = (t.gate[r, :] * mixed.astype(BF16).astype(F32)).astype(BF16)
        t.carry[b, 0:1, :] = top
        t.carry[b, 1:2, :] = bottom
        tail = tail * weight
        return keep * top + column_sum(tail * v), keep * bottom + column_sum(tail)

    zero = jnp.zeros((1, 256), F32)
    held = lax.fori_loop(0, 4, forward_block, (zero, zero))
    pass_on(B, 2)
    x_out(D, block[D](s))
    z_out(E, fv_in.at[pl.ds(0, 64)])
    x_out(H, fv_in.at[pl.ds(64, 64)])
    held = lax.fori_loop(4, 8, forward_block, held)

    pass_on(D, 0)
    sp_pass(1, fgview)
    sp_sib(1, fgview)
    all_in(B)

    def quarter(ref, q):
        return ref[pl.ds(multiple(q * 256, 256), 256), :]

    sum_begin(0, t.csa, t.cra, t.ysa, t.yra, t.acca, lambda q: nn(quarter(t.gated, q), t.wo[...]))
    adjoint_out(1)
    pass_on(D, 1)
    x_out(E, fv_in.at[pl.ds(0, 64)])
    z_out(H, fv_in.at[pl.ds(64, 64)])
    sp_pass(3, adjviews[0])
    sp_sib(3, adjviews[0])
    sp_sib(5, adjviews[1])
    pass_on(D, 2)
    sp_diag(1, fgview)
    neighbour_in(H)
    sum_end(0, t.yra, t.acca)

    secviews = halves(t.gfv)

    def second_tile(i):
        r = pl.ds(multiple(i * 32, 32), 32)
        middle = t.xo[r, :].astype(F32) + t.acca[r, :]
        t.mid[r, :] = middle
        hat, _ = spread_rows(middle)
        second = (hat * vector(GAIN2) + vector(BIAS2)).astype(BF16)
        t.gfv[pl.ds(multiple(p * 256 + i * 32, 32), 32), :] = second
        return second

    t.edge[p] = second_tile(7)[16:32]
    for k in range(1, 4):
        send(t.edge.at[p], t.edge.at[p], t.eds.at[k], t.edr.at[p], (s, sps[k]))

    @pl.loop(4, 7)
    def _(i):
        second_tile(i)

    sp_out(6, secviews[1])

    @pl.loop(0, 4)
    def _(i):
        second_tile(i)

    sp_out(2, secviews[0])
    pass_on(E, 0)

    def feed_gate_weight():
        return t.wfg[...].reshape(1024, 1024)

    def live_rows(r, base):
        pos = base + iota((32, 1), 0)
        return t.rgrad[r, :].astype(F32) * (pos < e3).astype(F32)

    def feed_rows(q, fgin, mine):
        before = (q + 3) % 4
        t.last[0:1, :] = t.edge[before, 15:16, :].astype(F32)

        @pl.loop(0, 8)
        def _(i):
            base = q * 256 + i * 32
            r, u = pl.ds(multiple(base, 32), 32), pl.ds(multiple(i * 32, 32), 32)
            second = t.gfv[r, :].astype(F32)
            row = iota((32, 1), 0)
            prior = jnp.where(row == 0, t.last[0:1, :], pltpu.roll(second, 1, 0)) * same_at(base + row)
            t.last[0:1, :] = second[31:32, :]
            diff = second - prior
            if mine:
                t.sec[u, :] = diff
            t.fkall[r, :] = (prior + diff * vector(FMIXK)).astype(BF16)
            fgin[u, :] = (prior + diff * vector(FMIXG)).astype(BF16)

        gate = t.sig if mine else t.fgg
        gate[...] = jax.nn.sigmoid(nn(fgin[...], feed_gate_weight()))

        @pl.loop(0, 8)
        def _(i):
            base = q * 256 + i * 32
            r, u = pl.ds(multiple(base, 32), 32), pl.ds(multiple(i * 32, 32), 32)
            t.cgall[r, :] = (live_rows(r, base) * gate[u, :]).astype(BF16)

    def upstream(i):
        pos = p * 256 + i * 32 + iota((32, 1), 0)
        return t.adj[pl.ds(multiple(i * 32, 32), 32), :].astype(F32) * (pos < e3).astype(F32)

    def raise_rows(q):
        r = pl.ds(multiple(q * 256, 256), 256)
        relu = jnp.maximum(nn(t.fkall[r, :], t.wfk[...]), 0.0)
        t.hidden[r, :] = (relu * relu).astype(BF16)

    for k in range(1, 4):
        arrive(t.edge.at[sps[k]], t.edr.at[sps[k]])
    feed_rows(p, t.fgin, True)
    pass_on(E, 1)
    sp_sib(6, secviews[1])
    sp_sib(2, secviews[0])
    feed_rows(p_sib, t.fpg, False)
    sp_diag(3, adjviews[0])
    sp_pass(5, adjviews[1])
    all_in(D)
    raise_rows(p)
    raise_rows(p_sib)
    pass_on(E, 2)
    pass_outwards(H)
    sp_diag(5, adjviews[1])
    sp_pass(6, secviews[1])
    sp_pass(2, secviews[0])
    feed_rows(p_y, t.fpg, False)
    raise_rows(p_y)
    sp_diag(6, secviews[1])
    sp_diag(2, secviews[0])
    feed_rows(p_diag, t.fpg, False)
    raise_rows(p_diag)
    settle(("sp", 2), ("sp", 3))

    def value_tile(k):
        q = pl.ds(multiple(dests[k] * 256, 256), 256)
        t.gfv[q, :] = tn(t.hidden[:, q], t.cgall[...]).astype(BF16)
        grad_x_out(FV, dests[k])

    value_tile(1)
    rest_in(H)
    all_in(E)
    sum_begin(1, t.csb, t.crb, t.ysb, t.yrb, t.accb, lambda q: nn(quarter(t.hidden, q), t.wfv[...]))

    def lower_rows(q):
        r = pl.ds(multiple(q * 256, 256), 256)
        t.rgrad[r, :] = (nt(t.cgall[r, :], t.wfv[...]) * 2.0 * jnp.sqrt(t.hidden[r, :].astype(F32))).astype(BF16)

    value_tile(2)
    for q in (p_diag, p_sib, p_y, p):
        lower_rows(q)
    grad_x_in(FV, 1)
    value_tile(3)
    sum_begin(2, t.csa, t.cra, t.ysa, t.yra, t.acca, lambda q: nt(quarter(t.rgrad, q), t.wfk[...]))

    value_tile(0)
    grad_x_in(FV, 2)
    settle(D)
    for k in (1, 2, 3, 0):
        q = pl.ds(multiple(dests[k] * 256, 256), 256)
        t.wfk[q, :] = tn(t.fkall[:, q], t.rgrad[...]).astype(BF16)
        grad_x_out(FK, dests[k])

    sum_end(1, t.yrb, t.accb)

    @pl.loop(0, 8)
    def _(i):
        r = pl.ds(multiple(i * 32, 32), 32)
        pos = p * 256 + i * 32 + iota((32, 1), 0)
        live = (pos < e3).astype(F32)
        sig, total, up = t.sig[r, :], t.accb[r, :], upstream(i)
        t.b_out[r, :] = (live * (t.mid[r, :] + sig * total)).astype(BF16)
        t.fpg[r, :] = (up * total * sig * (1.0 - sig)).astype(BF16)

    t.fgg[...] = nt(t.fpg[...], feed_gate_weight())
    settle(C, ("sp", 1))
    for k in range(4):
        part = tn(t.fgin[:, 256 * k : 256 * k + 256], t.fpg[...]).astype(BF16)
        t.wfg[2 * k : 2 * k + 2] = part.reshape(2, 128, 1024)
    for j, q in enumerate((p_diag, p_sib)):
        send(fgview(q), t.fgcr.at[j], t.rss.at[4, j], t.rsr.at[4, j], sib)
    results = []

    def result(src, dst):
        copy = pltpu.make_async_copy(src, dst, t.loc.at[12 + len(results)])
        copy.start()
        results.append(copy)

    result(t.b_out, out)
    grad_x_in(FV, 3)
    sum_end(2, t.yra, t.acca)

    @pl.loop(0, 8)
    def _(i):
        r = pl.ds(multiple(i * 32, 32), 32)
        pos = p * 256 + i * 32 + iota((32, 1), 0)
        through = t.acca[r, :] * (1.0 - vector(FMIXK)) + t.fgg[r, :] * (1.0 - vector(FMIXG))
        t.moved[r, :] = through * same_at(pos)

    down_edge = remote(t.moved.at[pl.ds(0, 8)], t.moved.at[pl.ds(256, 8)], t.eds.at[0], t.edr.at[4], (s, sps[3]))

    @pl.when(p > 0)
    def _():
        down_edge.start()

    @pl.when(p == 3)
    def _():
        t.moved[256:264, :] = jnp.zeros((8, 1024), F32)

    @pl.when(p < 3)
    def _():
        remote(t.moved.at[pl.ds(256, 8)], t.moved.at[pl.ds(256, 8)], t.eds.at[0], t.edr.at[4], sib).wait_recv()

    @pl.when(p > 0)
    def _():
        down_edge.wait_send()

    def norm_back(hat, scale, grad, gain):
        grad = grad * gain
        return scale * (
            grad - jnp.mean(grad, axis=1, keepdims=True) - hat * jnp.mean(grad * hat, axis=1, keepdims=True)
        )

    def add_vector(k, v):
        t.vg[k] += v[0:8] + v[8:16] + v[16:24] + v[24:32]

    def second_back(i):
        r = pl.ds(multiple(i * 32, 32), 32)
        after = pltpu.roll(t.moved[pl.ds(multiple(i * 32, 32), 40), :], 39, 0)[0:32]
        by_key, by_gate = t.acca[r, :], t.fgg[r, :]
        grad = by_key * vector(FMIXK) + by_gate * vector(FMIXG) + after
        diff = t.sec[r, :]
        hat, scale = spread_rows(t.mid[r, :])
        add_vector(FMIXK, diff * by_key)
        add_vector(FMIXG, diff * by_gate)
        add_vector(GAIN2, grad * hat)
        add_vector(BIAS2, grad)
        total = upstream(i) + norm_back(hat, scale, grad, vector(GAIN2))
        t.mid[r, :] = total
        t.xall[pl.ds(multiple(p * 256 + i * 32, 32), 32), :] = total.astype(BF16)

    agviews = halves(t.xall)
    pl.loop(0, 4)(second_back)
    sp_out(4, agviews[0])
    pl.loop(4, 8)(second_back)
    sp_out(7, agviews[1])
    grad_x_in(FK, 1)
    grad_x_in(FV, 0)

    arrive(t.fgcr.at[0], t.rsr.at[4, 0])
    there = pl.ds(multiple(p_y * 32, 32), 32)

    @pl.loop(0, 8)
    def _(i):
        t.wfg[i, there, :] = (t.wfg[i, there, :].astype(F32) + t.fgcr[0, i].astype(F32)).astype(BF16)

    send(fgview(p_y), t.fgyr, t.rss.at[4, 2], t.rsr.at[4, 2], ydev)
    grad_x_in(FK, 2)
    grad_x_in(FK, 3)
    for n, view in ((4, agviews[0]), (7, agviews[1])):
        sp_pass(n, view)
        sp_sib(n, view)
    for n, view in ((4, agviews[0]), (7, agviews[1])):
        sp_diag(n, view)

    @pl.loop(0, 4)
    def _(i):
        r = pl.ds(multiple(i * 256, 256), 256)
        grad = nt(t.xall[r, :], t.wo[...])
        gate = t.gate[r, :]
        t.hidden[r, 0:256] = (grad * gate).astype(BF16)
        t.hidden[r, 256:512] = (grad * t.mixed[r, :].astype(BF16).astype(F32) * gate * (1.0 - gate)).astype(BF16)

    for k in (1, 2, 3, 0):
        q = pl.ds(multiple(dests[k] * 256, 256), 256)
        t.rgrad[q, 512:768] = tn(t.gin[:, q], t.hidden[:, 256:512]).astype(BF16)
        grad_x_out(G, dests[k])
    settle(B)
    t.wo[...] = tn(t.gated[...], t.xall[...]).astype(BF16)
    first_z(O, 1)
    first_z(O, 2)

    def backward_block(k, held):
        b = 7 - k
        d_top, d_bottom, d_first, d_rate = held
        r = pl.ds(multiple(b * 128, 128), 128)
        alike, keep, memory, tail = block_parts(b)
        later = (alike & (iota((128, 128), 1) > iota((128, 128), 0))).astype(F32).astype(BF16)
        top, bottom = t.carry[b, 0:1, :], t.carry[b, 1:2, :]
        v = t.vv[r, :].astype(F32)
        weight = jnp.exp(t.kk[r, :].astype(F32))
        d_high = t.hidden[r, 0:256].astype(F32) * t.inverse[r, :]
        d_low = -d_high * t.mixed[r, :]
        shrink = t.tables[1]
        sums = exact_dot(later, jnp.concatenate([shrink * d_high, shrink * d_low], axis=1))
        scaled = t.tables[0] * weight
        own = t.small[1:2, :] * weight
        tail = tail * weight
        by_sum = scaled * (v * sums[:, :256] + sums[:, 256:])
        by_own = own * (v * d_high + d_low)
        by_tail = tail * (v * d_top + d_bottom)
        by_memory = memory * (top * d_high + bottom * d_low)
        t.vv[r, :] = (scaled * sums[:, :256] + own * d_high + tail * d_top).astype(BF16)
        t.kk[r, :] = (by_sum + by_own + by_tail).astype(BF16)
        place = iota((128, 1), 0).astype(F32)
        d_rate = d_rate + column_sum(
            place * by_sum + (place - 1.0) * by_own - by_memory - (127.0 - place) * by_tail
        )
        d_rate = d_rate - 128.0 * keep * (top * d_top + bottom * d_bottom)
        d_first = d_first + column_sum(by_own)
        d_top = keep * d_top + column_sum(memory * d_high)
        d_bottom = keep * d_bottom + column_sum(memory * d_low)
        return d_top, d_bottom, d_first, d_rate

    held = lax.fori_loop(0, 4, backward_block, (zero, zero, zero, zero))
    held = lax.fori_loop(4, 8, backward_block, held)
    first_z(O, 3)
    grad_x_in(G, 1)
    grad_x_in(G, 2)
    t.vgc[DECAY : DECAY + 1, :] = held[3] * t.small[2:3, :]
    t.vgc[FIRST : FIRST + 1, :] = held[2]

    t.last[...] = jnp.zeros_like(t.last)

    xbview = rows(t.cgall, 256)

    def rows_back(i):
        r = pl.ds(multiple(256 * i, 256), 256)
        t.acca[...] = nt(t.kk[r, :], t.wkvg[:, 0:256])
        t.accb[...] = nt(t.vv[r, :], t.wkvg[:, 256:512])
        t.fgg[...] = nt(t.hidden[r, 256:512], t.wkvg[:, 512:768])

        @pl.loop(0, 8)
        def _(k):
            j = 7 - k
            u = pl.ds(multiple(j * 32, 32), 32)
            base = i * 256 + j * 32
            here = pl.ds(multiple(base, 32), 32)
            by_key, by_value, by_gate = t.acca[u, :], t.accb[u, :], t.fgg[u, :]
            diff = t.spread[here, :].astype(F32)
            add_vector(MIXK, diff * by_key)
            add_vector(MIXV, diff * by_value)
            add_vector(MIXG, diff * by_gate)
            current = by_key * vector(MIXK) + by_value * vector(MIXV) + by_gate * vector(MIXG)
            row = iota((32, 1), 0)
            through = (by_key + by_value + by_gate - current) * same_at(base + row)
            after = jnp.where(row == 31, t.last[0:1, :], pltpu.roll(through, 31, 0))
            t.last[0:1, :] = through[0:1, :]
            t.cgall[here, :] = (current + after).astype(BF16)

    def first_row(r):
        by = [nt(t.kk[r, :], t.wkvg[:, 0:256]), nt(t.vv[r, :], t.wkvg[:, 256:512])]
        by.append(nt(t.hidden[r, 256:512], t.wkvg[:, 512:768]))
        through = sum(b * (1.0 - vector(k)) for b, k in zip(by, (MIXK, MIXV, MIXG)))
        return through[0:1, :] * same_at(512 + iota((1, 1), 0))

    lower = (y == 1).astype(F32)
    t.last[0:1, :] = first_row(pl.ds(512, 16)) * lower
    other, mine_too = 2 * (1 - y), 2 * y
    rows_back(other + 1)
    rows_back(other)
    t.last[0:1, :] = t.last[0:1, :] * (1.0 - lower)

    send(xbview(p_diag), t.crb.at[0], t.rss.at[3, 0], t.rsr.at[3, 0], sib, ("sum", 3))
    for k in (1, 2, 3, 0):
        q = pl.ds(multiple(dests[k] * 256, 256), 256)
        t.rgrad[q, 0:256] = tn(t.kin[:, q], t.kk[...]).astype(BF16)
        t.rgrad[q, 256:512] = tn(t.vin[:, q], t.vv[...]).astype(BF16)
        grad_x_out(KV, dests[k])

    arrive(t.crb.at[0], t.rsr.at[3, 0])

    def to_other(r):
        there = pl.ds(multiple(p_y * 256 + r.start, 32), 32)
        t.ysb[r, :] = (t.cgall[there, :].astype(F32) + t.crb[0, r, :].astype(F32)).astype(BF16)

    add_rows(256, to_other)
    send(t.ysb, t.yrb, t.rss.at[3, 2], t.rsr.at[3, 2], ydev, ("sum", 3))
    grad_x_in(KV, 1)
    rows_back(mine_too + 1)
    grad_x_in(KV, 2)
    grad_x_in(G, 3)
    rows_back(mine_too)
    send(xbview(p_sib), t.crb.at[1], t.rss.at[3, 1], t.rsr.at[3, 1], sib, ("sum", 3))
    grad_x_in(KV, 3)

    arrive(t.fgcr.at[1], t.rsr.at[4, 1])
    arrive(t.fgyr, t.rsr.at[4, 2])
    mine = pl.ds(multiple(p * 32, 32), 32)

    @pl.loop(0, 8)
    def _(i):
        total = t.wfg[i, mine, :].astype(F32) + t.fgcr[1, i].astype(F32) + t.fgyr[i].astype(F32)
        t.fgin[pl.ds(multiple(i * 32, 32), 32), :] = total.astype(BF16)

    for k in (1, 2, 3, 0):
        grad_x_out(FG, dests[k])
    then_x(O)
    arrive(t.crb.at[1], t.rsr.at[3, 1])

    def to_own(r):
        there = pl.ds(multiple(p * 256 + r.start, 32), 32)
        t.accb[r, :] = t.cgall[there, :].astype(F32) + t.crb[1, r, :].astype(F32)

    add_rows(256, to_own)
    grad_x_in(FG, 1)
    grad_x_in(FK, 0)

    def put_fv(i, r, v):
        t.moved[r, :] = v

    def put_fk(i, r, v):
        t.fkpart[i] = v.astype(BF16)

    def put_kv(i, r, v):
        t.kvgpart[i, :, 0:512] = v.astype(BF16)

    def put_g(i, r, v):
        t.kvgpart[i, :, 512:768] = v.astype(BF16)

    def put_o(i, r, v):
        t.o_out[r, :] = v

    def put_fg(i, r, v):
        t.fg_out[r, :] = v

    settle(("a2a", 1), ("a2a", 2))
    grad_z_in(FV, put_fv)
    result(t.moved.at[pl.ds(0, 128)], g_fv)
    grad_z_in(FK, put_fk)
    hand_back(0, t.fkpart, t.recfk)
    grad_x_in(FG, 2)
    grad_x_in(FG, 3)

    sum_end(3, t.yrb, t.accb)

    @pl.loop(0, 8)
    def _(i):
        r = pl.ds(multiple(i * 32, 32), 32)
        hat, scale = spread_rows(t.xo[r, :].astype(F32))
        grad = t.accb[r, :]
        add_vector(GAIN1, grad * hat)
        add_vector(BIAS1, grad)
        t.mid[r, :] = t.mid[r, :] + norm_back(hat, scale, grad, vector(GAIN1))

    lane = iota((16, 128), 1)
    mine_lanes = (lane >= 32 * p) & (lane < 32 * p + 32)
    for i in range(8):
        tile = t.vgc[:, 128 * (i // 4) : 128 * (i // 4) + 128]
        moved = pltpu.roll(tile, (32 * p + 128 - 32 * (i % 4)) % 128, 1)
        t.vmsg[i] = jnp.sum(t.vg[:, :, 128 * i : 128 * i + 128], axis=1) + jnp.where(mine_lanes, moved, 0.0)
    for k in range(1, 8):
        send(t.vmsg.at[sqs[k]], t.vrec.at[k], t.vss.at[0, k - 1], t.vsr.at[0, k], (sqs[k], p))
    result(t.mid, xgrad)
    grad_x_in(G, 0)
    grad_z_in(G, put_g)
    total = t.vmsg[s]
    for k in range(1, 8):
        arrive(t.vrec.at[k], t.vsr.at[0, k])
        total = total + t.vrec[k]
    t.vtwo[...] = total
    for k in range(1, 4):
        send(t.vtwo, t.vrec2.at[k], t.vss.at[1, k - 1], t.vsr.at[1, k], (s, sps[k]))
    grad_x_in(KV, 0)
    grad_z_in(KV, put_kv)
    hand_back(1, t.kvgpart, t.reckvg)
    last_x(O, put_o)
    result(t.o_out, g_o)
    grad_x_in(FG, 0)
    grad_z_in(FG, put_fg)
    result(t.fg_out, g_fg)
    handed_back(0, t.recfk)
    for i in range(8):
        for j in range(4):
            first = 512 * (i % 2) + 128 * j
            part = t.recfk[j, :, 128 * i : 128 * i + 128].astype(F32)
            t.acca[32 * (i // 2) : 32 * (i // 2) + 32, first : first + 128] = part
    for i in range(4):
        result(t.acca.at[pl.ds(32 * i, 32)], g_fk.at[:, pl.ds(1024 * i, 1024)])
    total = t.vtwo[...]
    for k in range(1, 4):
        arrive(t.vrec2.at[k], t.vsr.at[1, k])
        total = total + t.vrec2[k]
    t.v_out[...] = pltpu.roll(total, (128 - 32 * p) % 128, 1)
    result(t.v_out, g_vec)
    handed_back(1, t.reckvg)
    result(t.reckvg, g_kvg)
    for _, copy, cond in pending:
        left(copy, cond)
    for copy in results:
        copy.wait()


def finish_kernel(
    a_out, a_xgrad, a_o, a_fg, a_fk, a_fv, a_kvg, a_vec,
    out, xgrad, g_o, g_fg, g_fk, g_fv, g_k, g_v, g_g, *rest,
):
    vectors, held, (kvg, vec, *columns), sems = rest[:11], rest[11:17], rest[17:22], rest[22]
    pairs = ((a_xgrad, xgrad), (a_out, out), (a_fk, g_fk), (a_fv, g_fv), (a_o, g_o), (a_fg, g_fg))
    inward = [pltpu.make_async_copy(a_kvg, kvg, sems.at[0, 6]), pltpu.make_async_copy(a_vec, vec, sems.at[0, 7])]
    inward += [pltpu.make_async_copy(src, mid, sems.at[0, i]) for i, ((src, _), mid) in enumerate(zip(pairs, held))]
    outward = [pltpu.make_async_copy(mid, dst, sems.at[1, i]) for i, ((_, dst), mid) in enumerate(zip(pairs, held))]
    sorted_out = [pltpu.make_async_copy(mid, dst, sems.at[1, 6 + i]) for i, (mid, dst) in enumerate(zip(columns, (g_k, g_v, g_g)))]
    for copy in inward:
        copy.start()
    inward[0].wait()
    piece = iota((32, 128), 1) // 32
    for w, ref in enumerate(columns):
        for h in range(2):
            first = 256 * w + 128 * h
            tiles = [kvg[q, :, first : first + 128].astype(F32) for q in range(4)]
            for j in range(4):
                total = jnp.zeros((32, 128), F32)
                for q in range(4):
                    turn = 32 * (q - j) % 128
                    total = jnp.where(piece == q, pltpu.roll(tiles[q], turn, 1) if turn else tiles[q], total)
                ref[:, 512 * h + 128 * j : 512 * h + 128 * j + 128] = total
        sorted_out[w].start()
    inward[1].wait()
    for k, ref in enumerate(vectors):
        ref[...] = vec[k, 0:32]
    for first, second in zip(inward[2:], outward):
        first.wait()
        second.start()
    for copy in (*sorted_out, *outward):
        copy.wait()


def fast_body(
    incoming_signal,
    document_extents,
    adjoint_signal,
    layernorm_scaling,
    layernorm_offset,
    temporal_blend_lookup,
    temporal_blend_content,
    temporal_blend_receptor,
    temporal_shrinkage_log,
    diagonal_reward,
    lookup_projection,
    content_projection,
    receptor_projection,
    emission_projection,
    latter_scaling,
    latter_offset,
    channel_blend_lookup,
    channel_blend_receptor,
    channel_mixer_lookup,
    channel_mixer_content,
    channel_mixer_receptor,
):
    vecs = jnp.stack(
        [
            layernorm_scaling,
            layernorm_offset,
            temporal_blend_lookup,
            temporal_blend_content,
            temporal_blend_receptor,
            temporal_shrinkage_log,
            diagonal_reward,
            latter_scaling,
            latter_offset,
            channel_blend_lookup,
            channel_blend_receptor,
        ]
    )
    vecs = jnp.pad(vecs, ((0, 5), (0, 96)))
    anywhere = pl.BlockSpec(memory_space=pl.ANY)
    vmem = pl.BlockSpec(memory_space=pltpu.VMEM)
    shape = jax.ShapeDtypeStruct
    whole = (
        shape((256, 1024), BF16),
        shape((256, 1024), F32),
        shape((32, 1024), F32),
        shape((32, 1024), F32),
        shape((32, 4096), F32),
        shape((128, 1024), F32),
    )
    made = pl.pallas_call(
        step_kernel,
        out_shape=(*whole, shape((4, 32, 768), BF16), shape((16, 128), F32)),
        in_specs=[pl.BlockSpec(memory_space=pltpu.SMEM)] + [anywhere] * 10,
        out_specs=[anywhere] * 8,
        scratch_shapes=list(scratch_list().values()),
        compiler_params=pltpu.CompilerParams(
            collective_id=0, has_side_effects=True, vmem_limit_bytes=63 * 1024 * 1024
        ),
    )(
        document_extents,
        incoming_signal,
        adjoint_signal,
        vecs,
        lookup_projection,
        content_projection,
        receptor_projection,
        emission_projection,
        channel_mixer_receptor,
        channel_mixer_lookup,
        channel_mixer_content,
    )
    out, xgrad, g_o, g_fg, g_fk, g_fv, g_k, g_v, g_g, *v = pl.pallas_call(
        finish_kernel,
        out_shape=(*whole, *[shape((32, 1024), F32)] * 3, *[shape((32,), F32)] * 11),
        in_specs=[anywhere] * 8,
        out_specs=[anywhere] * 9 + [vmem] * 11,
        scratch_shapes=[
            *[pltpu.VMEM(whole[i].shape, whole[i].dtype) for i in (1, 0, 4, 5, 2, 3)],
            pltpu.VMEM((4, 32, 768), BF16),
            pltpu.VMEM((16, 128), F32),
            *[pltpu.VMEM((32, 1024), F32)] * 3,
            pltpu.SemaphoreType.DMA((2, 9)),
        ],
    )(*made)
    return (out, xgrad, *v[:7], g_k, g_v, g_g, g_o, *v[7:], g_fk, g_fv, g_fg)


def solution(mesh):
    fast = (mesh.shape["seq"], mesh.shape["sp"]) == (8, 4)
    flat, wide = P(("seq", "sp")), P(("seq", "sp"), None)
    return jax.shard_map(
        fast_body if fast else plain_body,
        mesh=mesh,
        in_specs=(wide, P("seq", None), wide, *[flat] * 7, *[wide] * 4, *[flat] * 4, *[wide] * 3),
        out_specs=(wide, wide, *[flat] * 7, *[wide] * 4, *[flat] * 4, *[wide] * 3),
        check_vma=False,
    )
```
